32 devices in a mesh: row: 4 (over z), col: 4 (over y, x), layer: 2 (over core).
Axes of the slice: x: 2, y: 2, z: 4, core: 2. Of those that a mesh axis runs over, the one named last changes fastest.
Arguments:
- density: bfloat16 [2048, 2048], P('row', ('col', 'layer')), may hold values from -4 to 4
- block_mask: int32 [16, 16], P('row', ('col', 'layer')), may hold values from 0 to 1, as said below
- keep_mask: int32 [16, 16], P('row', ('col', 'layer')), may hold values 0 or 1
- branch_flag: int32 [16], P('row'), may hold values from 0 to 1
Outputs:
- updated: float32 [2048, 2048], P('row', ('col', 'layer'))
- trace_new: float32 [], replicated
The draws below stay inside these ranges and needn't reach their ends.
Inputs may be any that keep to these rules, and one draw needn't show every extreme that they name: `block_mask`: symmetric, 1 on the diagonal; 1 where two blocks' centres in a periodic box lie within a cutoff distance of each other, else 0; block labels are in no spatial order. `keep_mask`: 0 or 1 for each block.
All inputs are finite; a program needn't handle non-finite values.
Results may differ from the reference program's by a relative error of at most 0.0004.
Values may be sent and summed in bfloat16 or wider, within the bound.
A program may use at most 64 MiB of HBM per device.

```python
import jax
import jax.numpy as jnp
from jax import lax

BLK = 128
NB = 16
N = 2048


def morton_coord(indices, offset):
    coord = jnp.zeros_like(indices)
    for level in range(11):
        digit = indices >> 3 * level + offset & 1
        coord = coord + (digit << level)
    return coord


def draw_block_mask(key, part):
    indices = jnp.arange(NB, dtype=jnp.int32)
    jitter = jax.random.randint(jax.random.fold_in(key, 7), (3, NB), 0, 4, dtype=jnp.int32)
    squared = jnp.zeros((NB, NB), jnp.int32)
    for offset in range(3):
        grid = morton_coord(indices, offset)
        extent = 4 * (jnp.max(grid) + 1)
        place = 4 * grid + jitter[offset]
        apart = jnp.abs(place[:, None] - place[None, :]) % extent
        apart = jnp.minimum(apart, extent - apart)
        squared = squared + apart * apart
    cutoff = int((3.8 * NB) ** (2.0 / 3.0))
    base = (squared <= cutoff).astype(jnp.int32)
    order = jax.random.permutation(jax.random.fold_in(key, 11), NB).astype(jnp.int32)
    return base[order][:, order]


def touch_ends(entries, stream_key, low, largest):
    shape = entries.shape
    spot = [jax.random.randint(jax.random.fold_in(stream_key, axis), (), 0, shape[axis]) for axis in range(len(shape))]
    entries = entries.at[tuple(spot)].set(low)
    longest = shape.index(max(shape))
    spot[longest] = (spot[longest] + 1) % shape[longest]
    return entries.at[tuple(spot)].set(largest)


def steps_of(stream_key, dims, shards, least, top_value):
    loudness, own = 1.0, jax.random.fold_in(stream_key, 6)
    for axis_at, parts in shards:
        draws = jnp.exp(jax.random.uniform(jax.random.fold_in(own, axis_at), (parts,), jnp.float32, least / len(shards), top_value / len(shards)))
        loudness = loudness * jnp.repeat(draws, dims[axis_at] // parts).reshape([-1 if axis == axis_at else 1 for axis in range(len(dims))])
    return loudness


def gaussian(stream_key, shape, scale, bound, pieces=(), kind=jnp.bfloat16):
    factor_of = steps_of(stream_key, shape, pieces, -0.22, 0.18) if pieces else 1.0
    drawn = jax.random.normal(stream_key, shape, jnp.float32) * scale * factor_of
    return jnp.minimum(jnp.maximum(drawn, -bound), bound).astype(kind)


def setup_inputs(seed: int = 0) -> dict:
    arg_keys = jax.random.split(jax.random.key(seed), 5)
    return {
        "density": gaussian(arg_keys[0], (N, N), ((N // 16) ** -0.25), 4.0, ((0, 4), (1, 8))),
        "block_mask": draw_block_mask(jax.random.fold_in(arg_keys[4], 71), 0),
        "keep_mask": touch_ends((jax.random.randint(arg_keys[2], (NB, NB), 0, 2) < 1).astype(jnp.int32), jax.random.fold_in(arg_keys[2], 1), 0, 1),
        "branch_flag": touch_ends(jax.random.randint(arg_keys[3], (NB,), 0, 2), jax.random.fold_in(arg_keys[3], 1), 0, 1).astype(jnp.int32),
    }


def expand_mask(block_mask):
    return jnp.repeat(jnp.repeat(block_mask, BLK, axis=0), BLK, axis=1)


def reference(density, block_mask, keep_mask, branch_flag):
    masked = density * expand_mask(block_mask).astype(jnp.bfloat16)
    wide = masked.astype(jnp.float32)
    square = jnp.dot(wide, wide, precision=lax.Precision.HIGHEST, preferred_element_type=jnp.float32)
    doubled = 2.0 * wide - square
    flag_rows = jnp.repeat(branch_flag, BLK)[:, None]
    chosen = jnp.where(flag_rows == 1, square, doubled)
    updated = chosen * expand_mask(keep_mask).astype(jnp.float32)
    trace_new = jnp.trace(updated)
    return updated, trace_new
```

```python
import functools

import jax
import jax.numpy as jnp
from jax import lax
from jax.experimental import pallas as pl
from jax.experimental.pallas import tpu as pltpu
from jax.sharding import PartitionSpec as P

MESH = pl.DeviceIdType.MESH
CHUNKS = 4
AHEAD = 2


def partner_of(index, step, size):
    if size & (size - 1):
        return (index + step) % size
    for bit in range(size.bit_length()):
        if step >> bit & 1:
            index = index + (1 - 2 * ((index // (1 << bit)) % 2)) * (1 << bit)
    return index


def passing_plan(n_row, late):
    plans = []
    for row in range(n_row - 1):
        order = [(block, q) for block in range(row, -1, -1) for q in range(CHUNKS)]
        for q in range(CHUNKS - late[min(row, len(late) - 1)], CHUNKS):
            if row:
                order.remove((1, q))
                order.append((1, q))
        plans.append(order)
    return plans


def kernel(
    sizes, density_hbm, block_hbm, keep_hbm, flag_hbm, updated, lines,
    density, block_mask, keep_mask, branch_flag,
    row_panel, col_panel, trace_own, trace_in, local_sem,
    plane_send, plane_recv, side_send, right_send, left_send, z_recv,
    trace_send, trace_recv, trace_sum, sum_send, sum_recv, ready,
):
    n_row, n_col, n_layer = sizes
    rows, width = density.shape
    blk = rows // block_mask.shape[1]
    per = rows // width
    piece = rows // CHUNKS
    slots = n_col * n_layer
    last = n_row - 1
    r, c, l = lax.axis_index("row"), lax.axis_index("col"), lax.axis_index("layer")
    me = c * n_layer + l
    has_left, has_right = r > 0, r < last
    left, right = jnp.maximum(r - 1, 0), jnp.minimum(r + 1, last)
    col_peers = [partner_of(c, d, n_col) for d in range(1, n_col)]
    layer_peers = [partner_of(l, d, n_layer) for d in range(1, n_layer)]
    plane_peers = [(p, q) for p in col_peers for q in range(n_layer)]
    plane_peers += [(c, q) for q in layer_peers]

    loads = [
        pltpu.make_async_copy(source, target, local_sem.at[i])
        for i, (source, target) in enumerate([
            (block_hbm, block_mask), (density_hbm, density),
            (keep_hbm, keep_mask), (flag_hbm, branch_flag)])
    ]
    for load in loads:
        load.start()

    barrier = pltpu.get_barrier_semaphore()

    def greet(target):
        pl.semaphore_signal(barrier, inc=1, device_id=target, device_id_type=MESH)

    def answer(which, target):
        pl.semaphore_signal(
            ready.at[which], inc=1, device_id=target, device_id_type=MESH)

    pl.when(has_right)(lambda: greet((right, c, l)))
    for p, q in plane_peers:
        pl.when(p * n_layer + q > me)(functools.partial(greet, (r, p, q)))
    below, above = jnp.where(has_left, 1, 0) + me, slots - 1 - me
    pl.when(below > 0)(lambda: pl.semaphore_wait(barrier, below))
    pl.when(has_left)(lambda: answer(0, (left, c, l)))
    for p, q in plane_peers:
        pl.when(p * n_layer + q < me)(functools.partial(answer, 1, (r, p, q)))
    for load in loads:
        load.wait()

    for i in range(rows // blk):
        for k in range(width // blk):
            at = (pl.ds(i * blk, blk), pl.ds(k * blk, blk))
            kept = jnp.full((blk, blk), block_mask[k, i].astype(jnp.float32))
            row_panel[(me,) + at] = density[at] * kept.astype(jnp.bfloat16)

    def span(q):
        return pl.ds(q * piece, piece)

    def z_copy(block, q, source, target, sem):
        return pltpu.make_async_remote_copy(
            src_ref=source, dst_ref=col_panel.at[block, span(q)],
            send_sem=sem.at[0], recv_sem=z_recv.at[block, q],
            device_id=(target, c, l), device_id_type=MESH,
        )

    def to_right(block, q, source):
        return z_copy(block, q, source, right, right_send)

    def to_left(block, q, source):
        return z_copy(block, q, source, left, left_send)

    def half_copy(slot, h, sem, target):
        half = pl.ds(h * (rows // 2), rows // 2)
        return pltpu.make_async_remote_copy(
            src_ref=row_panel.at[slot, half], dst_ref=row_panel.at[slot, half],
            send_sem=sem.at[0], recv_sem=plane_recv.at[slot, h],
            device_id=target, device_id_type=MESH,
        )

    def plane_copy(slot, h, peer):
        return half_copy(slot, h, plane_send, (r, peer, l))

    def side_copies(slot, h):
        for other in layer_peers:
            half_copy(slot, h, side_send, (r, c, other)).start()

    def side_wait(slot):
        for h in range(2):
            half_copy(slot, h, side_send, (r, c, l)).wait_recv()

    bits = [d for d in range(1, n_col) if d & (d - 1) == 0]
    relayed = [lo | hi for hi in bits for lo in bits if lo < hi]
    if n_col & (n_col - 1):
        bits, relayed = list(range(1, n_col)), []
    direct = [d for d in range(1, n_col) if d not in relayed]
    halves = {d: (1, 0) if relayed and d > 1 else (0, 1) for d in range(1, n_col)}

    def plane_start(chosen):
        for turn in range(2):
            for d in direct:
                peer = col_peers[d - 1]
                pl.when(chosen(peer))(
                    lambda: plane_copy(me, halves[d][turn], peer).start())

    def plane_arrive(d, turn):
        peer, h = col_peers[d - 1], halves[d][turn]
        slot = peer * n_layer + l
        plane_copy(slot, h, peer).wait_recv()
        for other in bits if relayed and d in bits else []:
            if (other > d) == (h == 0) and other != d:
                plane_copy(slot, h, col_peers[other - 1]).start()
        side_copies(slot, h)

    rightward = passing_plan(n_row, (0, 3)) + [[]]
    leftward = [[]] + [[(last - b, q) for b, q in plan]
                       for plan in reversed(passing_plan(n_row, (0, 1, 2)))]
    from_left = [[]] + rightward[:-1]
    from_right = leftward[1:] + [[]]

    def pass_on(copy, row, plan, first, arrived, limit=None):
        while first < len(plan) and (limit is None or first < limit):
            block, q = plan[first]
            if block == row:
                copy(row, q, row_panel.at[me, span(q)]).start()
            elif (block, q) in arrived:
                copy(block, q, col_panel.at[block, span(q)]).start()
            else:
                break
            first += 1
        return first

    sent_left, sent_right = [0] * n_row, [0] * n_row
    for row in range(1, n_row):
        @pl.when(r == row)
        def _():
            sent_left[row] = pass_on(to_left, row, leftward[row], 0, (), AHEAD)
    plane_start(lambda peer: peer < c)
    pl.when(has_right)(lambda: pl.semaphore_wait(ready.at[0], 1))
    for row in range(last):
        @pl.when(r == row)
        def _():
            sent_right[row] = pass_on(to_right, row, rightward[row], 0, (), AHEAD)
    pl.when(above > 0)(lambda: pl.semaphore_wait(ready.at[1], above))
    for row in range(n_row):
        @pl.when(r == row)
        def _():
            sent_left[row] = pass_on(to_left, row, leftward[row], sent_left[row], ())
            sent_right[row] = pass_on(to_right, row, rightward[row], sent_right[row], ())
    plane_start(lambda peer: peer > c)
    for h in range(2):
        side_copies(me, h)

    def z_arrive(k, then=None):
        for row in range(n_row):
            if k < max(len(from_right[row]), len(from_left[row])):
                @pl.when(r == row)
                def _():
                    if k < len(from_left[row]):
                        block, q = from_left[row][k]
                        to_right(block, q, col_panel.at[block, span(q)]).wait_recv()
                        sent_right[row] = pass_on(
                            to_right, row, rightward[row], sent_right[row],
                            from_left[row][:k + 1])
                        if then:
                            then(row, from_left[row], k)
                    if k < len(from_right[row]):
                        block, q = from_right[row][k]
                        to_left(block, q, col_panel.at[block, span(q)]).wait_recv()
                        sent_left[row] = pass_on(
                            to_left, row, leftward[row], sent_left[row],
                            from_right[row][:k + 1])
                        if then:
                            then(row, from_right[row], k)

    def terms(block, start, size):
        out = []
        while size:
            step = min(size, width - start % width)
            out.append(jnp.dot(
                row_panel[block * per + start // width, :, pl.ds(start % width, step)],
                col_panel[block, pl.ds(start, step), :],
                preferred_element_type=jnp.float32))
            start, size = start + step, size - step
        return out

    def add(products):
        total = products[0]
        for product in products[1:]:
            total = total + product
        updated[...] += total

    on_diagonal = me // per == r
    corner = pl.multiple_of((me % per) * width, width)
    tiles = width // blk
    lanes = lax.broadcasted_iota(jnp.int32, (1, blk), 1)
    eye = (lax.broadcasted_iota(jnp.int32, (blk, blk), 0)
           == lax.broadcasted_iota(jnp.int32, (blk, blk), 1))

    def weight(t, if_square, otherwise):
        kept = keep_mask[t, (me % per) * tiles + t]
        chosen = jnp.where(branch_flag[(me % per) * tiles + t] == 1, if_square, otherwise)
        return (kept * chosen).astype(jnp.float32)

    def pair_sums(block, k):
        slot = block * per + k * blk // width
        out = []
        for t in range(tiles):
            ours = row_panel[slot, pl.ds(corner + t * blk, blk), pl.ds(k * blk % width, blk)]
            if block is r:
                theirs = row_panel[me, pl.ds(k * blk, blk), pl.ds(t * blk, blk)]
            else:
                theirs = col_panel[block, pl.ds(k * blk, blk), pl.ds(t * blk, blk)]
            product = jnp.dot(ours, theirs, preferred_element_type=jnp.float32)
            out.append(jnp.sum(jnp.where(eye, product, 0.0), axis=0, keepdims=True))
        return out

    def trace_copy(z, col, layer):
        return pltpu.make_async_remote_copy(
            src_ref=trace_own, dst_ref=trace_in.at[me],
            send_sem=trace_send.at[0], recv_sem=trace_recv.at[jnp.where(r > 0, 1, 0)],
            device_id=(z, col, layer), device_id_type=MESH,
        )

    def heirs(row):
        planes = range(n_row) if row == 0 else range(1, max(row + 1, last))
        return [(z, col, layer) for z in planes for col in range(n_col)
                for layer in range(n_layer)]

    def add_trace(blocks, start):
        weights = [weight(t, 1, -1) for t in range(tiles)]
        part = spread = others = jnp.zeros((1, blk), jnp.float32)
        if not start:
            part, spread, others = (trace_own[n:n + 1, :] for n in range(3))
        for t in range(tiles if start else 0):
            own = row_panel[me, pl.ds(corner + t * blk, blk), pl.ds(t * blk, blk)]
            line = jnp.sum(
                jnp.where(eye, own.astype(jnp.float32), 0.0), axis=0, keepdims=True)
            part += weight(t, 0, 2) * line
            spread += jnp.where(lanes == me * tiles + t, weights[t], 0.0)
        for block in ([r] if start else []) + blocks:
            for k in range(rows // blk):
                sums = pair_sums(block, k)
                for t in range(tiles):
                    part += weights[t] * sums[t]
                if block is not r:
                    here = block * (rows // blk) + k
                    total = sum(jnp.sum(line, keepdims=True) for line in sums)
                    others += jnp.where(lanes == here, total, 0.0)
        trace_own[0:1, :] = part
        trace_own[1:2, :] = spread
        trace_own[2:3, :] = others

    def send_trace(row):
        trace_in[me] = trace_own[...]
        for z, col, layer in heirs(row):
            pl.when((z != row) | (col != c) | (layer != l))(
                lambda: trace_copy(z, col, layer).start())

    middle = (last - 1) * CHUNKS
    early = [b for b, _ in from_right[0][:middle]].count(last) == CHUNKS

    def partner(b, row):
        return (b * per // n_layer) ^ (row * per // n_layer)

    def diagonal(row):
        @pl.when(on_diagonal & (r == row))
        def _():
            pairs = [0] + list(range(row + 1, n_row)) if row else [last] if early else []
            add_trace([] if row == last else pairs, True)
            if row > 0 or early:
                send_trace(row)

    pl.when(has_left)(lambda: pl.semaphore_wait(ready.at[2], 1))
    pl.when(has_right)(lambda: answer(2, (right, c, l)))
    for other in layer_peers:
        side_wait(c * n_layer + other)
    diagonal(last)
    for k in range(CHUNKS // 2):
        z_arrive(k)
    for d in direct:
        plane_arrive(d, 0)
    for k in range(CHUNKS // 2, CHUNKS):
        z_arrive(k)
    for d in direct:
        plane_arrive(d, 1)
    soon = CHUNKS + 1
    for k in range(CHUNKS, soon):
        z_arrive(k)
    for other in layer_peers:
        for d in direct:
            side_wait(col_peers[d - 1] * n_layer + other)
    def needs(row):
        blocks = {0: [last], last: []}.get(row, [0] + list(range(row + 1, n_row)))
        late = [b for b in blocks if partner(b, row) in relayed]
        for b in blocks:
            arrived = (from_left if b < row else from_right)[row][:soon]
            late += [b] if [x for x, _ in arrived].count(b) < CHUNKS else []
        return late

    quick = [row for row in range(1, last) if not needs(row)]
    for row in quick:
        diagonal(row)
    for turn in range(2):
        for d in relayed:
            plane_arrive(d, turn)
    for k in range(soon, middle):
        z_arrive(k)
    for other in layer_peers:
        for d in relayed:
            side_wait(col_peers[d - 1] * n_layer + other)
    for row in range(last):
        if row not in quick:
            diagonal(row)

    total = None
    for t in range(per):
        term = jnp.dot(
            row_panel[r * per + t], row_panel[me, pl.ds(t * width, width), :],
            preferred_element_type=jnp.float32)
        total = term if total is None else total + term
    updated[...] = total
    inner = has_left & has_right
    for s in range(1, last):
        pl.when((r - s >= 0) & inner)(lambda: add(terms(r - s, 0, rows)))
        pl.when((r + s <= last) & inner)(lambda: add(terms(r + s, 0, rows)))
    for row, arrived in ((0, from_right[0]), (last, from_left[last])):
        @pl.when(r == row)
        def _():
            products = []
            for block in range(n_row):
                held = sorted(q for b, q in arrived[:middle] if b == block)
                if held:
                    assert held == list(range(len(held)))
                    products += terms(block, 0, len(held) * piece)
            add(products)

    def finish(row, arrived, k):
        block, q = arrived[k]
        held = [b for b, _ in arrived[:k + 1]].count(last)
        if row == 0 and block == last and held == CHUNKS and not early:
            @pl.when(on_diagonal)
            def _():
                add_trace([last], False)
                send_trace(0)
        add(terms(block, q * piece, piece))

    for k in range(middle, last * CHUNKS):
        z_arrive(k, finish)

    for i in range(rows // blk):
        flag = jnp.full((blk, blk), branch_flag[i]) == 1
        for k in range(width // blk):
            at = (pl.ds(i * blk, blk), pl.ds(k * blk, blk))
            product = updated[at]
            doubled = 2.0 * row_panel[(me,) + at].astype(jnp.float32) - product
            kept = jnp.full((blk, blk), keep_mask[k, i].astype(jnp.float32))
            updated[at] = jnp.where(flag, product, doubled) * kept

    def heard(first, count, sem):
        pltpu.make_async_remote_copy(
            src_ref=trace_in.at[pl.ds(first, count)],
            dst_ref=trace_in.at[pl.ds(first, count)],
            send_sem=trace_send.at[0], recv_sem=trace_recv.at[sem],
            device_id=(r, c, l), device_id_type=MESH,
        ).wait_recv()

    def hear(first, count, sem):
        pl.when(on_diagonal & (me >= first) & (me < first + count))(
            lambda: heard(first, count - 1, sem))
        pl.when(jnp.logical_not(on_diagonal & (me >= first) & (me < first + count)))(
            lambda: heard(first, count, sem))

    def sum_of(first, count):
        total = trace_in[first]
        for slot in range(first + 1, first + count):
            total = total + trace_in[slot]
        return total

    def sum_copy(n, target):
        return pltpu.make_async_remote_copy(
            src_ref=trace_sum.at[n], dst_ref=trace_sum.at[0],
            send_sem=sum_send.at[n], recv_sem=sum_recv.at[0],
            device_id=(target, c, l), device_id_type=MESH,
        )

    @pl.when(inner)
    def _():
        hear(per, slots - per, 1)

    @pl.when(r == 1)
    def _():
        trace_sum[1] = sum_of(per, slots - per)
        sum_copy(1, 0).start()

    @pl.when(r == last - 1)
    def _():
        trace_sum[2] = sum_of(per, slots - 2 * per)
        sum_copy(2, last).start()

    for row in range(n_row):
        @pl.when(r == row)
        def _():
            for copy, plan, sem in (
                    (to_left, leftward[row], left_send),
                    (to_right, rightward[row], right_send)):
                if plan:
                    blocks = pl.ds(0, len(plan) // CHUNKS)
                    pltpu.make_async_remote_copy(
                        src_ref=col_panel.at[blocks], dst_ref=col_panel.at[blocks],
                        send_sem=sem.at[0], recv_sem=z_recv.at[0, 0],
                        device_id=(left, c, l), device_id_type=MESH,
                    ).wait_send()

    def sent_slots(count, ref, sem):
        pltpu.make_async_remote_copy(
            src_ref=ref.at[pl.ds(0, count)], dst_ref=ref.at[pl.ds(0, count)],
            send_sem=sem.at[0], recv_sem=plane_recv.at[0, 0],
            device_id=(r, c, l), device_id_type=MESH,
        ).wait_send()

    sent_slots(n_col - 1, row_panel, plane_send)
    sent_slots((n_layer - 1) * n_col, row_panel, side_send)

    hear(0, per, 0)

    @pl.when(r == last)
    def _():
        hear(last * per, per, 1)

    @pl.when(jnp.logical_not(inner))
    def _():
        sum_copy(1, 0).wait_recv()

    @pl.when(inner)
    def _():
        lines[...] = sum_of(0, slots)

    @pl.when(r == 0)
    def _():
        lines[...] = sum_of(0, per) + trace_sum[0]

    @pl.when(r == last)
    def _():
        lines[...] = sum_of(0, per) + sum_of(last * per, per) + trace_sum[0]

    pl.when(r == 1)(lambda: sum_copy(1, 0).wait_send())
    pl.when(r == last - 1)(lambda: sum_copy(2, last).wait_send())
    for row in range(n_row):
        pl.when(on_diagonal & (r == row))(
            lambda: sent_slots(len(heirs(row)) - 1, trace_in, trace_send))


def deliver(updated, lines, out, trace):
    out[...] = updated[...]
    trace[0, 0] = jnp.sum(lines[0:1, :] + lines[1:2, :] * lines[2:3, :])


def on_device(sizes, density, block_mask, keep_mask, branch_flag):
    n_row, n_col, n_layer = sizes
    rows, width = density.shape
    blk = rows // block_mask.shape[0]
    dma = pltpu.SemaphoreType.DMA
    slots = n_col * n_layer
    vmem, smem = pl.BlockSpec(memory_space=pltpu.VMEM), pl.BlockSpec(memory_space=pltpu.SMEM)
    hbm = pl.BlockSpec(memory_space=pltpu.HBM)
    panel_bytes = 2 * rows * width * (slots + n_row + 1)
    updated, lines = pl.pallas_call(
        functools.partial(kernel, sizes),
        out_shape=(
            jax.ShapeDtypeStruct((rows, width), jnp.float32),
            jax.ShapeDtypeStruct((3, blk), jnp.float32),
        ),
        in_specs=[hbm, hbm, hbm, hbm],
        out_specs=(vmem, vmem),
        scratch_shapes=[
            pltpu.VMEM((rows, width), jnp.bfloat16),
            pltpu.SMEM(block_mask.T.shape, jnp.int32),
            pltpu.SMEM(keep_mask.T.shape, jnp.int32),
            pltpu.SMEM(branch_flag.shape, jnp.int32),
            pltpu.VMEM((slots, rows, width), jnp.bfloat16),
            pltpu.VMEM((n_row, rows, width), jnp.bfloat16),
            pltpu.VMEM((3, blk), jnp.float32),
            pltpu.VMEM((n_row * slots, 3, blk), jnp.float32),
            dma((4,)),
            dma((1,)),
            dma((slots, 2)),
            dma((1,)),
            dma((1,)),
            dma((1,)),
            dma((n_row, CHUNKS)),
            dma((1,)),
            dma((2,)),
            pltpu.VMEM((3, 3, blk), jnp.float32),
            dma((3,)),
            dma((1,)),
            pltpu.SemaphoreType.REGULAR((3,)),
        ],
        compiler_params=pltpu.CompilerParams(
            collective_id=0, has_side_effects=True,
            vmem_limit_bytes=panel_bytes + 8 * rows * width + (4 << 20)),
    )(*[
        pltpu.with_memory_space_constraint(x, pltpu.HBM)
        for x in (density, block_mask.T, keep_mask.T, branch_flag)
    ])
    updated, trace = pl.pallas_call(
        deliver,
        out_shape=(
            jax.ShapeDtypeStruct((rows, width), jnp.float32),
            jax.ShapeDtypeStruct((1, 1), jnp.float32),
        ),
        in_specs=[vmem, vmem],
        out_specs=(vmem, smem),
        compiler_params=pltpu.CompilerParams(
            vmem_limit_bytes=8 * rows * width + (4 << 20)),
    )(updated, lines)
    return updated, trace[0, 0]


def solution(mesh):
    sizes = tuple(mesh.shape[name] for name in ("row", "col", "layer"))
    in_specs = (
        P("row", ("col", "layer")),
        P("row", ("col", "layer")),
        P("row", ("col", "layer")),
        P("row"),
    )
    out_specs = (P("row", ("col", "layer")), P())
    return jax.shard_map(
        functools.partial(on_device, sizes), mesh=mesh, in_specs=in_specs,
        out_specs=out_specs, check_vma=False,
    )
```

```python
import functools

import jax
import jax.numpy as jnp
from jax import lax
from jax.experimental import pallas as pl
from jax.experimental.pallas import tpu as pltpu
from jax.sharding import PartitionSpec as P

MESH = pl.DeviceIdType.MESH
CHUNKS = 4
AHEAD = 2


def partner_of(index, step, size):
    if size & (size - 1):
        return (index + step) % size
    for bit in range(size.bit_length()):
        if step >> bit & 1:
            index = index + (1 - 2 * ((index // (1 << bit)) % 2)) * (1 << bit)
    return index


def passing_plans(n_row):
    last = n_row - 1
    blocks = [[(b, q) for q in range(CHUNKS)] for b in range(n_row)]
    rightward = [sum(blocks[row::-1], []) for row in range(last)] + [[]]
    leftward = [[]] + [sum(blocks[row:], []) for row in range(1, n_row)]
    leftward[1].append(leftward[1].pop(CHUNKS - 1))
    return rightward, leftward


def kernel(
    sizes, density_hbm, block_hbm, keep_hbm, flag_hbm, updated, lines,
    density, block_mask, keep_mask, branch_flag,
    row_panel, col_panel, trace_own, trace_in, local_sem,
    plane_send, plane_recv, side_send, right_send, left_send, z_recv,
    trace_send, trace_recv, ready,
):
    n_row, n_col, n_layer = sizes
    rows, width = density.shape
    blk = rows // block_mask.shape[1]
    per = rows // width
    piece = rows // CHUNKS
    slots = n_col * n_layer
    last = n_row - 1
    r, c, l = lax.axis_index("row"), lax.axis_index("col"), lax.axis_index("layer")
    me = c * n_layer + l
    has_left, has_right = r > 0, r < last
    left, right = jnp.maximum(r - 1, 0), jnp.minimum(r + 1, last)
    col_peers = [partner_of(c, d, n_col) for d in range(1, n_col)]
    layer_peers = [partner_of(l, d, n_layer) for d in range(1, n_layer)]
    plane_peers = [(p, q) for p in col_peers for q in range(n_layer)]
    plane_peers += [(c, q) for q in layer_peers]

    loads = [
        pltpu.make_async_copy(source, target, local_sem.at[i])
        for i, (source, target) in enumerate([
            (block_hbm, block_mask), (density_hbm, density),
            (keep_hbm, keep_mask), (flag_hbm, branch_flag)])
    ]
    for load in loads:
        load.start()

    barrier = pltpu.get_barrier_semaphore()

    def greet(target):
        pl.semaphore_signal(barrier, inc=1, device_id=target, device_id_type=MESH)

    def answer(which, target):
        pl.semaphore_signal(
            ready.at[which], inc=1, device_id=target, device_id_type=MESH)

    pl.when(has_right)(lambda: greet((right, c, l)))
    for p, q in plane_peers:
        pl.when(p * n_layer + q > me)(functools.partial(greet, (r, p, q)))
    below, above = jnp.where(has_left, 1, 0) + me, slots - 1 - me
    pl.when(below > 0)(lambda: pl.semaphore_wait(barrier, below))
    pl.when(has_left)(lambda: answer(0, (left, c, l)))
    for p, q in plane_peers:
        pl.when(p * n_layer + q < me)(functools.partial(answer, 1, (r, p, q)))
    for load in loads:
        load.wait()

    for i in range(rows // blk):
        for k in range(width // blk):
            at = (pl.ds(i * blk, blk), pl.ds(k * blk, blk))
            kept = jnp.full((blk, blk), block_mask[k, i].astype(jnp.float32))
            row_panel[(me,) + at] = density[at] * kept.astype(jnp.bfloat16)

    def span(q):
        return pl.ds(q * piece, piece)

    def z_copy(block, q, source, target, sem):
        return pltpu.make_async_remote_copy(
            src_ref=source, dst_ref=col_panel.at[block, span(q)],
            send_sem=sem.at[0], recv_sem=z_recv.at[block, q],
            device_id=(target, c, l), device_id_type=MESH,
        )

    def to_right(block, q, source):
        return z_copy(block, q, source, right, right_send)

    def to_left(block, q, source):
        return z_copy(block, q, source, left, left_send)

    def half_copy(slot, h, sem, target):
        half = pl.ds(h * (rows // 2), rows // 2)
        return pltpu.make_async_remote_copy(
            src_ref=row_panel.at[slot, half], dst_ref=row_panel.at[slot, half],
            send_sem=sem.at[0], recv_sem=plane_recv.at[slot, h],
            device_id=target, device_id_type=MESH,
        )

    def plane_copy(slot, h, peer):
        return half_copy(slot, h, plane_send, (r, peer, l))

    def side_copies(slot, h):
        for other in layer_peers:
            half_copy(slot, h, side_send, (r, c, other)).start()

    def side_wait(slot):
        for h in range(2):
            half_copy(slot, h, side_send, (r, c, l)).wait_recv()

    bits = [d for d in range(1, n_col) if d & (d - 1) == 0]
    relayed = [lo | hi for hi in bits for lo in bits if lo < hi]
    if n_col & (n_col - 1):
        bits, relayed = list(range(1, n_col)), []
    direct = [d for d in range(1, n_col) if d not in relayed]
    halves = {d: (1, 0) if relayed and d > 1 else (0, 1) for d in range(1, n_col)}

    def plane_start(chosen):
        for turn in range(2):
            for d in direct:
                peer = col_peers[d - 1]
                pl.when(chosen(peer))(
                    lambda: plane_copy(me, halves[d][turn], peer).start())

    def plane_arrive(d, turn):
        peer, h = col_peers[d - 1], halves[d][turn]
        slot = peer * n_layer + l
        plane_copy(slot, h, peer).wait_recv()
        for other in bits if relayed and d in bits else []:
            if (other > d) == (h == 0) and other != d:
                plane_copy(slot, h, col_peers[other - 1]).start()
        side_copies(slot, h)

    rightward, leftward = passing_plans(n_row)
    from_left = [[]] + rightward[:-1]
    from_right = leftward[1:] + [[]]

    on_diagonal = me // per == r

    def pass_on(copy, row, plan, first, arrived, stop=None, hold=None):
        while first < len(plan) and (stop is None or first < stop):
            block, q = plan[first]
            if block == row:
                source = row_panel.at[me, span(q)]
            elif (block, q) in arrived:
                source = col_panel.at[block, span(q)]
            else:
                break
            if hold is None or first < hold:
                copy(block, q, source).start()
            else:
                pl.when(jnp.logical_not(on_diagonal))(
                    functools.partial(lambda f: f.start(), copy(block, q, source)))
            first += 1
        return first

    sent_left, sent_right = [0] * n_row, [0] * n_row
    hold_left, hold_right = {1: last * CHUNKS - 3}, {last - 1: 2 * CHUNKS - 1}
    for row in range(1, n_row):
        @pl.when(r == row)
        def _():
            sent_left[row] = pass_on(to_left, row, leftward[row], 0, (), AHEAD)
    plane_start(lambda peer: peer < c)
    pl.when(has_right)(lambda: pl.semaphore_wait(ready.at[0], 1))
    for row in range(last):
        @pl.when(r == row)
        def _():
            sent_right[row] = pass_on(to_right, row, rightward[row], 0, (), AHEAD)
    pl.when(above > 0)(lambda: pl.semaphore_wait(ready.at[1], above))
    for row in range(n_row):
        @pl.when(r == row)
        def _():
            sent_left[row] = pass_on(
                to_left, row, leftward[row], sent_left[row], (), None, hold_left.get(row))
            sent_right[row] = pass_on(
                to_right, row, rightward[row], sent_right[row], (), None, hold_right.get(row))
    plane_start(lambda peer: peer > c)
    for h in range(2):
        side_copies(me, h)

    def z_arrive(k, then=None):
        for row in range(n_row):
            if k < max(len(from_right[row]), len(from_left[row])):
                @pl.when(r == row)
                def _():
                    if k < len(from_right[row]):
                        block, q = from_right[row][k]
                        to_left(block, q, col_panel.at[block, span(q)]).wait_recv()
                        sent_left[row] = pass_on(
                            to_left, row, leftward[row], sent_left[row],
                            from_right[row][:k + 1], None, hold_left.get(row))
                        if then:
                            then(row, from_right[row], k)
                    if k < len(from_left[row]):
                        block, q = from_left[row][k]
                        to_right(block, q, col_panel.at[block, span(q)]).wait_recv()
                        sent_right[row] = pass_on(
                            to_right, row, rightward[row], sent_right[row],
                            from_left[row][:k + 1], None, hold_right.get(row))
                        if then:
                            then(row, from_left[row], k)

    def terms(block, start, size):
        out = []
        while size:
            step = min(size, width - start % width)
            out.append(jnp.dot(
                row_panel[block * per + start // width, :, pl.ds(start % width, step)],
                col_panel[block, pl.ds(start, step), :],
                preferred_element_type=jnp.float32))
            start, size = start + step, size - step
        return out

    def add(products):
        total = products[0]
        for product in products[1:]:
            total = total + product
        updated[...] += total

    corner = pl.multiple_of((me % per) * width, width)
    tiles = width // blk
    lanes = lax.broadcasted_iota(jnp.int32, (1, blk), 1)
    eye = (lax.broadcasted_iota(jnp.int32, (blk, blk), 0)
           == lax.broadcasted_iota(jnp.int32, (blk, blk), 1))

    def weight(t, if_square, otherwise):
        kept = keep_mask[t, (me % per) * tiles + t]
        chosen = jnp.where(branch_flag[(me % per) * tiles + t] == 1, if_square, otherwise)
        return (kept * chosen).astype(jnp.float32)

    def pair_sums(block, k):
        slot = block * per + k * blk // width
        out = []
        for t in range(tiles):
            ours = row_panel[slot, pl.ds(corner + t * blk, blk), pl.ds(k * blk % width, blk)]
            if block is r:
                theirs = row_panel[me, pl.ds(k * blk, blk), pl.ds(t * blk, blk)]
            else:
                theirs = col_panel[block, pl.ds(k * blk, blk), pl.ds(t * blk, blk)]
            product = jnp.dot(ours, theirs, preferred_element_type=jnp.float32)
            out.append(jnp.sum(jnp.where(eye, product, 0.0), axis=0, keepdims=True))
        return out

    def trace_copy(z, col, layer):
        return pltpu.make_async_remote_copy(
            src_ref=trace_own, dst_ref=trace_in.at[me],
            send_sem=trace_send.at[0], recv_sem=trace_recv.at[0],
            device_id=(z, col, layer), device_id_type=MESH,
        )

    everyone = [(z, col, layer) for z in range(n_row) for col in range(n_col)
                for layer in range(n_layer)]

    def add_trace(blocks, start):
        weights = [weight(t, 1, -1) for t in range(tiles)]
        part = spread = others = jnp.zeros((1, blk), jnp.float32)
        if not start:
            part, spread, others = (trace_own[n:n + 1, :] for n in range(3))
        for t in range(tiles if start else 0):
            own = row_panel[me, pl.ds(corner + t * blk, blk), pl.ds(t * blk, blk)]
            line = jnp.sum(
                jnp.where(eye, own.astype(jnp.float32), 0.0), axis=0, keepdims=True)
            part += weight(t, 0, 2) * line
            spread += jnp.where(lanes == me * tiles + t, weights[t], 0.0)
        for block in ([r] if start else []) + blocks:
            for k in range(rows // blk):
                sums = pair_sums(block, k)
                for t in range(tiles):
                    part += weights[t] * sums[t]
                if block is not r:
                    here = block * (rows // blk) + k
                    total = sum(jnp.sum(line, keepdims=True) for line in sums)
                    others += jnp.where(lanes == here, total, 0.0)
        trace_own[0:1, :] = part
        trace_own[1:2, :] = spread
        trace_own[2:3, :] = others

    def send_trace(row):
        trace_in[me] = trace_own[...]
        for z, col, layer in everyone:
            pl.when((z != row) | (col != c) | (layer != l))(
                lambda: trace_copy(z, col, layer).start())

    middle = (last - 1) * CHUNKS
    pairs = {row: list(range(max(row + 1, 2 - row), n_row)) for row in range(n_row)}
    pairs[1] += [0]
    asked = list(range(1, n_row))

    def ready_rows(count, distances):
        def at_hand(b, row):
            arrived = (from_left if b < row else from_right)[row][:count]
            apart = (b * per // n_layer) ^ (row * per // n_layer)
            return ([x for x, _ in arrived].count(b) == CHUNKS
                    and (apart in distances or not relayed))

        return [row for row in asked if all(at_hand(b, row) for b in pairs[row])]

    def diagonals(chosen):
        for row in chosen:
            asked.remove(row)

            @pl.when(on_diagonal & (r == row))
            def _():
                add_trace(pairs[row], True)
                send_trace(row)
                for copy, plan, sent, hold in (
                        (to_left, leftward, sent_left, hold_left),
                        (to_right, rightward, sent_right, hold_right)):
                    if row in hold:
                        for block, q in plan[row][hold[row]:sent[row]]:
                            copy(block, q, row_panel.at[me, span(q)] if block == row
                                 else col_panel.at[block, span(q)]).start()
            hold_left.pop(row, None)
            hold_right.pop(row, None)

    pl.when(has_left)(lambda: pl.semaphore_wait(ready.at[2], 1))
    pl.when(has_right)(lambda: answer(2, (right, c, l)))
    for other in layer_peers:
        side_wait(c * n_layer + other)
    pl.when(on_diagonal & (r == 0))(lambda: add_trace([], True))
    diagonals(ready_rows(0, ()))
    for k in range(CHUNKS // 2):
        z_arrive(k)
    for d in direct:
        plane_arrive(d, 0)
    for k in range(CHUNKS // 2, CHUNKS):
        z_arrive(k)
    for d in direct:
        plane_arrive(d, 1)
    for k in range(CHUNKS, CHUNKS + 1):
        z_arrive(k)
    for other in layer_peers:
        for d in direct:
            side_wait(col_peers[d - 1] * n_layer + other)
    diagonals(ready_rows(CHUNKS + 1, direct))
    for k in range(CHUNKS + 1, CHUNKS + 2):
        z_arrive(k)
    for turn in range(2):
        for d in relayed:
            plane_arrive(d, turn)
    for other in layer_peers:
        for d in relayed:
            side_wait(col_peers[d - 1] * n_layer + other)
    diagonals(ready_rows(CHUNKS + 2, range(n_col)))
    for k in range(CHUNKS + 2, middle):
        z_arrive(k)
    diagonals(list(asked))

    total = None
    for t in range(per):
        term = jnp.dot(
            row_panel[r * per + t], row_panel[me, pl.ds(t * width, width), :],
            preferred_element_type=jnp.float32)
        total = term if total is None else total + term
    updated[...] = total
    inner = has_left & has_right
    for s in range(1, last):
        pl.when((r - s >= 0) & inner)(lambda: add(terms(r - s, 0, rows)))
        pl.when((r + s <= last) & inner)(lambda: add(terms(r + s, 0, rows)))
    for row, arrived in ((0, from_right[0]), (last, from_left[last])):
        @pl.when(r == row)
        def _():
            products = []
            for block in range(n_row):
                chunks = sorted(q for b, q in arrived[:middle] if b == block)
                if chunks:
                    assert chunks == list(range(len(chunks)))
                    products += terms(block, 0, len(chunks) * piece)
            add(products)

    def finish(row, arrived, k):
        block, q = arrived[k]
        if row == 0 and k == last * CHUNKS - 2:
            @pl.when(on_diagonal)
            def _():
                add_trace(pairs[0], False)
                send_trace(0)
        add(terms(block, q * piece, piece))

    for k in range(middle, last * CHUNKS):
        z_arrive(k, finish)

    for i in range(rows // blk):
        flag = jnp.full((blk, blk), branch_flag[i]) == 1
        for k in range(width // blk):
            at = (pl.ds(i * blk, blk), pl.ds(k * blk, blk))
            product = updated[at]
            doubled = 2.0 * row_panel[(me,) + at].astype(jnp.float32) - product
            kept = jnp.full((blk, blk), keep_mask[k, i].astype(jnp.float32))
            updated[at] = jnp.where(flag, product, doubled) * kept

    for row in range(n_row):
        @pl.when(r == row)
        def _():
            for copy, plan, sem in (
                    (to_left, leftward[row], left_send),
                    (to_right, rightward[row], right_send)):
                if plan:
                    blocks = pl.ds(0, len(plan) // CHUNKS)
                    pltpu.make_async_remote_copy(
                        src_ref=col_panel.at[blocks], dst_ref=col_panel.at[blocks],
                        send_sem=sem.at[0], recv_sem=z_recv.at[0, 0],
                        device_id=(left, c, l), device_id_type=MESH,
                    ).wait_send()

    def sent_slots(count, ref, sem):
        pltpu.make_async_remote_copy(
            src_ref=ref.at[pl.ds(0, count)], dst_ref=ref.at[pl.ds(0, count)],
            send_sem=sem.at[0], recv_sem=plane_recv.at[0, 0],
            device_id=(r, c, l), device_id_type=MESH,
        ).wait_send()

    sent_slots(n_col - 1, row_panel, plane_send)
    sent_slots((n_layer - 1) * n_col, row_panel, side_send)

    def heard(count):
        pltpu.make_async_remote_copy(
            src_ref=trace_in.at[pl.ds(0, count)], dst_ref=trace_in.at[pl.ds(0, count)],
            send_sem=trace_send.at[0], recv_sem=trace_recv.at[0],
            device_id=(r, c, l), device_id_type=MESH,
        ).wait_recv()

    pl.when(on_diagonal)(lambda: heard(slots - 1))
    pl.when(jnp.logical_not(on_diagonal))(lambda: heard(slots))
    parts = trace_in[0]
    for slot in range(1, slots):
        parts = parts + trace_in[slot]
    lines[...] = parts
    pl.when(on_diagonal)(
        lambda: sent_slots(n_row * slots - 1, trace_in, trace_send))


def deliver(updated, lines, out, trace):
    out[...] = updated[...]
    trace[0, 0] = jnp.sum(lines[0:1, :] + lines[1:2, :] * lines[2:3, :])


def on_device(sizes, density, block_mask, keep_mask, branch_flag):
    n_row, n_col, n_layer = sizes
    rows, width = density.shape
    blk = rows // block_mask.shape[0]
    dma = pltpu.SemaphoreType.DMA
    slots = n_col * n_layer
    vmem, smem = pl.BlockSpec(memory_space=pltpu.VMEM), pl.BlockSpec(memory_space=pltpu.SMEM)
    hbm = pl.BlockSpec(memory_space=pltpu.HBM)
    panel_bytes = 2 * rows * width * (slots + n_row + 1)
    updated, lines = pl.pallas_call(
        functools.partial(kernel, sizes),
        out_shape=(
            jax.ShapeDtypeStruct((rows, width), jnp.float32),
            jax.ShapeDtypeStruct((3, blk), jnp.float32),
        ),
        in_specs=[hbm, hbm, hbm, hbm],
        out_specs=(vmem, vmem),
        scratch_shapes=[
            pltpu.VMEM((rows, width), jnp.bfloat16),
            pltpu.SMEM(block_mask.T.shape, jnp.int32),
            pltpu.SMEM(keep_mask.T.shape, jnp.int32),
            pltpu.SMEM(branch_flag.shape, jnp.int32),
            pltpu.VMEM((slots, rows, width), jnp.bfloat16),
            pltpu.VMEM((n_row, rows, width), jnp.bfloat16),
            pltpu.VMEM((3, blk), jnp.float32),
            pltpu.VMEM((n_row * slots, 3, blk), jnp.float32),
            dma((4,)),
            dma((1,)),
            dma((slots, 2)),
            dma((1,)),
            dma((1,)),
            dma((1,)),
            dma((n_row, CHUNKS)),
            dma((1,)),
            dma((1,)),
            pltpu.SemaphoreType.REGULAR((3,)),
        ],
        compiler_params=pltpu.CompilerParams(
            collective_id=0, has_side_effects=True,
            vmem_limit_bytes=panel_bytes + 8 * rows * width + (4 << 20)),
    )(*[
        pltpu.with_memory_space_constraint(x, pltpu.HBM)
        for x in (density, block_mask.T, keep_mask.T, branch_flag)
    ])
    updated, trace = pl.pallas_call(
        deliver,
        out_shape=(
            jax.ShapeDtypeStruct((rows, width), jnp.float32),
            jax.ShapeDtypeStruct((1, 1), jnp.float32),
        ),
        in_specs=[vmem, vmem],
        out_specs=(vmem, smem),
        compiler_params=pltpu.CompilerParams(
            vmem_limit_bytes=8 * rows * width + (4 << 20)),
    )(updated, lines)
    return updated, trace[0, 0]


def solution(mesh):
    sizes = tuple(mesh.shape[name] for name in ("row", "col", "layer"))
    in_specs = (
        P("row", ("col", "layer")),
        P("row", ("col", "layer")),
        P("row", ("col", "layer")),
        P("row"),
    )
    out_specs = (P("row", ("col", "layer")), P())
    return jax.shard_map(
        functools.partial(on_device, sizes), mesh=mesh, in_specs=in_specs,
        out_specs=out_specs, check_vma=False,
    )
```

```python
import functools

import jax
import jax.numpy as jnp
from jax import lax
from jax.experimental import pallas as pl
from jax.experimental.pallas import tpu as pltpu
from jax.sharding import PartitionSpec as P

MESH = pl.DeviceIdType.MESH
CHUNKS = 4
AHEAD = 2


def partner_of(index, step, size):
    if size & (size - 1):
        return (index + step) % size
    for bit in range(size.bit_length()):
        if step >> bit & 1:
            index = index + (1 - 2 * ((index // (1 << bit)) % 2)) * (1 << bit)
    return index


def passing_plans(n_row):
    last = n_row - 1
    blocks = [[(b, q) for q in range(CHUNKS)] for b in range(n_row)]
    rightward = [sum(blocks[row::-1], []) for row in range(last)] + [[]]
    leftward = [[]] + [sum(blocks[row:], []) for row in range(1, n_row)]
    leftward[1].append(leftward[1].pop(CHUNKS - 1))
    return rightward, leftward


def kernel(
    sizes, density_hbm, block_hbm, keep_hbm, flag_hbm, updated, lines,
    density, block_mask, keep_mask, branch_flag,
    row_panel, col_panel, trace_own, trace_in, local_sem,
    plane_send, plane_recv, side_send, right_send, left_send, z_recv,
    trace_send, trace_recv, ready,
):
    n_row, n_col, n_layer = sizes
    rows, width = density.shape
    blk = rows // block_mask.shape[1]
    per = rows // width
    piece = rows // CHUNKS
    slots = n_col * n_layer
    last = n_row - 1
    r, c, l = lax.axis_index("row"), lax.axis_index("col"), lax.axis_index("layer")
    me = c * n_layer + l
    has_left, has_right = r > 0, r < last
    left, right = jnp.maximum(r - 1, 0), jnp.minimum(r + 1, last)
    col_peers = [partner_of(c, d, n_col) for d in range(1, n_col)]
    layer_peers = [partner_of(l, d, n_layer) for d in range(1, n_layer)]
    plane_peers = [(p, q) for p in col_peers for q in range(n_layer)]
    plane_peers += [(c, q) for q in layer_peers]

    def span(q):
        return pl.ds(q * piece, piece)

    loads = [
        pltpu.make_async_copy(source, target, local_sem.at[i])
        for i, (source, target) in enumerate(
            [(block_hbm, block_mask)]
            + [(density_hbm.at[span(q)], density.at[span(q)]) for q in range(CHUNKS)]
            + [(keep_hbm, keep_mask), (flag_hbm, branch_flag)])
    ]
    for load in loads:
        load.start()

    barrier = pltpu.get_barrier_semaphore()

    def greet(target):
        pl.semaphore_signal(barrier, inc=1, device_id=target, device_id_type=MESH)

    def answer(which, target):
        pl.semaphore_signal(
            ready.at[which], inc=1, device_id=target, device_id_type=MESH)

    pl.when(has_right)(lambda: greet((right, c, l)))
    for p, q in plane_peers:
        pl.when(p * n_layer + q > me)(functools.partial(greet, (r, p, q)))
    below, above = jnp.where(has_left, 1, 0) + me, slots - 1 - me
    pl.when(below > 0)(lambda: pl.semaphore_wait(barrier, below))
    pl.when(has_left)(lambda: answer(0, (left, c, l)))
    for p, q in plane_peers:
        pl.when(p * n_layer + q < me)(functools.partial(answer, 1, (r, p, q)))
    def mask(q):
        loads[1 + q].wait()
        for i in range(q * piece // blk, (q + 1) * piece // blk):
            for k in range(width // blk):
                at = (pl.ds(i * blk, blk), pl.ds(k * blk, blk))
                kept = jnp.full((blk, blk), block_mask[k, i].astype(jnp.float32))
                row_panel[(me,) + at] = density[at] * kept.astype(jnp.bfloat16)

    loads[0].wait()

    def z_copy(block, q, source, target, sem):
        return pltpu.make_async_remote_copy(
            src_ref=source, dst_ref=col_panel.at[block, span(q)],
            send_sem=sem.at[0], recv_sem=z_recv.at[block, q],
            device_id=(target, c, l), device_id_type=MESH,
        )

    def to_right(block, q, source):
        return z_copy(block, q, source, right, right_send)

    def to_left(block, q, source):
        return z_copy(block, q, source, left, left_send)

    def half_copy(slot, h, sem, target):
        half = pl.ds(h * (rows // 2), rows // 2)
        return pltpu.make_async_remote_copy(
            src_ref=row_panel.at[slot, half], dst_ref=row_panel.at[slot, half],
            send_sem=sem.at[0], recv_sem=plane_recv.at[slot, h],
            device_id=target, device_id_type=MESH,
        )

    def plane_copy(slot, h, peer):
        return half_copy(slot, h, plane_send, (r, peer, l))

    def side_copies(slot, h):
        for other in layer_peers:
            half_copy(slot, h, side_send, (r, c, other)).start()

    def side_wait(slot):
        for h in range(2):
            half_copy(slot, h, side_send, (r, c, l)).wait_recv()

    bits = [d for d in range(1, n_col) if d & (d - 1) == 0]
    relayed = [lo | hi for hi in bits for lo in bits if lo < hi]
    if n_col & (n_col - 1):
        bits, relayed = list(range(1, n_col)), []
    direct = [d for d in range(1, n_col) if d not in relayed]
    halves = {d: (1, 0) if relayed and d > 1 else (0, 1) for d in range(1, n_col)}

    def plane_start(chosen):
        for turn in range(2):
            for d in direct:
                peer = col_peers[d - 1]
                pl.when(chosen(peer))(
                    lambda: plane_copy(me, halves[d][turn], peer).start())

    def plane_arrive(d, turn):
        peer, h = col_peers[d - 1], halves[d][turn]
        slot = peer * n_layer + l
        plane_copy(slot, h, peer).wait_recv()
        for other in bits if relayed and d in bits else []:
            if (other > d) == (h == 0) and other != d:
                plane_copy(slot, h, col_peers[other - 1]).start()
        side_copies(slot, h)

    rightward, leftward = passing_plans(n_row)
    from_left = [[]] + rightward[:-1]
    from_right = leftward[1:] + [[]]

    on_diagonal = me // per == r

    def pass_on(copy, row, plan, first, arrived, stop=None, hold=None):
        while first < len(plan) and (stop is None or first < stop):
            block, q = plan[first]
            if block == row:
                source = row_panel.at[me, span(q)]
            elif (block, q) in arrived:
                source = col_panel.at[block, span(q)]
            else:
                break
            if hold is None or first < hold:
                copy(block, q, source).start()
            else:
                pl.when(jnp.logical_not(on_diagonal))(
                    functools.partial(lambda f: f.start(), copy(block, q, source)))
            first += 1
        return first

    sent_left, sent_right = [0] * n_row, [0] * n_row
    hold_left, hold_right = {1: last * CHUNKS - 3}, {last - 1: 2 * CHUNKS - 1}
    for q in range(CHUNKS):
        mask(q)
        for row in range(1, n_row) if q < AHEAD else []:
            @pl.when(r == row)
            def _():
                sent_left[row] = pass_on(
                    to_left, row, leftward[row], sent_left[row], (), q + 1)
    for load in loads[1 + CHUNKS:]:
        load.wait()
    plane_start(lambda peer: peer < c)
    pl.when(has_right)(lambda: pl.semaphore_wait(ready.at[0], 1))
    for row in range(last):
        @pl.when(r == row)
        def _():
            sent_right[row] = pass_on(to_right, row, rightward[row], 0, (), AHEAD)
    pl.when(above > 0)(lambda: pl.semaphore_wait(ready.at[1], above))
    for row in range(n_row):
        @pl.when(r == row)
        def _():
            sent_left[row] = pass_on(
                to_left, row, leftward[row], sent_left[row], (), None, hold_left.get(row))
            sent_right[row] = pass_on(
                to_right, row, rightward[row], sent_right[row], (), None, hold_right.get(row))
    plane_start(lambda peer: peer > c)
    for h in range(2):
        side_copies(me, h)

    def z_arrive(k, then=None):
        for row in range(n_row):
            if k < max(len(from_right[row]), len(from_left[row])):
                @pl.when(r == row)
                def _():
                    if k < len(from_right[row]):
                        block, q = from_right[row][k]
                        to_left(block, q, col_panel.at[block, span(q)]).wait_recv()
                        sent_left[row] = pass_on(
                            to_left, row, leftward[row], sent_left[row],
                            from_right[row][:k + 1], None, hold_left.get(row))
                        if then:
                            then(row, from_right[row], k)
                    if k < len(from_left[row]):
                        block, q = from_left[row][k]
                        to_right(block, q, col_panel.at[block, span(q)]).wait_recv()
                        sent_right[row] = pass_on(
                            to_right, row, rightward[row], sent_right[row],
                            from_left[row][:k + 1], None, hold_right.get(row))
                        if then:
                            then(row, from_left[row], k)

    def terms(block, start, size):
        out = []
        while size:
            step = min(size, width - start % width)
            out.append(jnp.dot(
                row_panel[block * per + start // width, :, pl.ds(start % width, step)],
                col_panel[block, pl.ds(start, step), :],
                preferred_element_type=jnp.float32))
            start, size = start + step, size - step
        return out

    def add(products):
        total = products[0]
        for product in products[1:]:
            total = total + product
        updated[...] += total

    corner = pl.multiple_of((me % per) * width, width)
    tiles = width // blk
    lanes = lax.broadcasted_iota(jnp.int32, (1, blk), 1)
    eye = (lax.broadcasted_iota(jnp.int32, (blk, blk), 0)
           == lax.broadcasted_iota(jnp.int32, (blk, blk), 1))

    def weight(t, if_square, otherwise):
        kept = keep_mask[t, (me % per) * tiles + t]
        chosen = jnp.where(branch_flag[(me % per) * tiles + t] == 1, if_square, otherwise)
        return (kept * chosen).astype(jnp.float32)

    def pair_sums(block, k):
        slot = block * per + k * blk // width
        out = []
        for t in range(tiles):
            ours = row_panel[slot, pl.ds(corner + t * blk, blk), pl.ds(k * blk % width, blk)]
            if block is r:
                theirs = row_panel[me, pl.ds(k * blk, blk), pl.ds(t * blk, blk)]
            else:
                theirs = col_panel[block, pl.ds(k * blk, blk), pl.ds(t * blk, blk)]
            product = jnp.dot(ours, theirs, preferred_element_type=jnp.float32)
            out.append(jnp.sum(jnp.where(eye, product, 0.0), axis=0, keepdims=True))
        return out

    def trace_copy(z, col, layer):
        return pltpu.make_async_remote_copy(
            src_ref=trace_own, dst_ref=trace_in.at[me],
            send_sem=trace_send.at[0], recv_sem=trace_recv.at[0],
            device_id=(z, col, layer), device_id_type=MESH,
        )

    everyone = [(z, col, layer) for z in range(n_row) for col in range(n_col)
                for layer in range(n_layer)]

    def add_trace(chunks, start):
        weights = [weight(t, 1, -1) for t in range(tiles)]
        part = spread = others = jnp.zeros((1, blk), jnp.float32)
        if not start:
            part, spread, others = (trace_own[n:n + 1, :] for n in range(3))
        for t in range(tiles if start else 0):
            own = row_panel[me, pl.ds(corner + t * blk, blk), pl.ds(t * blk, blk)]
            line = jnp.sum(
                jnp.where(eye, own.astype(jnp.float32), 0.0), axis=0, keepdims=True)
            part += weight(t, 0, 2) * line
            spread += jnp.where(lanes == me * tiles + t, weights[t], 0.0)
        every = range(rows // blk)
        for block, k in ([(r, k) for k in every] if start else []) + chunks:
            sums = pair_sums(block, k)
            for t in range(tiles):
                part += weights[t] * sums[t]
            if block is not r:
                here = block * (rows // blk) + k
                total = sum(jnp.sum(line, keepdims=True) for line in sums)
                others += jnp.where(lanes == here, total, 0.0)
        trace_own[0:1, :] = part
        trace_own[1:2, :] = spread
        trace_own[2:3, :] = others

    def send_trace(row):
        trace_in[me] = trace_own[...]
        for z, col, layer in everyone:
            pl.when((z != row) | (col != c) | (layer != l))(
                lambda: trace_copy(z, col, layer).start())

    middle = (last - 1) * CHUNKS
    pairs = {row: list(range(max(row + 1, 2 - row), n_row)) for row in range(n_row)}
    pairs[1] += [0]
    asked = list(range(1, n_row))

    def ready_rows(count, distances):
        def at_hand(b, row):
            arrived = (from_left if b < row else from_right)[row][:count]
            apart = (b * per // n_layer) ^ (row * per // n_layer)
            return ([x for x, _ in arrived].count(b) == CHUNKS
                    and (apart in distances or not relayed))

        return [row for row in asked if all(at_hand(b, row) for b in pairs[row])]

    def diagonals(chosen):
        for row in chosen:
            asked.remove(row)

            @pl.when(on_diagonal & (r == row))
            def _():
                add_trace([(b, k) for b in pairs[row] for k in range(rows // blk)], True)
                send_trace(row)
                for copy, plan, sent, hold in (
                        (to_left, leftward, sent_left, hold_left),
                        (to_right, rightward, sent_right, hold_right)):
                    if row in hold:
                        for block, q in plan[row][hold[row]:sent[row]]:
                            copy(block, q, row_panel.at[me, span(q)] if block == row
                                 else col_panel.at[block, span(q)]).start()
            hold_left.pop(row, None)
            hold_right.pop(row, None)

    pl.when(has_left)(lambda: pl.semaphore_wait(ready.at[2], 1))
    pl.when(has_right)(lambda: answer(2, (right, c, l)))
    for other in layer_peers:
        side_wait(c * n_layer + other)
    pl.when(on_diagonal & (r == 0))(lambda: add_trace([], True))
    diagonals(ready_rows(0, ()))
    for k in range(CHUNKS // 2):
        z_arrive(k)
    for d in direct:
        plane_arrive(d, 0)
    for k in range(CHUNKS // 2, CHUNKS):
        z_arrive(k)
    for d in direct:
        plane_arrive(d, 1)
    for k in range(CHUNKS, CHUNKS + 1):
        z_arrive(k)
    for other in layer_peers:
        for d in direct:
            side_wait(col_peers[d - 1] * n_layer + other)
    diagonals(ready_rows(CHUNKS + 1, direct))
    for k in range(CHUNKS + 1, CHUNKS + 2):
        z_arrive(k)
    for turn in range(2):
        for d in relayed:
            plane_arrive(d, turn)
    for other in layer_peers:
        for d in relayed:
            side_wait(col_peers[d - 1] * n_layer + other)
    diagonals(ready_rows(CHUNKS + 2, range(n_col)))
    for k in range(CHUNKS + 2, middle):
        z_arrive(k)
    diagonals(list(asked))

    total = None
    for t in range(per):
        term = jnp.dot(
            row_panel[r * per + t], row_panel[me, pl.ds(t * width, width), :],
            preferred_element_type=jnp.float32)
        total = term if total is None else total + term
    updated[...] = total
    inner = has_left & has_right
    for s in range(1, last):
        pl.when((r - s >= 0) & inner)(lambda: add(terms(r - s, 0, rows)))
        pl.when((r + s <= last) & inner)(lambda: add(terms(r + s, 0, rows)))
    for row, arrived in ((0, from_right[0]), (last, from_left[last])):
        @pl.when(r == row)
        def _():
            products = []
            for block in range(n_row):
                chunks = sorted(q for b, q in arrived[:middle] if b == block)
                if chunks:
                    assert chunks == list(range(len(chunks)))
                    products += terms(block, 0, len(chunks) * piece)
            add(products)

    def finish(row, arrived, k):
        block, q = arrived[k]
        if row == 0 and block in pairs[0]:
            @pl.when(on_diagonal)
            def _():
                add_trace(parts_of([(block, q)]), False)
                if k == last * CHUNKS - 2:
                    send_trace(0)
        add(terms(block, q * piece, piece))

    def parts_of(chunks):
        share = piece // blk
        return [(b, q * share + k) for b, q in chunks if b in pairs[0] for k in range(share)]

    pl.when(on_diagonal & (r == 0))(
        lambda: add_trace(parts_of(from_right[0][:middle]), False))
    for k in range(middle, last * CHUNKS):
        z_arrive(k, finish)

    for i in range(rows // blk):
        flag = jnp.full((blk, blk), branch_flag[i]) == 1
        for k in range(width // blk):
            at = (pl.ds(i * blk, blk), pl.ds(k * blk, blk))
            product = updated[at]
            doubled = 2.0 * row_panel[(me,) + at].astype(jnp.float32) - product
            kept = jnp.full((blk, blk), keep_mask[k, i].astype(jnp.float32))
            updated[at] = jnp.where(flag, product, doubled) * kept

    for row in range(n_row):
        @pl.when(r == row)
        def _():
            for copy, plan, sem in (
                    (to_left, leftward[row], left_send),
                    (to_right, rightward[row], right_send)):
                if plan:
                    blocks = pl.ds(0, len(plan) // CHUNKS)
                    pltpu.make_async_remote_copy(
                        src_ref=col_panel.at[blocks], dst_ref=col_panel.at[blocks],
                        send_sem=sem.at[0], recv_sem=z_recv.at[0, 0],
                        device_id=(left, c, l), device_id_type=MESH,
                    ).wait_send()

    def sent_slots(count, ref, sem):
        pltpu.make_async_remote_copy(
            src_ref=ref.at[pl.ds(0, count)], dst_ref=ref.at[pl.ds(0, count)],
            send_sem=sem.at[0], recv_sem=plane_recv.at[0, 0],
            device_id=(r, c, l), device_id_type=MESH,
        ).wait_send()

    sent_slots(n_col - 1, row_panel, plane_send)
    sent_slots((n_layer - 1) * n_col, row_panel, side_send)

    def heard(count):
        pltpu.make_async_remote_copy(
            src_ref=trace_in.at[pl.ds(0, count)], dst_ref=trace_in.at[pl.ds(0, count)],
            send_sem=trace_send.at[0], recv_sem=trace_recv.at[0],
            device_id=(r, c, l), device_id_type=MESH,
        ).wait_recv()

    pl.when(on_diagonal)(lambda: heard(slots - 1))
    pl.when(jnp.logical_not(on_diagonal))(lambda: heard(slots))
    parts = trace_in[0]
    for slot in range(1, slots):
        parts = parts + trace_in[slot]
    lines[...] = parts
    pl.when(on_diagonal)(
        lambda: sent_slots(n_row * slots - 1, trace_in, trace_send))


def deliver(updated, lines, out, trace):
    out[...] = updated[...]
    trace[0, 0] = jnp.sum(lines[0:1, :] + lines[1:2, :] * lines[2:3, :])


def on_device(sizes, density, block_mask, keep_mask, branch_flag):
    n_row, n_col, n_layer = sizes
    rows, width = density.shape
    blk = rows // block_mask.shape[0]
    dma = pltpu.SemaphoreType.DMA
    slots = n_col * n_layer
    vmem, smem = pl.BlockSpec(memory_space=pltpu.VMEM), pl.BlockSpec(memory_space=pltpu.SMEM)
    hbm = pl.BlockSpec(memory_space=pltpu.HBM)
    panel_bytes = 2 * rows * width * (slots + n_row + 1)
    updated, lines = pl.pallas_call(
        functools.partial(kernel, sizes),
        out_shape=(
            jax.ShapeDtypeStruct((rows, width), jnp.float32),
            jax.ShapeDtypeStruct((3, blk), jnp.float32),
        ),
        in_specs=[hbm, hbm, hbm, hbm],
        out_specs=(vmem, vmem),
        scratch_shapes=[
            pltpu.VMEM((rows, width), jnp.bfloat16),
            pltpu.SMEM(block_mask.T.shape, jnp.int32),
            pltpu.SMEM(keep_mask.T.shape, jnp.int32),
            pltpu.SMEM(branch_flag.shape, jnp.int32),
            pltpu.VMEM((slots, rows, width), jnp.bfloat16),
            pltpu.VMEM((n_row, rows, width), jnp.bfloat16),
            pltpu.VMEM((3, blk), jnp.float32),
            pltpu.VMEM((n_row * slots, 3, blk), jnp.float32),
            dma((CHUNKS + 3,)),
            dma((1,)),
            dma((slots, 2)),
            dma((1,)),
            dma((1,)),
            dma((1,)),
            dma((n_row, CHUNKS)),
            dma((1,)),
            dma((1,)),
            pltpu.SemaphoreType.REGULAR((3,)),
        ],
        compiler_params=pltpu.CompilerParams(
            collective_id=0, has_side_effects=True,
            vmem_limit_bytes=panel_bytes + 8 * rows * width + (4 << 20)),
    )(*[
        pltpu.with_memory_space_constraint(x, pltpu.HBM)
        for x in (density, block_mask.T, keep_mask.T, branch_flag)
    ])
    updated, trace = pl.pallas_call(
        deliver,
        out_shape=(
            jax.ShapeDtypeStruct((rows, width), jnp.float32),
            jax.ShapeDtypeStruct((1, 1), jnp.float32),
        ),
        in_specs=[vmem, vmem],
        out_specs=(vmem, smem),
        compiler_params=pltpu.CompilerParams(
            vmem_limit_bytes=8 * rows * width + (4 << 20)),
    )(updated, lines)
    return updated, trace[0, 0]


def solution(mesh):
    sizes = tuple(mesh.shape[name] for name in ("row", "col", "layer"))
    in_specs = (
        P("row", ("col", "layer")),
        P("row", ("col", "layer")),
        P("row", ("col", "layer")),
        P("row"),
    )
    out_specs = (P("row", ("col", "layer")), P())
    return jax.shard_map(
        functools.partial(on_device, sizes), mesh=mesh, in_specs=in_specs,
        out_specs=out_specs, check_vma=False,
    )
```

```python
import functools

import jax
import jax.numpy as jnp
from jax import lax
from jax.experimental import pallas as pl
from jax.experimental.pallas import tpu as pltpu
from jax.sharding import PartitionSpec as P

MESH = pl.DeviceIdType.MESH
CHUNKS = 4
AHEAD = 2


def partner_of(index, step, size):
    if size & (size - 1):
        return (index + step) % size
    for bit in range(size.bit_length()):
        if step >> bit & 1:
            index = index + (1 - 2 * ((index // (1 << bit)) % 2)) * (1 << bit)
    return index


def passing_plans(n_row):
    last = n_row - 1
    blocks = [[(b, q) for q in range(CHUNKS)] for b in range(n_row)]
    rightward = [sum(blocks[row::-1], []) for row in range(last)] + [[]]
    leftward = [[]] + [sum(blocks[row:], []) for row in range(1, n_row)]
    leftward[1].append(leftward[1].pop(CHUNKS - 1))
    return rightward, leftward


def kernel(
    sizes, density_hbm, block_hbm, keep_hbm, flag_hbm, updated, lines,
    density, block_mask, keep_mask, branch_flag,
    row_panel, col_panel, trace_own, trace_in, local_sem,
    plane_send, plane_recv, side_send, right_send, left_send, z_recv,
    trace_send, trace_recv, trace_swap, trace_sum, ready,
):
    n_row, n_col, n_layer = sizes
    rows, width = density.shape
    blk = rows // block_mask.shape[1]
    per = rows // width
    piece = rows // CHUNKS
    slots = n_col * n_layer
    last = n_row - 1
    r, c, l = lax.axis_index("row"), lax.axis_index("col"), lax.axis_index("layer")
    me = c * n_layer + l
    has_left, has_right = r > 0, r < last
    left, right = jnp.maximum(r - 1, 0), jnp.minimum(r + 1, last)
    col_peers = [partner_of(c, d, n_col) for d in range(1, n_col)]
    layer_peers = [partner_of(l, d, n_layer) for d in range(1, n_layer)]
    plane_peers = [(p, q) for p in col_peers for q in range(n_layer)]
    plane_peers += [(c, q) for q in layer_peers]

    def span(q):
        return pl.ds(q * piece, piece)

    loads = [
        pltpu.make_async_copy(source, target, local_sem.at[i])
        for i, (source, target) in enumerate(
            [(block_hbm, block_mask)]
            + [(density_hbm.at[span(q)], density.at[span(q)]) for q in range(CHUNKS)]
            + [(keep_hbm, keep_mask), (flag_hbm, branch_flag)])
    ]
    for load in loads:
        load.start()

    barrier = pltpu.get_barrier_semaphore()

    def greet(target):
        pl.semaphore_signal(barrier, inc=1, device_id=target, device_id_type=MESH)

    def answer(which, target):
        pl.semaphore_signal(
            ready.at[which], inc=1, device_id=target, device_id_type=MESH)

    pl.when(has_right)(lambda: greet((right, c, l)))
    for p, q in plane_peers:
        pl.when(p * n_layer + q > me)(functools.partial(greet, (r, p, q)))
    below, above = jnp.where(has_left, 1, 0) + me, slots - 1 - me
    pl.when(below > 0)(lambda: pl.semaphore_wait(barrier, below))
    pl.when(has_left)(lambda: answer(0, (left, c, l)))
    for p, q in plane_peers:
        pl.when(p * n_layer + q < me)(functools.partial(answer, 1, (r, p, q)))
    def mask(q):
        loads[1 + q].wait()
        for i in range(q * piece // blk, (q + 1) * piece // blk):
            for k in range(width // blk):
                at = (pl.ds(i * blk, blk), pl.ds(k * blk, blk))
                kept = jnp.full((blk, blk), block_mask[k, i].astype(jnp.float32))
                row_panel[(me,) + at] = density[at] * kept.astype(jnp.bfloat16)

    loads[0].wait()

    def z_copy(block, q, source, target, sem):
        return pltpu.make_async_remote_copy(
            src_ref=source, dst_ref=col_panel.at[block, span(q)],
            send_sem=sem.at[0], recv_sem=z_recv.at[block, q],
            device_id=(target, c, l), device_id_type=MESH,
        )

    def to_right(block, q, source):
        return z_copy(block, q, source, right, right_send)

    def to_left(block, q, source):
        return z_copy(block, q, source, left, left_send)

    def half_copy(slot, h, sem, target):
        half = pl.ds(h * (rows // 2), rows // 2)
        return pltpu.make_async_remote_copy(
            src_ref=row_panel.at[slot, half], dst_ref=row_panel.at[slot, half],
            send_sem=sem.at[0], recv_sem=plane_recv.at[slot, h],
            device_id=target, device_id_type=MESH,
        )

    def plane_copy(slot, h, peer):
        return half_copy(slot, h, plane_send, (r, peer, l))

    def side_copies(slot, h):
        for other in layer_peers:
            half_copy(slot, h, side_send, (r, c, other)).start()

    def side_wait(slot):
        for h in range(2):
            half_copy(slot, h, side_send, (r, c, l)).wait_recv()

    bits = [d for d in range(1, n_col) if d & (d - 1) == 0]
    relayed = [lo | hi for hi in bits for lo in bits if lo < hi]
    if n_col & (n_col - 1):
        bits, relayed = list(range(1, n_col)), []
    direct = [d for d in range(1, n_col) if d not in relayed]
    halves = {d: (1, 0) if relayed and d > 1 else (0, 1) for d in range(1, n_col)}

    def plane_start(chosen):
        for turn in range(2):
            for d in direct:
                peer = col_peers[d - 1]
                pl.when(chosen(peer))(
                    lambda: plane_copy(me, halves[d][turn], peer).start())

    def plane_arrive(d, turn):
        peer, h = col_peers[d - 1], halves[d][turn]
        slot = peer * n_layer + l
        plane_copy(slot, h, peer).wait_recv()
        for other in bits if relayed and d in bits else []:
            if (other > d) == (h == 0) and other != d:
                plane_copy(slot, h, col_peers[other - 1]).start()
        side_copies(slot, h)

    rightward, leftward = passing_plans(n_row)
    from_left = [[]] + rightward[:-1]
    from_right = leftward[1:] + [[]]

    on_diagonal = me // per == r

    def pass_on(copy, row, plan, first, arrived, stop=None, hold=None):
        while first < len(plan) and (stop is None or first < stop):
            block, q = plan[first]
            if block == row:
                source = row_panel.at[me, span(q)]
            elif (block, q) in arrived:
                source = col_panel.at[block, span(q)]
            else:
                break
            if hold is None or first < hold:
                copy(block, q, source).start()
            else:
                pl.when(jnp.logical_not(on_diagonal))(
                    functools.partial(lambda f: f.start(), copy(block, q, source)))
            first += 1
        return first

    sent_left, sent_right = [0] * n_row, [0] * n_row
    hold_left, hold_right = {1: last * CHUNKS - 3}, {last - 1: 2 * CHUNKS - 1}
    for q in range(CHUNKS):
        mask(q)
        for row in range(1, n_row) if q < AHEAD else []:
            @pl.when(r == row)
            def _():
                sent_left[row] = pass_on(
                    to_left, row, leftward[row], sent_left[row], (), q + 1)
    for load in loads[1 + CHUNKS:]:
        load.wait()
    plane_start(lambda peer: peer < c)
    pl.when(has_right)(lambda: pl.semaphore_wait(ready.at[0], 1))
    for row in range(last):
        @pl.when(r == row)
        def _():
            sent_right[row] = pass_on(to_right, row, rightward[row], 0, (), AHEAD)
    pl.when(above > 0)(lambda: pl.semaphore_wait(ready.at[1], above))
    for row in range(n_row):
        @pl.when(r == row)
        def _():
            sent_left[row] = pass_on(
                to_left, row, leftward[row], sent_left[row], (), None, hold_left.get(row))
            sent_right[row] = pass_on(
                to_right, row, rightward[row], sent_right[row], (), None, hold_right.get(row))
    plane_start(lambda peer: peer > c)
    for h in range(2):
        side_copies(me, h)

    def z_arrive(k, then=None):
        for row in range(n_row):
            if k < max(len(from_right[row]), len(from_left[row])):
                @pl.when(r == row)
                def _():
                    if k < len(from_right[row]):
                        block, q = from_right[row][k]
                        to_left(block, q, col_panel.at[block, span(q)]).wait_recv()
                        sent_left[row] = pass_on(
                            to_left, row, leftward[row], sent_left[row],
                            from_right[row][:k + 1], None, hold_left.get(row))
                        if then:
                            then(row, from_right[row], k)
                    if k < len(from_left[row]):
                        block, q = from_left[row][k]
                        to_right(block, q, col_panel.at[block, span(q)]).wait_recv()
                        sent_right[row] = pass_on(
                            to_right, row, rightward[row], sent_right[row],
                            from_left[row][:k + 1], None, hold_right.get(row))
                        if then:
                            then(row, from_left[row], k)

    def terms(block, start, size):
        out = []
        while size:
            step = min(size, width - start % width)
            out.append(jnp.dot(
                row_panel[block * per + start // width, :, pl.ds(start % width, step)],
                col_panel[block, pl.ds(start, step), :],
                preferred_element_type=jnp.float32))
            start, size = start + step, size - step
        return out

    def add(products):
        total = products[0]
        for product in products[1:]:
            total = total + product
        updated[...] += total

    corner = pl.multiple_of((me % per) * width, width)
    tiles = width // blk
    lanes = lax.broadcasted_iota(jnp.int32, (1, blk), 1)
    eye = (lax.broadcasted_iota(jnp.int32, (blk, blk), 0)
           == lax.broadcasted_iota(jnp.int32, (blk, blk), 1))

    def weight(t, if_square, otherwise):
        kept = keep_mask[t, (me % per) * tiles + t]
        chosen = jnp.where(branch_flag[(me % per) * tiles + t] == 1, if_square, otherwise)
        return (kept * chosen).astype(jnp.float32)

    def pair_sums(block, k):
        slot = block * per + k * blk // width
        out = []
        for t in range(tiles):
            ours = row_panel[slot, pl.ds(corner + t * blk, blk), pl.ds(k * blk % width, blk)]
            if block is r:
                theirs = row_panel[me, pl.ds(k * blk, blk), pl.ds(t * blk, blk)]
            else:
                theirs = col_panel[block, pl.ds(k * blk, blk), pl.ds(t * blk, blk)]
            product = jnp.dot(ours, theirs, preferred_element_type=jnp.float32)
            out.append(jnp.sum(jnp.where(eye, product, 0.0), axis=0, keepdims=True))
        return out

    def trace_copy(z, col, layer):
        return pltpu.make_async_remote_copy(
            src_ref=trace_own, dst_ref=trace_in.at[me],
            send_sem=trace_send.at[0], recv_sem=trace_recv.at[0],
            device_id=(z, col, layer), device_id_type=MESH,
        )

    assert per % n_layer == 0
    firsts = per // n_layer

    def swap_copy(other):
        return pltpu.make_async_remote_copy(
            src_ref=trace_own, dst_ref=trace_swap.at[l],
            send_sem=trace_send.at[0], recv_sem=trace_recv.at[1],
            device_id=(r, c, other), device_id_type=MESH,
        )

    def sum_copy(z, col):
        return pltpu.make_async_remote_copy(
            src_ref=trace_sum, dst_ref=trace_in.at[me],
            send_sem=trace_send.at[0], recv_sem=trace_recv.at[0],
            device_id=(z, col, l), device_id_type=MESH,
        )

    def send_first():
        trace_swap[l] = trace_own[...]
        for other in layer_peers:
            swap_copy(other).start()
        if n_layer > 1:
            pltpu.make_async_remote_copy(
                src_ref=trace_in.at[pl.ds(0, n_layer - 1)],
                dst_ref=trace_in.at[pl.ds(0, n_layer - 1)],
                send_sem=trace_send.at[0], recv_sem=trace_recv.at[1],
                device_id=(r, c, l), device_id_type=MESH,
            ).wait_recv()
        total = trace_swap[0]
        for layer in range(1, n_layer):
            total = total + trace_swap[layer]
        trace_sum[...] = total
        trace_in[me] = total
        for z in range(n_row - 1, -1, -1):
            for col in range(n_col):
                pl.when((z != r) | (col != c))(lambda: sum_copy(z, col).start())

    everyone = [(z, col, layer) for z in range(n_row) for col in range(n_col)
                for layer in range(n_layer)]

    def add_trace(chunks, start):
        weights = [weight(t, 1, -1) for t in range(tiles)]
        part = spread = others = jnp.zeros((1, blk), jnp.float32)
        if not start:
            part, spread, others = (trace_own[n:n + 1, :] for n in range(3))
        for t in range(tiles if start else 0):
            own = row_panel[me, pl.ds(corner + t * blk, blk), pl.ds(t * blk, blk)]
            line = jnp.sum(
                jnp.where(eye, own.astype(jnp.float32), 0.0), axis=0, keepdims=True)
            part += weight(t, 0, 2) * line
            spread += jnp.where(lanes == me * tiles + t, weights[t], 0.0)
        every = range(rows // blk)
        for block, k in ([(r, k) for k in every] if start else []) + chunks:
            sums = pair_sums(block, k)
            for t in range(tiles):
                part += weights[t] * sums[t]
            if block is not r:
                here = block * (rows // blk) + k
                total = sum(jnp.sum(line, keepdims=True) for line in sums)
                others += jnp.where(lanes == here, total, 0.0)
        trace_own[0:1, :] = part
        trace_own[1:2, :] = spread
        trace_own[2:3, :] = others

    def send_trace(row):
        trace_in[me] = trace_own[...]
        for z, col, layer in everyone:
            pl.when((z != row) | (col != c) | (layer != l))(
                lambda: trace_copy(z, col, layer).start())

    middle = (last - 1) * CHUNKS
    pairs = {row: list(range(max(row + 1, 2 - row), n_row)) for row in range(n_row)}
    pairs[1] += [0]
    asked = list(range(1, n_row))

    def ready_rows(count, distances):
        def at_hand(b, row):
            arrived = (from_left if b < row else from_right)[row][:count]
            apart = (b * per // n_layer) ^ (row * per // n_layer)
            return ([x for x, _ in arrived].count(b) == CHUNKS
                    and (apart in distances or not relayed))

        return [row for row in asked if all(at_hand(b, row) for b in pairs[row])]

    def diagonals(chosen):
        for row in chosen:
            asked.remove(row)

            @pl.when(on_diagonal & (r == row))
            def _():
                add_trace([(b, k) for b in pairs[row] for k in range(rows // blk)], True)
                send_trace(row)
                for copy, plan, sent, hold in (
                        (to_left, leftward, sent_left, hold_left),
                        (to_right, rightward, sent_right, hold_right)):
                    if row in hold:
                        for block, q in plan[row][hold[row]:sent[row]]:
                            copy(block, q, row_panel.at[me, span(q)] if block == row
                                 else col_panel.at[block, span(q)]).start()
            hold_left.pop(row, None)
            hold_right.pop(row, None)

    pl.when(has_left)(lambda: pl.semaphore_wait(ready.at[2], 1))
    pl.when(has_right)(lambda: answer(2, (right, c, l)))
    for other in layer_peers:
        side_wait(c * n_layer + other)
    pl.when(on_diagonal & (r == 0))(lambda: add_trace([], True))
    diagonals(ready_rows(0, ()))
    for k in range(CHUNKS // 2):
        z_arrive(k)
    for d in direct:
        plane_arrive(d, 0)
    for k in range(CHUNKS // 2, CHUNKS):
        z_arrive(k)
    for d in direct:
        plane_arrive(d, 1)
    for k in range(CHUNKS, CHUNKS + 1):
        z_arrive(k)
    def sides(chosen):
        for other in layer_peers:
            for d in chosen:
                side_wait(col_peers[d - 1] * n_layer + other)

    soon = ready_rows(CHUNKS + 1, direct)
    in_soon = functools.reduce(jnp.logical_or, [r == row for row in soon], r < 0)
    pl.when(in_soon)(lambda: sides(direct))
    diagonals(soon)
    for k in range(CHUNKS + 1, CHUNKS + 2):
        z_arrive(k)
    for turn in range(2):
        for d in relayed:
            plane_arrive(d, turn)
    for k in range(CHUNKS + 2, middle):
        z_arrive(k)
    pl.when(jnp.logical_not(in_soon))(lambda: sides(direct))
    sides(relayed)
    diagonals(list(asked))

    total = None
    for t in range(per):
        term = jnp.dot(
            row_panel[r * per + t], row_panel[me, pl.ds(t * width, width), :],
            preferred_element_type=jnp.float32)
        total = term if total is None else total + term
    updated[...] = total
    inner = has_left & has_right
    for s in range(1, last):
        pl.when((r - s >= 0) & inner)(lambda: add(terms(r - s, 0, rows)))
        pl.when((r + s <= last) & inner)(lambda: add(terms(r + s, 0, rows)))
    for row, arrived in ((0, from_right[0]), (last, from_left[last])):
        @pl.when(r == row)
        def _():
            products = []
            for block in range(n_row):
                chunks = sorted(q for b, q in arrived[:middle] if b == block)
                if chunks:
                    assert chunks == list(range(len(chunks)))
                    products += terms(block, 0, len(chunks) * piece)
            add(products)

    def finish(row, arrived, k):
        block, q = arrived[k]
        if row == 0 and block in pairs[0]:
            @pl.when(on_diagonal)
            def _():
                add_trace(parts_of([(block, q)]), False)
                if k == last * CHUNKS - 2:
                    send_first()
        if k < last * CHUNKS - 1:
            add(terms(block, q * piece, piece))
        else:
            update(terms(block, q * piece, piece))

    def update(products):
        for i in range(rows // blk):
            flag = jnp.full((blk, blk), branch_flag[i]) == 1
            for k in range(width // blk):
                at = (pl.ds(i * blk, blk), pl.ds(k * blk, blk))
                square = updated[at]
                for product in products:
                    square += product[i * blk:(i + 1) * blk, k * blk:(k + 1) * blk]
                doubled = 2.0 * row_panel[(me,) + at].astype(jnp.float32) - square
                kept = jnp.full((blk, blk), keep_mask[k, i].astype(jnp.float32))
                updated[at] = jnp.where(flag, square, doubled) * kept

    def parts_of(chunks):
        share = piece // blk
        return [(b, q * share + k) for b, q in chunks if b in pairs[0] for k in range(share)]

    pl.when(on_diagonal & (r == 0))(
        lambda: add_trace(parts_of(from_right[0][:middle]), False))
    for k in range(middle, last * CHUNKS):
        z_arrive(k, finish)

    pl.when(inner)(lambda: update([]))

    for row in range(n_row):
        @pl.when(r == row)
        def _():
            for copy, plan, sem in (
                    (to_left, leftward[row], left_send),
                    (to_right, rightward[row], right_send)):
                if plan:
                    blocks = pl.ds(0, len(plan) // CHUNKS)
                    pltpu.make_async_remote_copy(
                        src_ref=col_panel.at[blocks], dst_ref=col_panel.at[blocks],
                        send_sem=sem.at[0], recv_sem=z_recv.at[0, 0],
                        device_id=(left, c, l), device_id_type=MESH,
                    ).wait_send()

    def sent_slots(count, ref, sem):
        pltpu.make_async_remote_copy(
            src_ref=ref.at[pl.ds(0, count)], dst_ref=ref.at[pl.ds(0, count)],
            send_sem=sem.at[0], recv_sem=plane_recv.at[0, 0],
            device_id=(r, c, l), device_id_type=MESH,
        ).wait_send()

    sent_slots(n_col - 1, row_panel, plane_send)
    sent_slots((n_layer - 1) * n_col, row_panel, side_send)

    def heard(count):
        pltpu.make_async_remote_copy(
            src_ref=trace_in.at[pl.ds(0, count)], dst_ref=trace_in.at[pl.ds(0, count)],
            send_sem=trace_send.at[0], recv_sem=trace_recv.at[0],
            device_id=(r, c, l), device_id_type=MESH,
        ).wait_recv()

    pl.when(on_diagonal)(lambda: heard(slots - per + firsts - 1))
    pl.when(jnp.logical_not(on_diagonal))(lambda: heard(slots - per + firsts))
    parts = trace_in[l]
    for slot in range(1, firsts):
        parts = parts + trace_in[slot * n_layer + l]
    for slot in range(per, slots):
        parts = parts + trace_in[slot]
    lines[...] = parts
    pl.when(on_diagonal & has_left)(
        lambda: sent_slots(n_row * slots - 1, trace_in, trace_send))
    pl.when(on_diagonal & jnp.logical_not(has_left))(
        lambda: sent_slots(n_row * n_col + n_layer - 2, trace_in, trace_send))


def deliver(updated, lines, out, trace):
    out[...] = updated[...]
    trace[0, 0] = jnp.sum(lines[0:1, :] + lines[1:2, :] * lines[2:3, :])


def on_device(sizes, density, block_mask, keep_mask, branch_flag):
    n_row, n_col, n_layer = sizes
    rows, width = density.shape
    blk = rows // block_mask.shape[0]
    dma = pltpu.SemaphoreType.DMA
    slots = n_col * n_layer
    vmem, smem = pl.BlockSpec(memory_space=pltpu.VMEM), pl.BlockSpec(memory_space=pltpu.SMEM)
    hbm = pl.BlockSpec(memory_space=pltpu.HBM)
    panel_bytes = 2 * rows * width * (slots + n_row + 1)
    updated, lines = pl.pallas_call(
        functools.partial(kernel, sizes),
        out_shape=(
            jax.ShapeDtypeStruct((rows, width), jnp.float32),
            jax.ShapeDtypeStruct((3, blk), jnp.float32),
        ),
        in_specs=[hbm, hbm, hbm, hbm],
        out_specs=(vmem, vmem),
        scratch_shapes=[
            pltpu.VMEM((rows, width), jnp.bfloat16),
            pltpu.SMEM(block_mask.T.shape, jnp.int32),
            pltpu.SMEM(keep_mask.T.shape, jnp.int32),
            pltpu.SMEM(branch_flag.shape, jnp.int32),
            pltpu.VMEM((slots, rows, width), jnp.bfloat16),
            pltpu.VMEM((n_row, rows, width), jnp.bfloat16),
            pltpu.VMEM((3, blk), jnp.float32),
            pltpu.VMEM((n_row * slots, 3, blk), jnp.float32),
            dma((CHUNKS + 3,)),
            dma((1,)),
            dma((slots, 2)),
            dma((1,)),
            dma((1,)),
            dma((1,)),
            dma((n_row, CHUNKS)),
            dma((1,)),
            dma((2,)),
            pltpu.VMEM((n_layer, 3, blk), jnp.float32),
            pltpu.VMEM((3, blk), jnp.float32),
            pltpu.SemaphoreType.REGULAR((3,)),
        ],
        compiler_params=pltpu.CompilerParams(
            collective_id=0, has_side_effects=True,
            vmem_limit_bytes=panel_bytes + 8 * rows * width + (4 << 20)),
    )(*[
        pltpu.with_memory_space_constraint(x, pltpu.HBM)
        for x in (density, block_mask.T, keep_mask.T, branch_flag)
    ])
    updated, trace = pl.pallas_call(
        deliver,
        out_shape=(
            jax.ShapeDtypeStruct((rows, width), jnp.float32),
            jax.ShapeDtypeStruct((1, 1), jnp.float32),
        ),
        in_specs=[vmem, vmem],
        out_specs=(vmem, smem),
        compiler_params=pltpu.CompilerParams(
            vmem_limit_bytes=8 * rows * width + (4 << 20)),
    )(updated, lines)
    return updated, trace[0, 0]


def solution(mesh):
    sizes = tuple(mesh.shape[name] for name in ("row", "col", "layer"))
    in_specs = (
        P("row", ("col", "layer")),
        P("row", ("col", "layer")),
        P("row", ("col", "layer")),
        P("row"),
    )
    out_specs = (P("row", ("col", "layer")), P())
    return jax.shard_map(
        functools.partial(on_device, sizes), mesh=mesh, in_specs=in_specs,
        out_specs=out_specs, check_vma=False,
    )
```

```python
import functools

import jax
import jax.numpy as jnp
from jax import lax
from jax.experimental import pallas as pl
from jax.experimental.pallas import tpu as pltpu
from jax.sharding import PartitionSpec as P

MESH = pl.DeviceIdType.MESH
CHUNKS = 4
AHEAD = 2


def partner_of(index, step, size):
    if size & (size - 1):
        return (index + step) % size
    for bit in range(size.bit_length()):
        if step >> bit & 1:
            index = index + (1 - 2 * ((index // (1 << bit)) % 2)) * (1 << bit)
    return index


def passing_plans(n_row):
    last = n_row - 1
    blocks = [[(b, q) for q in range(CHUNKS)] for b in range(n_row)]
    rightward = [sum(blocks[row::-1], []) for row in range(last)] + [[]]
    leftward = [[]] + [sum(blocks[row:], []) for row in range(1, n_row)]
    leftward[1].append(leftward[1].pop(CHUNKS - 1))
    return rightward, leftward


def kernel(
    sizes, density_hbm, block_hbm, keep_hbm, flag_hbm, updated, lines,
    density, block_mask, keep_mask, branch_flag,
    row_panel, col_panel, trace_own, trace_in, local_sem,
    plane_send, plane_recv, side_send, right_send, left_send, z_recv,
    trace_send, trace_recv, trace_swap, trace_sum, aside, aside_send, aside_sems, ready,
):
    n_row, n_col, n_layer = sizes
    rows, width = density.shape
    blk = rows // block_mask.shape[1]
    per = rows // width
    piece = rows // CHUNKS
    slots = n_col * n_layer
    last = n_row - 1
    r, c, l = lax.axis_index("row"), lax.axis_index("col"), lax.axis_index("layer")
    me = c * n_layer + l
    has_left, has_right = r > 0, r < last
    left, right = jnp.maximum(r - 1, 0), jnp.minimum(r + 1, last)
    col_peers = [partner_of(c, d, n_col) for d in range(1, n_col)]
    layer_peers = [partner_of(l, d, n_layer) for d in range(1, n_layer)]

    bits = [d for d in range(1, n_col) if d & (d - 1) == 0]
    relayed = [lo | hi for hi in bits for lo in bits if lo < hi]
    if n_col & (n_col - 1):
        bits, relayed = list(range(1, n_col)), []
    direct = [d for d in range(1, n_col) if d not in relayed]
    halves = {d: (1, 0) if relayed and d > 1 else (0, 1) for d in range(1, n_col)}

    plane_peers = [(c, q, True, 1) for q in layer_peers]
    for d in range(1, n_col):
        p = col_peers[d - 1]
        met = (p * c == 0) if d in relayed and len(bits) == 2 else True
        plane_peers += [(p, q, met, 3 if d in relayed else 1) for q in range(n_layer)]

    def counted(which, above):
        return sum(jnp.where(((p * n_layer + q > me) == above) & met, 1, 0)
                   for p, q, met, to in plane_peers if to in which)

    def span(q):
        return pl.ds(q * piece, piece)

    loads = [
        pltpu.make_async_copy(source, target, local_sem.at[i])
        for i, (source, target) in enumerate(
            [(block_hbm, block_mask)]
            + [(density_hbm.at[span(q)], density.at[span(q)]) for q in range(CHUNKS)]
            + [(keep_hbm, keep_mask), (flag_hbm, branch_flag)])
    ]
    for load in loads:
        load.start()

    barrier = pltpu.get_barrier_semaphore()

    def greet(target):
        pl.semaphore_signal(barrier, inc=1, device_id=target, device_id_type=MESH)

    def answer(which, target):
        pl.semaphore_signal(
            ready.at[which], inc=1, device_id=target, device_id_type=MESH)

    pl.when(has_right)(lambda: greet((right, c, l)))
    for p, q, met, _ in plane_peers:
        pl.when((p * n_layer + q > me) & met)(functools.partial(greet, (r, p, q)))
    below = jnp.where(has_left, 1, 0) + counted((1, 3), False)
    pl.when(below > 0)(lambda: pl.semaphore_wait(barrier, below))
    pl.when(has_left)(lambda: answer(0, (left, c, l)))
    for p, q, met, to in plane_peers:
        pl.when((p * n_layer + q < me) & met)(functools.partial(answer, to, (r, p, q)))
    def mask(q):
        loads[1 + q].wait()
        for i in range(q * piece // blk, (q + 1) * piece // blk):
            for k in range(width // blk):
                at = (pl.ds(i * blk, blk), pl.ds(k * blk, blk))
                kept = jnp.full((blk, blk), block_mask[k, i].astype(jnp.float32))
                row_panel[(me,) + at] = density[at] * kept.astype(jnp.bfloat16)

    loads[0].wait()

    def z_copy(block, q, source, target, sem):
        return pltpu.make_async_remote_copy(
            src_ref=source, dst_ref=col_panel.at[block, span(q)],
            send_sem=sem.at[0], recv_sem=z_recv.at[block, q],
            device_id=(target, c, l), device_id_type=MESH,
        )

    def to_right(block, q, source):
        return z_copy(block, q, source, right, right_send)

    def to_left(block, q, source):
        return z_copy(block, q, source, left, left_send)

    def half_copy(slot, h, sem, target):
        half = pl.ds(h * (rows // 2), rows // 2)
        return pltpu.make_async_remote_copy(
            src_ref=row_panel.at[slot, half], dst_ref=row_panel.at[slot, half],
            send_sem=sem.at[0], recv_sem=plane_recv.at[slot, h],
            device_id=target, device_id_type=MESH,
        )

    def plane_copy(slot, h, peer):
        return half_copy(slot, h, plane_send, (r, peer, l))

    def side_copies(slot, h):
        for other in layer_peers:
            half_copy(slot, h, side_send, (r, c, other)).start()

    def side_wait(slot):
        for h in range(2):
            half_copy(slot, h, side_send, (r, c, l)).wait_recv()

    def plane_start(chosen):
        for turn in range(2):
            for d in direct:
                peer = col_peers[d - 1]
                pl.when(chosen(peer))(
                    lambda: plane_copy(me, halves[d][turn], peer).start())

    def plane_arrive(d, turn):
        peer, h = col_peers[d - 1], halves[d][turn]
        slot = peer * n_layer + l
        plane_copy(slot, h, peer).wait_recv()
        for other in bits if relayed and d in bits else []:
            if (other > d) == (h == 0) and other != d:
                plane_copy(slot, h, col_peers[other - 1]).start()
        side_copies(slot, h)

    rightward, leftward = passing_plans(n_row)
    from_left = [[]] + rightward[:-1]
    from_right = leftward[1:] + [[]]

    on_diagonal = me // per == r

    detour = bool(relayed) and n_layer <= len(bits)
    by_way = functools.reduce(jnp.logical_or, [
        (l == layer) & (c == bits[layer]) for layer in range(n_layer if detour else 0)],
        c < 0)

    def detour_copy(source, target, column, row, sem, recv):
        return pltpu.make_async_remote_copy(
            src_ref=source, dst_ref=target, send_sem=sem.at[0], recv_sem=recv,
            device_id=(row, column, l), device_id_type=MESH,
        )

    def detour_start():
        for layer in range(n_layer):
            pl.when((r == 1) & (c == 0) & (l == layer))(detour_copy(
                row_panel.at[me, span(CHUNKS - 1)], aside, bits[layer], 1,
                left_send, aside_sems.at[0]).start)

    def detour_pass(row):
        target, recv = ((aside, aside_sems.at[0]) if row else
                        (col_panel.at[1, span(CHUNKS - 1)], z_recv.at[1, CHUNKS - 1]))

        @pl.when(by_way & (r == row))
        def _():
            detour_copy(aside, aside, c, 0, aside_send, aside_sems.at[0]).wait_recv()
            detour_copy(aside, target, c if row else 0, 0, aside_send, recv).start()

    def pass_on(copy, row, plan, first, arrived, stop=None, hold=None):
        while first < len(plan) and (stop is None or first < stop):
            block, q = plan[first]
            if block == row:
                source = row_panel.at[me, span(q)]
            elif (block, q) in arrived:
                source = col_panel.at[block, span(q)]
            else:
                break
            if detour and copy is to_left and (row, block, q) == (1, 1, CHUNKS - 1):
                pl.when(jnp.logical_not(on_diagonal) & (c > 0))(
                    functools.partial(lambda f: f.start(), copy(block, q, source)))
            elif hold is None or first < hold:
                copy(block, q, source).start()
            else:
                pl.when(jnp.logical_not(on_diagonal))(
                    functools.partial(lambda f: f.start(), copy(block, q, source)))
            first += 1
        return first

    sent_left, sent_right = [0] * n_row, [0] * n_row
    hold_left, hold_right = {1: last * CHUNKS - 2}, {last - 1: 2 * CHUNKS - 1}
    for q in range(CHUNKS):
        mask(q)
        for row in range(1, n_row) if q < AHEAD else []:
            @pl.when(r == row)
            def _():
                sent_left[row] = pass_on(
                    to_left, row, leftward[row], sent_left[row], (), q + 1)
    for load in loads[1 + CHUNKS:]:
        load.wait()
    plane_start(lambda peer: peer < c)
    pl.when(has_right)(lambda: pl.semaphore_wait(ready.at[0], 1))
    for row in range(last):
        @pl.when(r == row)
        def _():
            sent_right[row] = pass_on(to_right, row, rightward[row], 0, (), AHEAD)
    near_above, far_above = counted((1,), True), counted((3,), True)
    pl.when(near_above > 0)(lambda: pl.semaphore_wait(ready.at[1], near_above))
    for row in range(n_row):
        @pl.when(r == row)
        def _():
            sent_left[row] = pass_on(
                to_left, row, leftward[row], sent_left[row], (),
                CHUNKS - 1 if row == last else None, hold_left.get(row))
            sent_right[row] = pass_on(
                to_right, row, rightward[row], sent_right[row], (), None, hold_right.get(row))
    plane_start(lambda peer: peer > c)
    if detour:
        detour_start()
    for h in range(2):
        side_copies(me, h)

    def z_arrive(k, then=None):
        for row in range(n_row):
            if k < max(len(from_right[row]), len(from_left[row])):
                @pl.when(r == row)
                def _():
                    if k < len(from_right[row]):
                        block, q = from_right[row][k]
                        to_left(block, q, col_panel.at[block, span(q)]).wait_recv()
                        sent_left[row] = pass_on(
                            to_left, row, leftward[row], sent_left[row],
                            from_right[row][:k + 1], None, hold_left.get(row))
                        if then:
                            then(row, from_right[row], k)
                    if k < len(from_left[row]):
                        block, q = from_left[row][k]
                        to_right(block, q, col_panel.at[block, span(q)]).wait_recv()
                        sent_right[row] = pass_on(
                            to_right, row, rightward[row], sent_right[row],
                            from_left[row][:k + 1], None, hold_right.get(row))
                        if then:
                            then(row, from_left[row], k)

    def terms(block, start, size):
        out = []
        while size:
            step = min(size, width - start % width)
            out.append(jnp.dot(
                row_panel[block * per + start // width, :, pl.ds(start % width, step)],
                col_panel[block, pl.ds(start, step), :],
                preferred_element_type=jnp.float32))
            start, size = start + step, size - step
        return out

    def add(products):
        total = products[0]
        for product in products[1:]:
            total = total + product
        updated[...] += total

    corner = pl.multiple_of((me % per) * width, width)
    tiles = width // blk
    lanes = lax.broadcasted_iota(jnp.int32, (1, blk), 1)
    eye = (lax.broadcasted_iota(jnp.int32, (blk, blk), 0)
           == lax.broadcasted_iota(jnp.int32, (blk, blk), 1))

    def weight(t, if_square, otherwise):
        kept = keep_mask[t, (me % per) * tiles + t]
        chosen = jnp.where(branch_flag[(me % per) * tiles + t] == 1, if_square, otherwise)
        return (kept * chosen).astype(jnp.float32)

    def pair_sums(block, k):
        slot = block * per + k * blk // width
        out = []
        for t in range(tiles):
            ours = row_panel[slot, pl.ds(corner + t * blk, blk), pl.ds(k * blk % width, blk)]
            if block is r:
                theirs = row_panel[me, pl.ds(k * blk, blk), pl.ds(t * blk, blk)]
            else:
                theirs = col_panel[block, pl.ds(k * blk, blk), pl.ds(t * blk, blk)]
            product = jnp.dot(ours, theirs, preferred_element_type=jnp.float32)
            out.append(jnp.sum(jnp.where(eye, product, 0.0), axis=0, keepdims=True))
        return out

    def trace_copy(z, col, layer):
        return pltpu.make_async_remote_copy(
            src_ref=trace_own, dst_ref=trace_in.at[me],
            send_sem=trace_send.at[0], recv_sem=trace_recv.at[0],
            device_id=(z, col, layer), device_id_type=MESH,
        )

    assert per % n_layer == 0
    firsts = per // n_layer

    def swap_copy(other):
        return pltpu.make_async_remote_copy(
            src_ref=trace_own, dst_ref=trace_swap.at[l],
            send_sem=trace_send.at[0], recv_sem=trace_recv.at[1],
            device_id=(r, c, other), device_id_type=MESH,
        )

    def sum_copy(z, col):
        return pltpu.make_async_remote_copy(
            src_ref=trace_sum, dst_ref=trace_in.at[me],
            send_sem=trace_send.at[0], recv_sem=trace_recv.at[0],
            device_id=(z, col, l), device_id_type=MESH,
        )

    def send_first():
        trace_swap[l] = trace_own[...]
        for other in layer_peers:
            swap_copy(other).start()
        if n_layer > 1:
            pltpu.make_async_remote_copy(
                src_ref=trace_in.at[pl.ds(0, n_layer - 1)],
                dst_ref=trace_in.at[pl.ds(0, n_layer - 1)],
                send_sem=trace_send.at[0], recv_sem=trace_recv.at[1],
                device_id=(r, c, l), device_id_type=MESH,
            ).wait_recv()
        total = trace_swap[0]
        for layer in range(1, n_layer):
            total = total + trace_swap[layer]
        trace_sum[...] = total
        trace_in[me] = total
        for z in range(n_row - 1, -1, -1):
            for col in range(n_col):
                pl.when((z != r) | (col != c))(lambda: sum_copy(z, col).start())

    everyone = [(z, col, layer) for z in range(n_row) for col in range(n_col)
                for layer in range(n_layer)]

    def add_trace(chunks, start):
        weights = [weight(t, 1, -1) for t in range(tiles)]
        part = spread = others = jnp.zeros((1, blk), jnp.float32)
        if not start:
            part, spread, others = (trace_own[n:n + 1, :] for n in range(3))
        for t in range(tiles if start else 0):
            own = row_panel[me, pl.ds(corner + t * blk, blk), pl.ds(t * blk, blk)]
            line = jnp.sum(
                jnp.where(eye, own.astype(jnp.float32), 0.0), axis=0, keepdims=True)
            part += weight(t, 0, 2) * line
            spread += jnp.where(lanes == me * tiles + t, weights[t], 0.0)
        every = range(rows // blk)
        for block, k in ([(r, k) for k in every] if start else []) + chunks:
            sums = pair_sums(block, k)
            for t in range(tiles):
                part += weights[t] * sums[t]
            if block is not r:
                here = block * (rows // blk) + k
                total = sum(jnp.sum(line, keepdims=True) for line in sums)
                others += jnp.where(lanes == here, total, 0.0)
        trace_own[0:1, :] = part
        trace_own[1:2, :] = spread
        trace_own[2:3, :] = others

    def send_trace(row):
        trace_in[me] = trace_own[...]
        for z, col, layer in everyone:
            pl.when((z != row) | (col != c) | (layer != l))(
                lambda: trace_copy(z, col, layer).start())

    middle = (last - 1) * CHUNKS
    pairs = {row: list(range(max(row + 1, 2 - row), n_row)) for row in range(n_row)}
    pairs[1] += [0]
    asked = list(range(1, n_row))

    def ready_rows(count, distances):
        def at_hand(b, row):
            arrived = (from_left if b < row else from_right)[row][:count]
            apart = (b * per // n_layer) ^ (row * per // n_layer)
            return ([x for x, _ in arrived].count(b) == CHUNKS
                    and (apart in distances or not relayed))

        return [row for row in asked if all(at_hand(b, row) for b in pairs[row])]

    def diagonals(chosen):
        for row in chosen:
            asked.remove(row)

            @pl.when(on_diagonal & (r == row))
            def _():
                add_trace([(b, k) for b in pairs[row] for k in range(rows // blk)], True)
                send_trace(row)
                for copy, plan, sent, hold in (
                        (to_left, leftward, sent_left, hold_left),
                        (to_right, rightward, sent_right, hold_right)):
                    if row in hold:
                        for block, q in plan[row][hold[row]:sent[row]]:
                            copy(block, q, row_panel.at[me, span(q)] if block == row
                                 else col_panel.at[block, span(q)]).start()
            hold_left.pop(row, None)
            hold_right.pop(row, None)

    pl.when(far_above > 0)(lambda: pl.semaphore_wait(ready.at[3], far_above))
    @pl.when(r == last)
    def _():
        sent_left[last] = pass_on(to_left, last, leftward[last], sent_left[last], ())
    pl.when(has_left)(lambda: pl.semaphore_wait(ready.at[2], 1))
    pl.when(has_right)(lambda: answer(2, (right, c, l)))
    for other in layer_peers:
        side_wait(c * n_layer + other)
    pl.when(on_diagonal & (r == 0))(lambda: add_trace([], True))
    diagonals(ready_rows(0, ()))
    for k in range(CHUNKS // 2):
        z_arrive(k)
    for d in direct:
        plane_arrive(d, 0)
    for k in range(CHUNKS // 2, CHUNKS):
        z_arrive(k)
    for d in direct:
        plane_arrive(d, 1)
    for k in range(CHUNKS, CHUNKS + 1):
        z_arrive(k)
    def sides(chosen):
        for other in layer_peers:
            for d in chosen:
                side_wait(col_peers[d - 1] * n_layer + other)

    soon = ready_rows(CHUNKS + 1, direct)
    in_soon = functools.reduce(jnp.logical_or, [r == row for row in soon], r < 0)
    pl.when(in_soon)(lambda: sides(direct))
    diagonals(soon)
    if detour:
        detour_pass(1)
    for k in range(CHUNKS + 1, CHUNKS + 2):
        z_arrive(k)
    for turn in range(2):
        for d in relayed:
            plane_arrive(d, turn)
    for k in range(CHUNKS + 2, middle):
        z_arrive(k)
    pl.when(jnp.logical_not(in_soon))(lambda: sides(direct))
    sides(relayed)
    diagonals(list(asked))

    total = None
    for t in range(per):
        term = jnp.dot(
            row_panel[r * per + t], row_panel[me, pl.ds(t * width, width), :],
            preferred_element_type=jnp.float32)
        total = term if total is None else total + term
    updated[...] = total
    inner = has_left & has_right
    for s in range(1, last):
        pl.when((r - s >= 0) & inner)(lambda: add(terms(r - s, 0, rows)))
        pl.when((r + s <= last) & inner)(lambda: add(terms(r + s, 0, rows)))
    for row, arrived in ((0, from_right[0]), (last, from_left[last])):
        @pl.when(r == row)
        def _():
            products = []
            for block in range(n_row):
                chunks = sorted(q for b, q in arrived[:middle] if b == block)
                if chunks:
                    assert chunks == list(range(len(chunks)))
                    products += terms(block, 0, len(chunks) * piece)
            add(products)

    def finish(row, arrived, k):
        block, q = arrived[k]
        if row == 0 and block in pairs[0]:
            @pl.when(on_diagonal)
            def _():
                add_trace(parts_of([(block, q)]), False)
                if k == last * CHUNKS - 2:
                    send_first()
        if k < last * CHUNKS - 1:
            add(terms(block, q * piece, piece))
        else:
            update(terms(block, q * piece, piece))

    def update(products):
        for i in range(rows // blk):
            flag = jnp.full((blk, blk), branch_flag[i]) == 1
            for k in range(width // blk):
                at = (pl.ds(i * blk, blk), pl.ds(k * blk, blk))
                square = updated[at]
                for product in products:
                    square += product[i * blk:(i + 1) * blk, k * blk:(k + 1) * blk]
                doubled = 2.0 * row_panel[(me,) + at].astype(jnp.float32) - square
                kept = jnp.full((blk, blk), keep_mask[k, i].astype(jnp.float32))
                updated[at] = jnp.where(flag, square, doubled) * kept

    def parts_of(chunks):
        share = piece // blk
        return [(b, q * share + k) for b, q in chunks if b in pairs[0] for k in range(share)]

    if detour:
        detour_pass(0)
    pl.when(on_diagonal & (r == 0))(
        lambda: add_trace(parts_of(from_right[0][:middle]), False))
    for k in range(middle, last * CHUNKS):
        z_arrive(k, finish)

    pl.when(inner)(lambda: update([]))

    if detour:
        pl.when(by_way & (r < 2))(
            detour_copy(aside, aside, c, 0, aside_send, aside_sems.at[0]).wait_send)
    for row in range(n_row):
        @pl.when(r == row)
        def _():
            for copy, plan, sem in (
                    (to_left, leftward[row], left_send),
                    (to_right, rightward[row], right_send)):
                if plan:
                    blocks = pl.ds(0, len(plan) // CHUNKS)
                    pltpu.make_async_remote_copy(
                        src_ref=col_panel.at[blocks], dst_ref=col_panel.at[blocks],
                        send_sem=sem.at[0], recv_sem=z_recv.at[0, 0],
                        device_id=(left, c, l), device_id_type=MESH,
                    ).wait_send()

    def sent_slots(count, ref, sem):
        pltpu.make_async_remote_copy(
            src_ref=ref.at[pl.ds(0, count)], dst_ref=ref.at[pl.ds(0, count)],
            send_sem=sem.at[0], recv_sem=plane_recv.at[0, 0],
            device_id=(r, c, l), device_id_type=MESH,
        ).wait_send()

    sent_slots(n_col - 1, row_panel, plane_send)
    sent_slots((n_layer - 1) * n_col, row_panel, side_send)

    def heard(count):
        pltpu.make_async_remote_copy(
            src_ref=trace_in.at[pl.ds(0, count)], dst_ref=trace_in.at[pl.ds(0, count)],
            send_sem=trace_send.at[0], recv_sem=trace_recv.at[0],
            device_id=(r, c, l), device_id_type=MESH,
        ).wait_recv()

    pl.when(on_diagonal)(lambda: heard(slots - per + firsts - 1))
    pl.when(jnp.logical_not(on_diagonal))(lambda: heard(slots - per + firsts))
    parts = trace_in[l]
    for slot in range(1, firsts):
        parts = parts + trace_in[slot * n_layer + l]
    for slot in range(per, slots):
        parts = parts + trace_in[slot]
    lines[...] = parts
    pl.when(on_diagonal & has_left)(
        lambda: sent_slots(n_row * slots - 1, trace_in, trace_send))
    pl.when(on_diagonal & jnp.logical_not(has_left))(
        lambda: sent_slots(n_row * n_col + n_layer - 2, trace_in, trace_send))


def deliver(updated, lines, out, trace):
    out[...] = updated[...]
    trace[0, 0] = jnp.sum(lines[0:1, :] + lines[1:2, :] * lines[2:3, :])


def on_device(sizes, density, block_mask, keep_mask, branch_flag):
    n_row, n_col, n_layer = sizes
    rows, width = density.shape
    blk = rows // block_mask.shape[0]
    dma = pltpu.SemaphoreType.DMA
    slots = n_col * n_layer
    vmem, smem = pl.BlockSpec(memory_space=pltpu.VMEM), pl.BlockSpec(memory_space=pltpu.SMEM)
    hbm = pl.BlockSpec(memory_space=pltpu.HBM)
    panel_bytes = 2 * rows * width * (slots + n_row + 1)
    updated, lines = pl.pallas_call(
        functools.partial(kernel, sizes),
        out_shape=(
            jax.ShapeDtypeStruct((rows, width), jnp.float32),
            jax.ShapeDtypeStruct((3, blk), jnp.float32),
        ),
        in_specs=[hbm, hbm, hbm, hbm],
        out_specs=(vmem, vmem),
        scratch_shapes=[
            pltpu.VMEM((rows, width), jnp.bfloat16),
            pltpu.SMEM(block_mask.T.shape, jnp.int32),
            pltpu.SMEM(keep_mask.T.shape, jnp.int32),
            pltpu.SMEM(branch_flag.shape, jnp.int32),
            pltpu.VMEM((slots, rows, width), jnp.bfloat16),
            pltpu.VMEM((n_row, rows, width), jnp.bfloat16),
            pltpu.VMEM((3, blk), jnp.float32),
            pltpu.VMEM((n_row * slots, 3, blk), jnp.float32),
            dma((CHUNKS + 3,)),
            dma((1,)),
            dma((slots, 2)),
            dma((1,)),
            dma((1,)),
            dma((1,)),
            dma((n_row, CHUNKS)),
            dma((1,)),
            dma((2,)),
            pltpu.VMEM((n_layer, 3, blk), jnp.float32),
            pltpu.VMEM((3, blk), jnp.float32),
            pltpu.VMEM((rows // CHUNKS, width), jnp.bfloat16),
            dma((1,)),
            dma((1,)),
            pltpu.SemaphoreType.REGULAR((4,)),
        ],
        compiler_params=pltpu.CompilerParams(
            collective_id=0, has_side_effects=True,
            vmem_limit_bytes=panel_bytes + 8 * rows * width + (4 << 20)),
    )(*[
        pltpu.with_memory_space_constraint(x, pltpu.HBM)
        for x in (density, block_mask.T, keep_mask.T, branch_flag)
    ])
    updated, trace = pl.pallas_call(
        deliver,
        out_shape=(
            jax.ShapeDtypeStruct((rows, width), jnp.float32),
            jax.ShapeDtypeStruct((1, 1), jnp.float32),
        ),
        in_specs=[vmem, vmem],
        out_specs=(vmem, smem),
        compiler_params=pltpu.CompilerParams(
            vmem_limit_bytes=8 * rows * width + (4 << 20)),
    )(updated, lines)
    return updated, trace[0, 0]


def solution(mesh):
    sizes = tuple(mesh.shape[name] for name in ("row", "col", "layer"))
    in_specs = (
        P("row", ("col", "layer")),
        P("row", ("col", "layer")),
        P("row", ("col", "layer")),
        P("row"),
    )
    out_specs = (P("row", ("col", "layer")), P())
    return jax.shard_map(
        functools.partial(on_device, sizes), mesh=mesh, in_specs=in_specs,
        out_specs=out_specs, check_vma=False,
    )
```

```python
import functools

import jax
import jax.numpy as jnp
from jax import lax
from jax.experimental import pallas as pl
from jax.experimental.pallas import tpu as pltpu
from jax.sharding import PartitionSpec as P

MESH = pl.DeviceIdType.MESH
CHUNKS = 4
AHEAD = 2


def partner_of(index, step, size):
    if size & (size - 1):
        return (index + step) % size
    for bit in range(size.bit_length()):
        if step >> bit & 1:
            index = index + (1 - 2 * ((index // (1 << bit)) % 2)) * (1 << bit)
    return index


def passing_plans(n_row):
    last = n_row - 1
    blocks = [[(b, q) for q in range(CHUNKS)] for b in range(n_row)]
    rightward = [sum(blocks[row::-1], []) for row in range(last)] + [[]]
    leftward = [[]] + [sum(blocks[row:], []) for row in range(1, n_row)]
    leftward[1].append(leftward[1].pop(CHUNKS - 1))
    return rightward, leftward


def kernel(
    sizes, density_hbm, block_hbm, keep_hbm, flag_hbm, updated, lines,
    density, block_mask, keep_mask, branch_flag,
    row_panel, col_panel, trace_own, trace_in, local_sem,
    plane_send, plane_recv, side_send, side_recv, right_send, left_send, z_recv,
    trace_send, trace_recv, trace_swap, trace_sum, aside, aside_send, aside_sems, ready,
):
    n_row, n_col, n_layer = sizes
    rows, width = density.shape
    blk = rows // block_mask.shape[1]
    per = rows // width
    piece = rows // CHUNKS
    slots = n_col * n_layer
    last = n_row - 1
    r, c, l = lax.axis_index("row"), lax.axis_index("col"), lax.axis_index("layer")
    me = c * n_layer + l
    has_left, has_right = r > 0, r < last
    left, right = jnp.maximum(r - 1, 0), jnp.minimum(r + 1, last)
    col_peers = [partner_of(c, d, n_col) for d in range(1, n_col)]
    layer_peers = [partner_of(l, d, n_layer) for d in range(1, n_layer)]

    bits = [d for d in range(1, n_col) if d & (d - 1) == 0]
    relayed = [lo | hi for hi in bits for lo in bits if lo < hi]
    if n_col & (n_col - 1):
        bits, relayed = list(range(1, n_col)), []
    direct = [d for d in range(1, n_col) if d not in relayed]
    halves = {d: (1, 0) if relayed and d > 1 else (0, 1) for d in range(1, n_col)}

    plane_peers = [(c, q, True, 1) for q in layer_peers]
    for d in range(1, n_col):
        p = col_peers[d - 1]
        met = (p * c == 0) if d in relayed and len(bits) == 2 else True
        plane_peers += [(p, q, met, 3 if d in relayed else 1) for q in range(n_layer)]

    def counted(which, above):
        return sum(jnp.where(((p * n_layer + q > me) == above) & met, 1, 0)
                   for p, q, met, to in plane_peers if to in which)

    def span(q):
        return pl.ds(q * piece, piece)

    loads = [
        pltpu.make_async_copy(source, target, local_sem.at[i])
        for i, (source, target) in enumerate(
            [(block_hbm, block_mask)]
            + [(density_hbm.at[span(q)], density.at[span(q)]) for q in range(CHUNKS)]
            + [(keep_hbm, keep_mask), (flag_hbm, branch_flag)])
    ]
    for load in loads:
        load.start()

    barrier = pltpu.get_barrier_semaphore()

    def greet(target):
        pl.semaphore_signal(barrier, inc=1, device_id=target, device_id_type=MESH)

    def answer(which, target):
        pl.semaphore_signal(
            ready.at[which], inc=1, device_id=target, device_id_type=MESH)

    pl.when(has_right)(lambda: greet((right, c, l)))
    for p, q, met, _ in plane_peers:
        pl.when((p * n_layer + q > me) & met)(functools.partial(greet, (r, p, q)))
    below = jnp.where(has_left, 1, 0) + counted((1, 3), False)
    pl.when(below > 0)(lambda: pl.semaphore_wait(barrier, below))
    pl.when(has_left)(lambda: answer(0, (left, c, l)))
    for p, q, met, to in plane_peers:
        pl.when((p * n_layer + q < me) & met)(functools.partial(answer, to, (r, p, q)))
    def mask(q):
        loads[1 + q].wait()
        for i in range(q * piece // blk, (q + 1) * piece // blk):
            for k in range(width // blk):
                at = (pl.ds(i * blk, blk), pl.ds(k * blk, blk))
                kept = jnp.full((blk, blk), block_mask[k, i].astype(jnp.float32))
                row_panel[(me,) + at] = density[at] * kept.astype(jnp.bfloat16)

    loads[0].wait()

    def z_copy(block, q, source, target, sem):
        return pltpu.make_async_remote_copy(
            src_ref=source, dst_ref=col_panel.at[block, span(q)],
            send_sem=sem.at[0], recv_sem=z_recv.at[block, q],
            device_id=(target, c, l), device_id_type=MESH,
        )

    def to_right(block, q, source):
        return z_copy(block, q, source, right, right_send)

    def to_left(block, q, source):
        return z_copy(block, q, source, left, left_send)

    def half_copy(slot, h, sem, recv, target):
        half = pl.ds(h * (rows // 2), rows // 2)
        return pltpu.make_async_remote_copy(
            src_ref=row_panel.at[slot, half], dst_ref=row_panel.at[slot, half],
            send_sem=sem.at[0], recv_sem=recv, device_id=target, device_id_type=MESH,
        )

    def plane_copy(slot, h, d, peer):
        return half_copy(slot, h, plane_send, plane_recv.at[d - 1, h], (r, peer, l))

    def side_copies(slot, h, group):
        for other in layer_peers:
            half_copy(slot, h, side_send, side_recv.at[group], (r, c, other)).start()

    def side_wait(count, group):
        blocks = row_panel.at[pl.ds(0, count)]
        if count:
            pltpu.make_async_remote_copy(
                src_ref=blocks, dst_ref=blocks, send_sem=side_send.at[0],
                recv_sem=side_recv.at[group], device_id=(r, c, l), device_id_type=MESH,
            ).wait_recv()

    def seen(d):
        return n_col - d if n_col & (n_col - 1) else d

    def plane_start(chosen):
        for turn in range(2):
            for d in direct:
                peer = col_peers[d - 1]
                pl.when(chosen(peer))(
                    lambda: plane_copy(me, halves[d][turn], seen(d), peer).start())

    def plane_arrive(d, turn):
        peer, h = col_peers[d - 1], halves[d][turn]
        slot = peer * n_layer + l
        plane_copy(slot, h, d, peer).wait_recv()
        for other in bits if relayed and d in bits else []:
            if (other > d) == (h == 0) and other != d:
                plane_copy(slot, h, d | other, col_peers[other - 1]).start()
        side_copies(slot, h, 2 if d in relayed else 1)

    rightward, leftward = passing_plans(n_row)
    from_left = [[]] + rightward[:-1]
    from_right = leftward[1:] + [[]]

    on_diagonal = me // per == r

    detour = bool(relayed) and n_layer <= len(bits)
    by_way = functools.reduce(jnp.logical_or, [
        (l == layer) & (c == bits[layer]) for layer in range(n_layer if detour else 0)],
        c < 0)

    def detour_copy(source, target, column, row, sem, recv):
        return pltpu.make_async_remote_copy(
            src_ref=source, dst_ref=target, send_sem=sem.at[0], recv_sem=recv,
            device_id=(row, column, l), device_id_type=MESH,
        )

    def detour_start():
        for layer in range(n_layer):
            pl.when((r == 1) & (c == 0) & (l == layer))(detour_copy(
                row_panel.at[me, span(CHUNKS - 1)], aside, bits[layer], 1,
                left_send, aside_sems.at[0]).start)

    def detour_pass(row):
        target, recv = ((aside, aside_sems.at[0]) if row else
                        (col_panel.at[1, span(CHUNKS - 1)], z_recv.at[1, CHUNKS - 1]))

        @pl.when(by_way & (r == row))
        def _():
            detour_copy(aside, aside, c, 0, aside_send, aside_sems.at[0]).wait_recv()
            detour_copy(aside, target, c if row else 0, 0, aside_send, recv).start()

    def pass_on(copy, row, plan, first, arrived, stop=None, hold=None):
        while first < len(plan) and (stop is None or first < stop):
            block, q = plan[first]
            if block == row:
                source = row_panel.at[me, span(q)]
            elif (block, q) in arrived:
                source = col_panel.at[block, span(q)]
            else:
                break
            if detour and copy is to_left and (row, block, q) == (1, 1, CHUNKS - 1):
                pl.when(jnp.logical_not(on_diagonal) & (c > 0))(
                    functools.partial(lambda f: f.start(), copy(block, q, source)))
            elif hold is None or first < hold:
                copy(block, q, source).start()
            else:
                pl.when(jnp.logical_not(on_diagonal))(
                    functools.partial(lambda f: f.start(), copy(block, q, source)))
            first += 1
        return first

    sent_left, sent_right = [0] * n_row, [0] * n_row
    hold_left, hold_right = {1: last * CHUNKS - 2}, {last - 1: 2 * CHUNKS - 1}
    for q in range(CHUNKS):
        mask(q)
        for row in range(1, n_row) if q < AHEAD else []:
            @pl.when(r == row)
            def _():
                sent_left[row] = pass_on(
                    to_left, row, leftward[row], sent_left[row], (), q + 1)
    for load in loads[1 + CHUNKS:]:
        load.wait()
    plane_start(lambda peer: peer < c)
    pl.when(has_right)(lambda: pl.semaphore_wait(ready.at[0], 1))
    for row in range(last):
        @pl.when(r == row)
        def _():
            sent_right[row] = pass_on(to_right, row, rightward[row], 0, (), AHEAD)
    near_above, far_above = counted((1,), True), counted((3,), True)
    pl.when(near_above > 0)(lambda: pl.semaphore_wait(ready.at[1], near_above))
    for row in range(n_row):
        @pl.when(r == row)
        def _():
            sent_left[row] = pass_on(
                to_left, row, leftward[row], sent_left[row], (),
                CHUNKS - 1 if row == last else None, hold_left.get(row))
            sent_right[row] = pass_on(
                to_right, row, rightward[row], sent_right[row], (), None, hold_right.get(row))
    if detour:
        detour_start()
    plane_start(lambda peer: peer > c)
    for h in range(2):
        side_copies(me, h, 0)

    def z_arrive(k, then=None):
        for row in range(n_row):
            if k < max(len(from_right[row]), len(from_left[row])):
                @pl.when(r == row)
                def _():
                    if k < len(from_right[row]):
                        block, q = from_right[row][k]
                        to_left(block, q, col_panel.at[block, span(q)]).wait_recv()
                        sent_left[row] = pass_on(
                            to_left, row, leftward[row], sent_left[row],
                            from_right[row][:k + 1], None, hold_left.get(row))
                        if then:
                            then(row, from_right[row], k)
                    if k < len(from_left[row]):
                        block, q = from_left[row][k]
                        to_right(block, q, col_panel.at[block, span(q)]).wait_recv()
                        sent_right[row] = pass_on(
                            to_right, row, rightward[row], sent_right[row],
                            from_left[row][:k + 1], None, hold_right.get(row))
                        if then:
                            then(row, from_left[row], k)

    def terms(block, start, size):
        out = []
        while size:
            step = min(size, width - start % width)
            out.append(jnp.dot(
                row_panel[block * per + start // width, :, pl.ds(start % width, step)],
                col_panel[block, pl.ds(start, step), :],
                preferred_element_type=jnp.float32))
            start, size = start + step, size - step
        return out

    def add(products):
        total = products[0]
        for product in products[1:]:
            total = total + product
        updated[...] += total

    corner = pl.multiple_of((me % per) * width, width)
    tiles = width // blk
    lanes = lax.broadcasted_iota(jnp.int32, (1, blk), 1)
    eye = (lax.broadcasted_iota(jnp.int32, (blk, blk), 0)
           == lax.broadcasted_iota(jnp.int32, (blk, blk), 1))

    def weight(t, if_square, otherwise):
        kept = keep_mask[t, (me % per) * tiles + t]
        chosen = jnp.where(branch_flag[(me % per) * tiles + t] == 1, if_square, otherwise)
        return (kept * chosen).astype(jnp.float32)

    def pair_sums(block, k):
        slot = block * per + k * blk // width
        out = []
        for t in range(tiles):
            ours = row_panel[slot, pl.ds(corner + t * blk, blk), pl.ds(k * blk % width, blk)]
            if block is r:
                theirs = row_panel[me, pl.ds(k * blk, blk), pl.ds(t * blk, blk)]
            else:
                theirs = col_panel[block, pl.ds(k * blk, blk), pl.ds(t * blk, blk)]
            product = jnp.dot(ours, theirs, preferred_element_type=jnp.float32)
            out.append(jnp.sum(jnp.where(eye, product, 0.0), axis=0, keepdims=True))
        return out

    def trace_copy(z, col, layer):
        return pltpu.make_async_remote_copy(
            src_ref=trace_own, dst_ref=trace_in.at[me],
            send_sem=trace_send.at[0], recv_sem=trace_recv.at[0],
            device_id=(z, col, layer), device_id_type=MESH,
        )

    assert per % n_layer == 0
    firsts = per // n_layer

    def swap_copy(other):
        return pltpu.make_async_remote_copy(
            src_ref=trace_own, dst_ref=trace_swap.at[l],
            send_sem=trace_send.at[0], recv_sem=trace_recv.at[1],
            device_id=(r, c, other), device_id_type=MESH,
        )

    def sum_copy(z, col, layer):
        return pltpu.make_async_remote_copy(
            src_ref=trace_sum, dst_ref=trace_in.at[me],
            send_sem=trace_send.at[0], recv_sem=trace_recv.at[0],
            device_id=(z, col, layer), device_id_type=MESH,
        )

    def send_first():
        trace_swap[l] = trace_own[...]
        for other in layer_peers:
            swap_copy(other).start()
        if n_layer > 1:
            pltpu.make_async_remote_copy(
                src_ref=trace_in.at[pl.ds(0, n_layer - 1)],
                dst_ref=trace_in.at[pl.ds(0, n_layer - 1)],
                send_sem=trace_send.at[0], recv_sem=trace_recv.at[1],
                device_id=(r, c, l), device_id_type=MESH,
            ).wait_recv()
        total = trace_swap[0]
        for layer in range(1, n_layer):
            total = total + trace_swap[layer]
        trace_sum[...] = total
        trace_in[me] = total
        @pl.when(l == 0)
        def _():
            for col in range(n_col):
                for layer in range(n_layer):
                    sum_copy(last, col, layer).start()

        for z in range(last - 1, -1, -1):
            for col in range(n_col):
                pl.when((z != r) | (col != c))(lambda: sum_copy(z, col, l).start())

    everyone = [(z, col, layer) for z in range(n_row) for col in range(n_col)
                for layer in range(n_layer)]

    def add_trace(chunks, start):
        weights = [weight(t, 1, -1) for t in range(tiles)]
        part = spread = others = jnp.zeros((1, blk), jnp.float32)
        if not start:
            part, spread, others = (trace_own[n:n + 1, :] for n in range(3))
        for t in range(tiles if start else 0):
            own = row_panel[me, pl.ds(corner + t * blk, blk), pl.ds(t * blk, blk)]
            line = jnp.sum(
                jnp.where(eye, own.astype(jnp.float32), 0.0), axis=0, keepdims=True)
            part += weight(t, 0, 2) * line
            spread += jnp.where(lanes == me * tiles + t, weights[t], 0.0)
        every = range(rows // blk)
        for block, k in ([(r, k) for k in every] if start else []) + chunks:
            sums = pair_sums(block, k)
            for t in range(tiles):
                part += weights[t] * sums[t]
            if block is not r:
                here = block * (rows // blk) + k
                total = sum(jnp.sum(line, keepdims=True) for line in sums)
                others += jnp.where(lanes == here, total, 0.0)
        trace_own[0:1, :] = part
        trace_own[1:2, :] = spread
        trace_own[2:3, :] = others

    def send_trace(row):
        trace_in[me] = trace_own[...]
        for z, col, layer in everyone:
            pl.when((z != row) | (col != c) | (layer != l))(
                lambda: trace_copy(z, col, layer).start())

    middle = (last - 1) * CHUNKS
    pairs = {row: list(range(max(row + 1, 2 - row), n_row)) for row in range(n_row)}
    pairs[1] += [0]
    asked = list(range(1, n_row))

    def ready_rows(count, distances):
        def at_hand(b, row):
            arrived = (from_left if b < row else from_right)[row][:count]
            apart = (b * per // n_layer) ^ (row * per // n_layer)
            return ([x for x, _ in arrived].count(b) == CHUNKS
                    and (apart in distances or not relayed))

        return [row for row in asked if all(at_hand(b, row) for b in pairs[row])]

    def diagonals(chosen):
        for row in chosen:
            asked.remove(row)

            @pl.when(on_diagonal & (r == row))
            def _():
                add_trace([(b, k) for b in pairs[row] for k in range(rows // blk)], True)
                send_trace(row)
                for copy, plan, sent, hold in (
                        (to_left, leftward, sent_left, hold_left),
                        (to_right, rightward, sent_right, hold_right)):
                    if row in hold:
                        for block, q in plan[row][hold[row]:sent[row]]:
                            copy(block, q, row_panel.at[me, span(q)] if block == row
                                 else col_panel.at[block, span(q)]).start()
            hold_left.pop(row, None)
            hold_right.pop(row, None)

    pl.when(far_above > 0)(lambda: pl.semaphore_wait(ready.at[3], far_above))
    @pl.when(r == last)
    def _():
        sent_left[last] = pass_on(to_left, last, leftward[last], sent_left[last], ())
    pl.when(has_left)(lambda: pl.semaphore_wait(ready.at[2], 1))
    pl.when(has_right)(lambda: answer(2, (right, c, l)))
    side_wait(n_layer - 1, 0)
    pl.when(on_diagonal & (r == 0))(lambda: add_trace([], True))
    diagonals(ready_rows(0, ()))
    for k in range(CHUNKS // 2):
        z_arrive(k)
    for d in direct:
        plane_arrive(d, 0)
    for k in range(CHUNKS // 2, CHUNKS):
        z_arrive(k)
    if detour:
        detour_pass(1)
    for d in direct:
        plane_arrive(d, 1)
    for k in range(CHUNKS, CHUNKS + 1):
        z_arrive(k)
    def sides(chosen):
        side_wait(len(chosen) * (n_layer - 1), 2 if chosen is relayed else 1)

    soon = ready_rows(CHUNKS + 1, direct)
    in_soon = functools.reduce(jnp.logical_or, [r == row for row in soon], r < 0)
    pl.when(in_soon)(lambda: sides(direct))
    diagonals(soon)
    for k in range(CHUNKS + 1, CHUNKS + 2):
        z_arrive(k)
    for turn in range(2):
        for d in relayed:
            plane_arrive(d, turn)
    if detour:
        detour_pass(0)
    for k in range(CHUNKS + 2, middle):
        z_arrive(k)
    pl.when(jnp.logical_not(in_soon))(lambda: sides(direct))
    sides(relayed)
    diagonals(list(asked))

    total = None
    for t in range(per):
        term = jnp.dot(
            row_panel[r * per + t], row_panel[me, pl.ds(t * width, width), :],
            preferred_element_type=jnp.float32)
        total = term if total is None else total + term
    updated[...] = total
    inner = has_left & has_right
    for s in range(1, last):
        pl.when((r - s >= 0) & inner)(lambda: add(terms(r - s, 0, rows)))
        pl.when((r + s <= last) & inner)(lambda: add(terms(r + s, 0, rows)))
    for row, arrived in ((0, from_right[0]), (last, from_left[last])):
        @pl.when(r == row)
        def _():
            products = []
            for block in range(n_row):
                chunks = sorted(q for b, q in arrived[:middle] if b == block)
                if chunks:
                    assert chunks == list(range(len(chunks)))
                    products += terms(block, 0, len(chunks) * piece)
            add(products)

    def finish(row, arrived, k):
        block, q = arrived[k]
        if row == 0 and block in pairs[0]:
            @pl.when(on_diagonal)
            def _():
                add_trace(parts_of([(block, q)]), False)
                if k == last * CHUNKS - 2:
                    send_first()
        if k < last * CHUNKS - 1:
            add(terms(block, q * piece, piece))
        else:
            update(terms(block, q * piece, piece))

    def update(products):
        for i in range(rows // blk):
            flag = jnp.full((blk, blk), branch_flag[i]) == 1
            for k in range(width // blk):
                at = (pl.ds(i * blk, blk), pl.ds(k * blk, blk))
                square = updated[at]
                for product in products:
                    square += product[i * blk:(i + 1) * blk, k * blk:(k + 1) * blk]
                doubled = 2.0 * row_panel[(me,) + at].astype(jnp.float32) - square
                kept = jnp.full((blk, blk), keep_mask[k, i].astype(jnp.float32))
                updated[at] = jnp.where(flag, square, doubled) * kept

    def parts_of(chunks):
        share = piece // blk
        return [(b, q * share + k) for b, q in chunks if b in pairs[0] for k in range(share)]

    pl.when(on_diagonal & (r == 0))(
        lambda: add_trace(parts_of(from_right[0][:middle]), False))
    for k in range(middle, last * CHUNKS):
        z_arrive(k, finish)

    pl.when(inner)(lambda: update([]))

    if detour:
        pl.when(by_way & (r < 2))(
            detour_copy(aside, aside, c, 0, aside_send, aside_sems.at[0]).wait_send)
    for row in range(n_row):
        @pl.when(r == row)
        def _():
            for copy, plan, sem in (
                    (to_left, leftward[row], left_send),
                    (to_right, rightward[row], right_send)):
                if plan:
                    blocks = pl.ds(0, len(plan) // CHUNKS)
                    pltpu.make_async_remote_copy(
                        src_ref=col_panel.at[blocks], dst_ref=col_panel.at[blocks],
                        send_sem=sem.at[0], recv_sem=z_recv.at[0, 0],
                        device_id=(left, c, l), device_id_type=MESH,
                    ).wait_send()

    def sent_slots(count, ref, sem):
        pltpu.make_async_remote_copy(
            src_ref=ref.at[pl.ds(0, count)], dst_ref=ref.at[pl.ds(0, count)],
            send_sem=sem.at[0], recv_sem=plane_recv.at[0, 0],
            device_id=(r, c, l), device_id_type=MESH,
        ).wait_send()

    sent_slots(n_col - 1, row_panel, plane_send)
    sent_slots((n_layer - 1) * n_col, row_panel, side_send)

    def heard(count):
        pltpu.make_async_remote_copy(
            src_ref=trace_in.at[pl.ds(0, count)], dst_ref=trace_in.at[pl.ds(0, count)],
            send_sem=trace_send.at[0], recv_sem=trace_recv.at[0],
            device_id=(r, c, l), device_id_type=MESH,
        ).wait_recv()

    pl.when(on_diagonal)(lambda: heard(slots - per + firsts - 1))
    pl.when(jnp.logical_not(on_diagonal))(lambda: heard(slots - per + firsts))
    giver = jnp.where(r == last, 0, l)
    parts = trace_in[giver]
    for slot in range(1, firsts):
        parts = parts + trace_in[slot * n_layer + giver]
    for slot in range(per, slots):
        parts = parts + trace_in[slot]
    lines[...] = parts
    pl.when(on_diagonal & has_left)(
        lambda: sent_slots(n_row * slots - 1, trace_in, trace_send))
    first_sent = last * n_col + n_layer - 2
    for core, count in ((l == 0, first_sent + n_col * n_layer), (l > 0, first_sent)):
        pl.when(on_diagonal & jnp.logical_not(has_left) & core)(
            functools.partial(sent_slots, count, trace_in, trace_send))


def deliver(updated, lines, out, trace):
    out[...] = updated[...]
    trace[0, 0] = jnp.sum(lines[0:1, :] + lines[1:2, :] * lines[2:3, :])


def on_device(sizes, density, block_mask, keep_mask, branch_flag):
    n_row, n_col, n_layer = sizes
    rows, width = density.shape
    blk = rows // block_mask.shape[0]
    dma = pltpu.SemaphoreType.DMA
    slots = n_col * n_layer
    vmem, smem = pl.BlockSpec(memory_space=pltpu.VMEM), pl.BlockSpec(memory_space=pltpu.SMEM)
    hbm = pl.BlockSpec(memory_space=pltpu.HBM)
    panel_bytes = 2 * rows * width * (slots + n_row + 1)
    updated, lines = pl.pallas_call(
        functools.partial(kernel, sizes),
        out_shape=(
            jax.ShapeDtypeStruct((rows, width), jnp.float32),
            jax.ShapeDtypeStruct((3, blk), jnp.float32),
        ),
        in_specs=[hbm, hbm, hbm, hbm],
        out_specs=(vmem, vmem),
        scratch_shapes=[
            pltpu.VMEM((rows, width), jnp.bfloat16),
            pltpu.SMEM(block_mask.T.shape, jnp.int32),
            pltpu.SMEM(keep_mask.T.shape, jnp.int32),
            pltpu.SMEM(branch_flag.shape, jnp.int32),
            pltpu.VMEM((slots, rows, width), jnp.bfloat16),
            pltpu.VMEM((n_row, rows, width), jnp.bfloat16),
            pltpu.VMEM((3, blk), jnp.float32),
            pltpu.VMEM((n_row * slots, 3, blk), jnp.float32),
            dma((CHUNKS + 3,)),
            dma((1,)),
            dma((max(n_col - 1, 1), 2)),
            dma((1,)),
            dma((3,)),
            dma((1,)),
            dma((1,)),
            dma((n_row, CHUNKS)),
            dma((1,)),
            dma((2,)),
            pltpu.VMEM((n_layer, 3, blk), jnp.float32),
            pltpu.VMEM((3, blk), jnp.float32),
            pltpu.VMEM((rows // CHUNKS, width), jnp.bfloat16),
            dma((1,)),
            dma((1,)),
            pltpu.SemaphoreType.REGULAR((4,)),
        ],
        compiler_params=pltpu.CompilerParams(
            collective_id=0, has_side_effects=True,
            vmem_limit_bytes=panel_bytes + 8 * rows * width + (4 << 20)),
    )(*[
        pltpu.with_memory_space_constraint(x, pltpu.HBM)
        for x in (density, block_mask.T, keep_mask.T, branch_flag)
    ])
    updated, trace = pl.pallas_call(
        deliver,
        out_shape=(
            jax.ShapeDtypeStruct((rows, width), jnp.float32),
            jax.ShapeDtypeStruct((1, 1), jnp.float32),
        ),
        in_specs=[vmem, vmem],
        out_specs=(vmem, smem),
        compiler_params=pltpu.CompilerParams(
            vmem_limit_bytes=8 * rows * width + (4 << 20)),
    )(updated, lines)
    return updated, trace[0, 0]


def solution(mesh):
    sizes = tuple(mesh.shape[name] for name in ("row", "col", "layer"))
    in_specs = (
        P("row", ("col", "layer")),
        P("row", ("col", "layer")),
        P("row", ("col", "layer")),
        P("row"),
    )
    out_specs = (P("row", ("col", "layer")), P())
    return jax.shard_map(
        functools.partial(on_device, sizes), mesh=mesh, in_specs=in_specs,
        out_specs=out_specs, check_vma=False,
    )
```

```python
import functools

import jax
import jax.numpy as jnp
from jax import lax
from jax.experimental import pallas as pl
from jax.experimental.pallas import tpu as pltpu
from jax.sharding import PartitionSpec as P

MESH = pl.DeviceIdType.MESH
CHUNKS = 4
AHEAD = 2


def partner_of(index, step, size):
    if size & (size - 1):
        return (index + step) % size
    for bit in range(size.bit_length()):
        if step >> bit & 1:
            index = index + (1 - 2 * ((index // (1 << bit)) % 2)) * (1 << bit)
    return index


def passing_plans(n_row):
    last = n_row - 1
    blocks = [[(b, q) for q in range(CHUNKS)] for b in range(n_row)]
    rightward = [sum(blocks[row::-1], []) for row in range(last)] + [[]]
    leftward = [[]] + [sum(blocks[row:], []) for row in range(1, n_row)]
    for row in range(1, last):
        for order, block, count in ((rightward[row], 1, 2), (leftward[row], last - 1, 1)):
            for q in range(CHUNKS - count, CHUNKS):
                order.remove((block, q))
                order.append((block, q))
    leftward[1].remove((1, CHUNKS - 1))
    leftward[1].append((1, CHUNKS - 1))
    return rightward, leftward


def kernel(
    sizes, density_hbm, block_hbm, keep_hbm, flag_hbm, updated, lines,
    density, block_mask, keep_mask, branch_flag,
    row_panel, col_panel, trace_own, trace_in, local_sem,
    plane_send, plane_recv, side_send, side_recv, right_send, left_send, z_recv,
    trace_send, trace_recv, trace_swap, trace_sum, aside, aside_send, aside_sems, ready,
):
    n_row, n_col, n_layer = sizes
    rows, width = density.shape
    blk = rows // block_mask.shape[1]
    per = rows // width
    piece = rows // CHUNKS
    slots = n_col * n_layer
    last = n_row - 1
    r, c, l = lax.axis_index("row"), lax.axis_index("col"), lax.axis_index("layer")
    me = c * n_layer + l
    has_left, has_right = r > 0, r < last
    left, right = jnp.maximum(r - 1, 0), jnp.minimum(r + 1, last)
    col_peers = [partner_of(c, d, n_col) for d in range(1, n_col)]
    layer_peers = [partner_of(l, d, n_layer) for d in range(1, n_layer)]

    bits = [d for d in range(1, n_col) if d & (d - 1) == 0]
    relayed = [lo | hi for hi in bits for lo in bits if lo < hi]
    if n_col & (n_col - 1):
        bits, relayed = list(range(1, n_col)), []
    direct = [d for d in range(1, n_col) if d not in relayed]
    halves = {d: (1, 0) if relayed and d > 1 else (0, 1) for d in range(1, n_col)}

    plane_peers = [(c, q, True, 1) for q in layer_peers]
    for d in range(1, n_col):
        p = col_peers[d - 1]
        met = (p * c == 0) if d in relayed and len(bits) == 2 else True
        plane_peers += [(p, q, met, 3 if d in relayed else 1) for q in range(n_layer)]

    def counted(which, above):
        return sum(jnp.where(((p * n_layer + q > me) == above) & met, 1, 0)
                   for p, q, met, to in plane_peers if to in which)

    def span(q):
        return pl.ds(q * piece, piece)

    loads = [
        pltpu.make_async_copy(source, target, local_sem.at[i])
        for i, (source, target) in enumerate(
            [(block_hbm, block_mask)]
            + [(density_hbm.at[span(q)], density.at[span(q)]) for q in range(CHUNKS)]
            + [(keep_hbm, keep_mask), (flag_hbm, branch_flag)])
    ]
    for load in loads:
        load.start()

    barrier = pltpu.get_barrier_semaphore()

    def greet(target):
        pl.semaphore_signal(barrier, inc=1, device_id=target, device_id_type=MESH)

    def answer(which, target):
        pl.semaphore_signal(
            ready.at[which], inc=1, device_id=target, device_id_type=MESH)

    pl.when(has_right)(lambda: greet((right, c, l)))
    for p, q, met, _ in plane_peers:
        pl.when((p * n_layer + q > me) & met)(functools.partial(greet, (r, p, q)))
    below = jnp.where(has_left, 1, 0) + counted((1, 3), False)
    pl.when(below > 0)(lambda: pl.semaphore_wait(barrier, below))
    pl.when(has_left)(lambda: answer(0, (left, c, l)))
    for p, q, met, to in plane_peers:
        pl.when((p * n_layer + q < me) & met)(functools.partial(answer, to, (r, p, q)))
    def mask(q):
        loads[1 + q].wait()
        for i in range(q * piece // blk, (q + 1) * piece // blk):
            for k in range(width // blk):
                at = (pl.ds(i * blk, blk), pl.ds(k * blk, blk))
                kept = jnp.full((blk, blk), block_mask[k, i].astype(jnp.float32))
                row_panel[(me,) + at] = density[at] * kept.astype(jnp.bfloat16)

    loads[0].wait()

    def z_copy(block, q, source, target, sem):
        return pltpu.make_async_remote_copy(
            src_ref=source, dst_ref=col_panel.at[block, span(q)],
            send_sem=sem.at[0], recv_sem=z_recv.at[block, q],
            device_id=(target, c, l), device_id_type=MESH,
        )

    def to_right(block, q, source):
        return z_copy(block, q, source, right, right_send)

    def to_left(block, q, source):
        return z_copy(block, q, source, left, left_send)

    def half_copy(slot, h, sem, recv, target):
        half = pl.ds(h * (rows // 2), rows // 2)
        return pltpu.make_async_remote_copy(
            src_ref=row_panel.at[slot, half], dst_ref=row_panel.at[slot, half],
            send_sem=sem.at[0], recv_sem=recv, device_id=target, device_id_type=MESH,
        )

    def plane_copy(slot, h, d, peer):
        return half_copy(slot, h, plane_send, plane_recv.at[d - 1, h], (r, peer, l))

    def side_copies(slot, h, group):
        for other in layer_peers:
            half_copy(slot, h, side_send, side_recv.at[group], (r, c, other)).start()

    def side_wait(count, group):
        blocks = row_panel.at[pl.ds(0, count)]
        if count:
            pltpu.make_async_remote_copy(
                src_ref=blocks, dst_ref=blocks, send_sem=side_send.at[0],
                recv_sem=side_recv.at[group], device_id=(r, c, l), device_id_type=MESH,
            ).wait_recv()

    def seen(d):
        return n_col - d if n_col & (n_col - 1) else d

    def plane_start(chosen):
        for turn in range(2):
            for d in direct:
                peer = col_peers[d - 1]
                pl.when(chosen(peer))(
                    lambda: plane_copy(me, halves[d][turn], seen(d), peer).start())

    def plane_arrive(d, turn):
        peer, h = col_peers[d - 1], halves[d][turn]
        slot = peer * n_layer + l
        plane_copy(slot, h, d, peer).wait_recv()
        for other in bits if relayed and d in bits else []:
            if (other > d) == (h == 0) and other != d:
                plane_copy(slot, h, d | other, col_peers[other - 1]).start()
        side_copies(slot, h, 2 if d in relayed else 1)

    rightward, leftward = passing_plans(n_row)
    from_left = [[]] + rightward[:-1]
    from_right = leftward[1:] + [[]]

    on_diagonal = me // per == r

    detour = bool(relayed) and n_layer <= len(bits)
    by_way = functools.reduce(jnp.logical_or, [
        (l == layer) & (c == bits[layer]) for layer in range(n_layer if detour else 0)],
        c < 0)

    def detour_copy(source, target, column, row, sem, recv):
        return pltpu.make_async_remote_copy(
            src_ref=source, dst_ref=target, send_sem=sem.at[0], recv_sem=recv,
            device_id=(row, column, l), device_id_type=MESH,
        )

    def detour_start():
        for layer in range(n_layer):
            pl.when((r == 1) & (c == 0) & (l == layer))(detour_copy(
                row_panel.at[me, span(CHUNKS - 1)], aside, bits[layer], 1,
                left_send, aside_sems.at[0]).start)

    def detour_pass(row):
        target, recv = ((aside, aside_sems.at[0]) if row else
                        (col_panel.at[1, span(CHUNKS - 1)], z_recv.at[1, CHUNKS - 1]))

        @pl.when(by_way & (r == row))
        def _():
            detour_copy(aside, aside, c, 0, aside_send, aside_sems.at[0]).wait_recv()
            detour_copy(aside, target, c if row else 0, 0, aside_send, recv).start()

    def pass_on(copy, row, plan, first, arrived, stop=None, hold=None):
        while first < len(plan) and (stop is None or first < stop):
            block, q = plan[first]
            if block == row:
                source = row_panel.at[me, span(q)]
            elif (block, q) in arrived:
                source = col_panel.at[block, span(q)]
            else:
                break
            if detour and copy is to_left and (row, block, q) == (1, 1, CHUNKS - 1):
                pl.when(jnp.logical_not(on_diagonal) & (c > 0))(
                    functools.partial(lambda f: f.start(), copy(block, q, source)))
            elif hold is None or first < hold:
                copy(block, q, source).start()
            else:
                pl.when(jnp.logical_not(on_diagonal))(
                    functools.partial(lambda f: f.start(), copy(block, q, source)))
            first += 1
        return first

    sent_left, sent_right = [0] * n_row, [0] * n_row
    hold_left, hold_right = {1: last * CHUNKS - 2}, {last - 1: 2 * CHUNKS - 1}
    for q in range(CHUNKS):
        mask(q)
        for row in range(1, n_row) if q < AHEAD else []:
            @pl.when(r == row)
            def _():
                sent_left[row] = pass_on(
                    to_left, row, leftward[row], sent_left[row], (), q + 1)
    for load in loads[1 + CHUNKS:]:
        load.wait()
    plane_start(lambda peer: peer < c)
    pl.when(has_right)(lambda: pl.semaphore_wait(ready.at[0], 1))
    for row in range(last):
        @pl.when(r == row)
        def _():
            sent_right[row] = pass_on(to_right, row, rightward[row], 0, (), AHEAD)
    near_above, far_above = counted((1,), True), counted((3,), True)
    pl.when(near_above > 0)(lambda: pl.semaphore_wait(ready.at[1], near_above))
    for row in range(n_row):
        @pl.when(r == row)
        def _():
            sent_left[row] = pass_on(
                to_left, row, leftward[row], sent_left[row], (),
                CHUNKS - 1 if row == last else None, hold_left.get(row))
            sent_right[row] = pass_on(
                to_right, row, rightward[row], sent_right[row], (), None, hold_right.get(row))
    if detour:
        detour_start()
    plane_start(lambda peer: peer > c)
    for h in range(2):
        side_copies(me, h, 0)

    def z_arrive(k, then=None):
        for row in range(n_row):
            if k < max(len(from_right[row]), len(from_left[row])):
                @pl.when(r == row)
                def _():
                    if k < len(from_right[row]):
                        block, q = from_right[row][k]
                        to_left(block, q, col_panel.at[block, span(q)]).wait_recv()
                        sent_left[row] = pass_on(
                            to_left, row, leftward[row], sent_left[row],
                            from_right[row][:k + 1], None, hold_left.get(row))
                        if then:
                            then(row, from_right[row], k)
                    if k < len(from_left[row]):
                        block, q = from_left[row][k]
                        to_right(block, q, col_panel.at[block, span(q)]).wait_recv()
                        sent_right[row] = pass_on(
                            to_right, row, rightward[row], sent_right[row],
                            from_left[row][:k + 1], None, hold_right.get(row))
                        if then:
                            then(row, from_left[row], k)

    def terms(block, start, size):
        out = []
        while size:
            step = min(size, width - start % width)
            out.append(jnp.dot(
                row_panel[block * per + start // width, :, pl.ds(start % width, step)],
                col_panel[block, pl.ds(start, step), :],
                preferred_element_type=jnp.float32))
            start, size = start + step, size - step
        return out

    def add(products):
        total = products[0]
        for product in products[1:]:
            total = total + product
        updated[...] += total

    corner = pl.multiple_of((me % per) * width, width)
    tiles = width // blk
    lanes = lax.broadcasted_iota(jnp.int32, (1, blk), 1)
    eye = (lax.broadcasted_iota(jnp.int32, (blk, blk), 0)
           == lax.broadcasted_iota(jnp.int32, (blk, blk), 1))

    def weight(t, if_square, otherwise):
        kept = keep_mask[t, (me % per) * tiles + t]
        chosen = jnp.where(branch_flag[(me % per) * tiles + t] == 1, if_square, otherwise)
        return (kept * chosen).astype(jnp.float32)

    def pair_sums(block, k):
        slot = block * per + k * blk // width
        out = []
        for t in range(tiles):
            ours = row_panel[slot, pl.ds(corner + t * blk, blk), pl.ds(k * blk % width, blk)]
            if block is r:
                theirs = row_panel[me, pl.ds(k * blk, blk), pl.ds(t * blk, blk)]
            else:
                theirs = col_panel[block, pl.ds(k * blk, blk), pl.ds(t * blk, blk)]
            product = jnp.dot(ours, theirs, preferred_element_type=jnp.float32)
            out.append(jnp.sum(jnp.where(eye, product, 0.0), axis=0, keepdims=True))
        return out

    def trace_copy(z, col, layer):
        return pltpu.make_async_remote_copy(
            src_ref=trace_own, dst_ref=trace_in.at[me],
            send_sem=trace_send.at[0], recv_sem=trace_recv.at[0],
            device_id=(z, col, layer), device_id_type=MESH,
        )

    assert per % n_layer == 0
    firsts = per // n_layer

    def swap_copy(other):
        return pltpu.make_async_remote_copy(
            src_ref=trace_own, dst_ref=trace_swap.at[l],
            send_sem=trace_send.at[0], recv_sem=trace_recv.at[1],
            device_id=(r, c, other), device_id_type=MESH,
        )

    def sum_copy(z, col, layer):
        return pltpu.make_async_remote_copy(
            src_ref=trace_sum, dst_ref=trace_in.at[me],
            send_sem=trace_send.at[0], recv_sem=trace_recv.at[0],
            device_id=(z, col, layer), device_id_type=MESH,
        )

    def send_first():
        trace_swap[l] = trace_own[...]
        for other in layer_peers:
            swap_copy(other).start()
        if n_layer > 1:
            pltpu.make_async_remote_copy(
                src_ref=trace_in.at[pl.ds(0, n_layer - 1)],
                dst_ref=trace_in.at[pl.ds(0, n_layer - 1)],
                send_sem=trace_send.at[0], recv_sem=trace_recv.at[1],
                device_id=(r, c, l), device_id_type=MESH,
            ).wait_recv()
        total = trace_swap[0]
        for layer in range(1, n_layer):
            total = total + trace_swap[layer]
        trace_sum[...] = total
        trace_in[me] = total
        @pl.when(l == 0)
        def _():
            for col in range(n_col):
                for layer in range(n_layer):
                    sum_copy(last, col, layer).start()

        for z in range(last - 1, -1, -1):
            for col in range(n_col):
                if z:
                    sum_copy(z, col, l).start()
                else:
                    pl.when(col != c)(lambda: sum_copy(z, col, l).start())

    everyone = [(z, col, layer) for z in range(n_row) for col in range(n_col)
                for layer in range(n_layer)]

    def add_trace(chunks, start):
        weights = [weight(t, 1, -1) for t in range(tiles)]
        part = spread = others = jnp.zeros((1, blk), jnp.float32)
        if not start:
            part, spread, others = (trace_own[n:n + 1, :] for n in range(3))
        for t in range(tiles if start else 0):
            own = row_panel[me, pl.ds(corner + t * blk, blk), pl.ds(t * blk, blk)]
            line = jnp.sum(
                jnp.where(eye, own.astype(jnp.float32), 0.0), axis=0, keepdims=True)
            part += weight(t, 0, 2) * line
            spread += jnp.where(lanes == me * tiles + t, weights[t], 0.0)
        every = range(rows // blk)
        for block, k in ([(r, k) for k in every] if start else []) + chunks:
            sums = pair_sums(block, k)
            for t in range(tiles):
                part += weights[t] * sums[t]
            if block is not r:
                here = block * (rows // blk) + k
                total = sum(jnp.sum(line, keepdims=True) for line in sums)
                others += jnp.where(lanes == here, total, 0.0)
        trace_own[0:1, :] = part
        trace_own[1:2, :] = spread
        trace_own[2:3, :] = others

    def send_trace(row):
        trace_in[me] = trace_own[...]
        for z, col, layer in everyone:
            if z != row:
                trace_copy(z, col, layer).start()
            else:
                pl.when((col != c) | (layer != l))(
                    lambda: trace_copy(z, col, layer).start())

    middle = (last - 1) * CHUNKS
    pairs = {row: [0] + list(range(row + 1, n_row)) for row in range(1, last)}
    pairs.update({0: [last], last: []})
    asked = list(range(1, n_row))

    def ready_rows(count, distances):
        def at_hand(b, row):
            arrived = (from_left if b < row else from_right)[row][:count]
            apart = (b * per // n_layer) ^ (row * per // n_layer)
            return ([x for x, _ in arrived].count(b) == CHUNKS
                    and (apart in distances or not relayed))

        return [row for row in asked if all(at_hand(b, row) for b in pairs[row])]

    def diagonals(chosen):
        for row in chosen:
            asked.remove(row)

            @pl.when(on_diagonal & (r == row))
            def _():
                add_trace([(b, k) for b in pairs[row] for k in range(rows // blk)], True)
                send_trace(row)
                for copy, plan, sent, hold in (
                        (to_left, leftward, sent_left, hold_left),
                        (to_right, rightward, sent_right, hold_right)):
                    if row in hold:
                        for block, q in plan[row][hold[row]:sent[row]]:
                            copy(block, q, row_panel.at[me, span(q)] if block == row
                                 else col_panel.at[block, span(q)]).start()
            hold_left.pop(row, None)
            hold_right.pop(row, None)

    pl.when(far_above > 0)(lambda: pl.semaphore_wait(ready.at[3], far_above))
    @pl.when(r == last)
    def _():
        sent_left[last] = pass_on(to_left, last, leftward[last], sent_left[last], ())
    pl.when(has_left)(lambda: pl.semaphore_wait(ready.at[2], 1))
    pl.when(has_right)(lambda: answer(2, (right, c, l)))
    side_wait(n_layer - 1, 0)
    pl.when(on_diagonal & (r == 0))(lambda: add_trace([], True))
    diagonals(ready_rows(0, ()))
    for k in range(CHUNKS // 2):
        z_arrive(k)
    for d in direct:
        plane_arrive(d, 0)
    for k in range(CHUNKS // 2, CHUNKS):
        z_arrive(k)
    if detour:
        detour_pass(1)
    for d in direct:
        plane_arrive(d, 1)
    for k in range(CHUNKS, CHUNKS + 1):
        z_arrive(k)
    for k in range(CHUNKS + 1, CHUNKS + 2):
        z_arrive(k)
    def sides(chosen):
        side_wait(len(chosen) * (n_layer - 1), 2 if chosen is relayed else 1)

    soon = ready_rows(CHUNKS + 2, direct)
    in_soon = functools.reduce(jnp.logical_or, [r == row for row in soon], r < 0)
    pl.when(in_soon)(lambda: sides(direct))
    diagonals(soon)
    for turn in range(2):
        for d in relayed:
            plane_arrive(d, turn)
    if detour:
        detour_pass(0)
    for k in range(CHUNKS + 2, middle):
        z_arrive(k)
    pl.when(jnp.logical_not(in_soon))(lambda: sides(direct))
    sides(relayed)
    diagonals(list(asked))

    total = None
    for t in range(per):
        term = jnp.dot(
            row_panel[r * per + t], row_panel[me, pl.ds(t * width, width), :],
            preferred_element_type=jnp.float32)
        total = term if total is None else total + term
    updated[...] = total
    inner = has_left & has_right
    for s in range(1, last):
        pl.when((r - s >= 0) & inner)(lambda: add(terms(r - s, 0, rows)))
        pl.when((r + s <= last) & inner)(lambda: add(terms(r + s, 0, rows)))
    for row, arrived in ((0, from_right[0]), (last, from_left[last])):
        @pl.when(r == row)
        def _():
            products = []
            for block in range(n_row):
                chunks = sorted(q for b, q in arrived[:middle] if b == block)
                if chunks:
                    assert chunks == list(range(len(chunks)))
                    products += terms(block, 0, len(chunks) * piece)
            add(products)

    def finish(row, arrived, k):
        block, q = arrived[k]
        if row == 0 and block in pairs[0]:
            @pl.when(on_diagonal)
            def _():
                add_trace(parts_of([(block, q)]), False)
                if (block, q) == (last, CHUNKS - 1):
                    send_first()
        if k < last * CHUNKS - 1:
            add(terms(block, q * piece, piece))
        else:
            update(terms(block, q * piece, piece))

    def update(products):
        for i in range(rows // blk):
            flag = jnp.full((blk, blk), branch_flag[i]) == 1
            for k in range(width // blk):
                at = (pl.ds(i * blk, blk), pl.ds(k * blk, blk))
                square = updated[at]
                for product in products:
                    square += product[i * blk:(i + 1) * blk, k * blk:(k + 1) * blk]
                doubled = 2.0 * row_panel[(me,) + at].astype(jnp.float32) - square
                kept = jnp.full((blk, blk), keep_mask[k, i].astype(jnp.float32))
                updated[at] = jnp.where(flag, square, doubled) * kept

    def parts_of(chunks):
        share = piece // blk
        return [(b, q * share + k) for b, q in chunks if b in pairs[0] for k in range(share)]

    pl.when(on_diagonal & (r == 0))(
        lambda: add_trace(parts_of(from_right[0][:middle]), False))
    for k in range(middle, last * CHUNKS):
        z_arrive(k, finish)

    pl.when(inner)(lambda: update([]))

    if detour:
        pl.when(by_way & (r < 2))(
            detour_copy(aside, aside, c, 0, aside_send, aside_sems.at[0]).wait_send)
    for row in range(n_row):
        @pl.when(r == row)
        def _():
            for copy, plan, sem in (
                    (to_left, leftward[row], left_send),
                    (to_right, rightward[row], right_send)):
                if plan:
                    blocks = pl.ds(0, len(plan) // CHUNKS)
                    pltpu.make_async_remote_copy(
                        src_ref=col_panel.at[blocks], dst_ref=col_panel.at[blocks],
                        send_sem=sem.at[0], recv_sem=z_recv.at[0, 0],
                        device_id=(left, c, l), device_id_type=MESH,
                    ).wait_send()

    def sent_slots(count, ref, sem):
        pltpu.make_async_remote_copy(
            src_ref=ref.at[pl.ds(0, count)], dst_ref=ref.at[pl.ds(0, count)],
            send_sem=sem.at[0], recv_sem=plane_recv.at[0, 0],
            device_id=(r, c, l), device_id_type=MESH,
        ).wait_send()

    sent_slots(n_col - 1, row_panel, plane_send)
    sent_slots((n_layer - 1) * n_col, row_panel, side_send)

    def heard(count):
        pltpu.make_async_remote_copy(
            src_ref=trace_in.at[pl.ds(0, count)], dst_ref=trace_in.at[pl.ds(0, count)],
            send_sem=trace_send.at[0], recv_sem=trace_recv.at[0],
            device_id=(r, c, l), device_id_type=MESH,
        ).wait_recv()

    pl.when(on_diagonal)(lambda: heard(slots - per + firsts - 1))
    pl.when(jnp.logical_not(on_diagonal))(lambda: heard(slots - per + firsts))
    giver = jnp.where(r == last, 0, l)
    parts = trace_in[giver]
    for slot in range(1, firsts):
        parts = parts + trace_in[slot * n_layer + giver]
    for slot in range(per, slots):
        parts = parts + trace_in[slot]
    lines[...] = parts
    pl.when(on_diagonal & has_left)(
        lambda: sent_slots(n_row * slots - 1, trace_in, trace_send))
    first_sent = last * n_col + n_layer - 2
    for core, count in ((l == 0, first_sent + n_col * n_layer), (l > 0, first_sent)):
        pl.when(on_diagonal & jnp.logical_not(has_left) & core)(
            functools.partial(sent_slots, count, trace_in, trace_send))


def deliver(updated, lines, out, trace):
    out[...] = updated[...]
    trace[0, 0] = jnp.sum(lines[0:1, :] + lines[1:2, :] * lines[2:3, :])


def on_device(sizes, density, block_mask, keep_mask, branch_flag):
    n_row, n_col, n_layer = sizes
    rows, width = density.shape
    blk = rows // block_mask.shape[0]
    dma = pltpu.SemaphoreType.DMA
    slots = n_col * n_layer
    vmem, smem = pl.BlockSpec(memory_space=pltpu.VMEM), pl.BlockSpec(memory_space=pltpu.SMEM)
    hbm = pl.BlockSpec(memory_space=pltpu.HBM)
    panel_bytes = 2 * rows * width * (slots + n_row + 1)
    updated, lines = pl.pallas_call(
        functools.partial(kernel, sizes),
        out_shape=(
            jax.ShapeDtypeStruct((rows, width), jnp.float32),
            jax.ShapeDtypeStruct((3, blk), jnp.float32),
        ),
        in_specs=[hbm, hbm, hbm, hbm],
        out_specs=(vmem, vmem),
        scratch_shapes=[
            pltpu.VMEM((rows, width), jnp.bfloat16),
            pltpu.SMEM(block_mask.T.shape, jnp.int32),
            pltpu.SMEM(keep_mask.T.shape, jnp.int32),
            pltpu.SMEM(branch_flag.shape, jnp.int32),
            pltpu.VMEM((slots, rows, width), jnp.bfloat16),
            pltpu.VMEM((n_row, rows, width), jnp.bfloat16),
            pltpu.VMEM((3, blk), jnp.float32),
            pltpu.VMEM((n_row * slots, 3, blk), jnp.float32),
            dma((CHUNKS + 3,)),
            dma((1,)),
            dma((max(n_col - 1, 1), 2)),
            dma((1,)),
            dma((3,)),
            dma((1,)),
            dma((1,)),
            dma((n_row, CHUNKS)),
            dma((1,)),
            dma((2,)),
            pltpu.VMEM((n_layer, 3, blk), jnp.float32),
            pltpu.VMEM((3, blk), jnp.float32),
            pltpu.VMEM((rows // CHUNKS, width), jnp.bfloat16),
            dma((1,)),
            dma((1,)),
            pltpu.SemaphoreType.REGULAR((4,)),
        ],
        compiler_params=pltpu.CompilerParams(
            collective_id=0, has_side_effects=True,
            vmem_limit_bytes=panel_bytes + 8 * rows * width + (4 << 20)),
    )(*[
        pltpu.with_memory_space_constraint(x, pltpu.HBM)
        for x in (density, block_mask.T, keep_mask.T, branch_flag)
    ])
    updated, trace = pl.pallas_call(
        deliver,
        out_shape=(
            jax.ShapeDtypeStruct((rows, width), jnp.float32),
            jax.ShapeDtypeStruct((1, 1), jnp.float32),
        ),
        in_specs=[vmem, vmem],
        out_specs=(vmem, smem),
        compiler_params=pltpu.CompilerParams(
            vmem_limit_bytes=8 * rows * width + (4 << 20)),
    )(updated, lines)
    return updated, trace[0, 0]


def solution(mesh):
    sizes = tuple(mesh.shape[name] for name in ("row", "col", "layer"))
    in_specs = (
        P("row", ("col", "layer")),
        P("row", ("col", "layer")),
        P("row", ("col", "layer")),
        P("row"),
    )
    out_specs = (P("row", ("col", "layer")), P())
    return jax.shard_map(
        functools.partial(on_device, sizes), mesh=mesh, in_specs=in_specs,
        out_specs=out_specs, check_vma=False,
    )
```

```python
import functools

import jax
import jax.numpy as jnp
from jax import lax
from jax.experimental import pallas as pl
from jax.experimental.pallas import tpu as pltpu
from jax.sharding import PartitionSpec as P

MESH = pl.DeviceIdType.MESH
CHUNKS = 4
AHEAD = 2


def partner_of(index, step, size):
    if size & (size - 1):
        return (index + step) % size
    for bit in range(size.bit_length()):
        if step >> bit & 1:
            index = index + (1 - 2 * ((index // (1 << bit)) % 2)) * (1 << bit)
    return index


def passing_plans(n_row):
    last = n_row - 1
    blocks = [[(b, q) for q in range(CHUNKS)] for b in range(n_row)]
    rightward = [sum(blocks[row::-1], []) for row in range(last)] + [[]]
    leftward = [[]] + [sum(blocks[row:], []) for row in range(1, n_row)]
    for row in range(1, last):
        for order, block, count in ((rightward[row], 1, 2), (leftward[row], last - 1, 1)):
            for q in range(CHUNKS - count, CHUNKS):
                order.remove((block, q))
                order.append((block, q))
    leftward[1].remove((1, CHUNKS - 1))
    leftward[1].append((1, CHUNKS - 1))
    return rightward, leftward


def kernel(
    sizes, density_hbm, block_hbm, keep_hbm, flag_hbm, updated, lines,
    density, block_mask, keep_mask, branch_flag,
    row_panel, col_panel, trace_own, trace_in, local_sem,
    plane_send, plane_recv, side_send, side_recv, right_send, left_send, z_recv,
    trace_send, trace_recv, trace_swap, trace_sum, aside, aside_send, aside_sems, ready,
):
    n_row, n_col, n_layer = sizes
    rows, width = density.shape
    blk = rows // block_mask.shape[1]
    per = rows // width
    piece = rows // CHUNKS
    slots = n_col * n_layer
    last = n_row - 1
    r, c, l = lax.axis_index("row"), lax.axis_index("col"), lax.axis_index("layer")
    me = c * n_layer + l
    has_left, has_right = r > 0, r < last
    left, right = jnp.maximum(r - 1, 0), jnp.minimum(r + 1, last)
    col_peers = [partner_of(c, d, n_col) for d in range(1, n_col)]
    layer_peers = [partner_of(l, d, n_layer) for d in range(1, n_layer)]

    bits = [d for d in range(1, n_col) if d & (d - 1) == 0]
    relayed = [lo | hi for hi in bits for lo in bits if lo < hi]
    if n_col & (n_col - 1):
        bits, relayed = list(range(1, n_col)), []
    direct = [d for d in range(1, n_col) if d not in relayed]
    halves = {d: (1, 0) if relayed and d > 1 else (0, 1) for d in range(1, n_col)}

    plane_peers = [(c, q, True, 1) for q in layer_peers]
    for d in range(1, n_col):
        p = col_peers[d - 1]
        met = (p * c == 0) if d in relayed and len(bits) == 2 else True
        plane_peers += [(p, q, met, 3 if d in relayed else 1) for q in range(n_layer)]

    def counted(which, above):
        return sum(jnp.where(((p * n_layer + q > me) == above) & met, 1, 0)
                   for p, q, met, to in plane_peers if to in which)

    def span(q):
        return pl.ds(q * piece, piece)

    loads = [
        pltpu.make_async_copy(source, target, local_sem.at[i])
        for i, (source, target) in enumerate(
            [(block_hbm, block_mask)]
            + [(density_hbm.at[span(q)], density.at[span(q)]) for q in range(CHUNKS)]
            + [(keep_hbm, keep_mask), (flag_hbm, branch_flag)])
    ]
    for load in loads:
        load.start()

    barrier = pltpu.get_barrier_semaphore()

    def greet(target):
        pl.semaphore_signal(barrier, inc=1, device_id=target, device_id_type=MESH)

    def answer(which, target):
        pl.semaphore_signal(
            ready.at[which], inc=1, device_id=target, device_id_type=MESH)

    pl.when(has_right)(lambda: greet((right, c, l)))
    for p, q, met, _ in plane_peers:
        pl.when((p * n_layer + q > me) & met)(functools.partial(greet, (r, p, q)))
    below = jnp.where(has_left, 1, 0) + counted((1, 3), False)
    pl.when(below > 0)(lambda: pl.semaphore_wait(barrier, below))
    pl.when(has_left)(lambda: answer(0, (left, c, l)))
    for p, q, met, to in plane_peers:
        pl.when((p * n_layer + q < me) & met)(functools.partial(answer, to, (r, p, q)))
    def mask(q):
        loads[1 + q].wait()
        for i in range(q * piece // blk, (q + 1) * piece // blk):
            for k in range(width // blk):
                at = (pl.ds(i * blk, blk), pl.ds(k * blk, blk))
                kept = jnp.full((blk, blk), block_mask[k, i].astype(jnp.float32))
                row_panel[(me,) + at] = density[at] * kept.astype(jnp.bfloat16)

    loads[0].wait()

    def z_copy(block, q, source, target, sem):
        return pltpu.make_async_remote_copy(
            src_ref=source, dst_ref=col_panel.at[block, span(q)],
            send_sem=sem.at[0], recv_sem=z_recv.at[block, q],
            device_id=(target, c, l), device_id_type=MESH,
        )

    def to_right(block, q, source):
        return z_copy(block, q, source, right, right_send)

    def to_left(block, q, source):
        return z_copy(block, q, source, left, left_send)

    def half_copy(slot, h, sem, recv, target):
        half = pl.ds(h * (rows // 2), rows // 2)
        return pltpu.make_async_remote_copy(
            src_ref=row_panel.at[slot, half], dst_ref=row_panel.at[slot, half],
            send_sem=sem.at[0], recv_sem=recv, device_id=target, device_id_type=MESH,
        )

    def plane_copy(slot, h, d, peer):
        return half_copy(slot, h, plane_send, plane_recv.at[d - 1, h], (r, peer, l))

    def side_copies(slot, h, group):
        for other in layer_peers:
            half_copy(slot, h, side_send, side_recv.at[group], (r, c, other)).start()

    def side_wait(count, group):
        blocks = row_panel.at[pl.ds(0, count)]
        if count:
            pltpu.make_async_remote_copy(
                src_ref=blocks, dst_ref=blocks, send_sem=side_send.at[0],
                recv_sem=side_recv.at[group], device_id=(r, c, l), device_id_type=MESH,
            ).wait_recv()

    def seen(d):
        return n_col - d if n_col & (n_col - 1) else d

    def plane_start(chosen):
        for turn in range(2):
            for d in direct:
                peer = col_peers[d - 1]
                pl.when(chosen(peer))(
                    lambda: plane_copy(me, halves[d][turn], seen(d), peer).start())

    def plane_arrive(d, turn):
        peer, h = col_peers[d - 1], halves[d][turn]
        slot = peer * n_layer + l
        plane_copy(slot, h, d, peer).wait_recv()
        for other in bits if relayed and d in bits else []:
            if (other > d) == (h == 0) and other != d:
                plane_copy(slot, h, d | other, col_peers[other - 1]).start()
        side_copies(slot, h, 2 if d in relayed else 1)

    rightward, leftward = passing_plans(n_row)
    from_left = [[]] + rightward[:-1]
    from_right = leftward[1:] + [[]]

    on_diagonal = me // per == r

    detour = bool(relayed)
    ways = [(c == d) & (l == n_layer - 1) for d in bits[:2]] if detour else []
    by_way = functools.reduce(jnp.logical_or, ways, c < 0)

    def part_of(h):
        return pl.ds((CHUNKS - 1) * piece + h * (piece // 2), piece // 2)

    def detour_copy(source, target, device, sem, recv):
        return pltpu.make_async_remote_copy(
            src_ref=source, dst_ref=target, send_sem=sem.at[0], recv_sem=recv,
            device_id=device, device_id_type=MESH,
        )

    def detour_start():
        for h, d in enumerate(bits[:2]):
            pl.when((r == 1) & (me == n_layer - 1))(detour_copy(
                row_panel.at[me, part_of(h)], aside, (1, d, n_layer - 1),
                left_send, aside_sems.at[0]).start)

    def detour_pass(row):
        @pl.when(by_way & (r == row))
        def _():
            detour_copy(aside, aside, (0, c, l), aside_send, aside_sems.at[0]).wait_recv()
            if row:
                detour_copy(aside, aside, (0, c, l), aside_send, aside_sems.at[0]).start()

        for h, way in enumerate(ways if row == 0 else []):
            pl.when(way & (r == row))(detour_copy(
                aside, col_panel.at[1, part_of(h)], (0, 0, n_layer - 1),
                aside_send, z_recv.at[1, CHUNKS - 1]).start)

    def pass_on(copy, row, plan, first, arrived, stop=None, hold=None):
        while first < len(plan) and (stop is None or first < stop):
            block, q = plan[first]
            if block == row:
                source = row_panel.at[me, span(q)]
            elif (block, q) in arrived:
                source = col_panel.at[block, span(q)]
            else:
                break
            if detour and copy is to_left and (row, block, q) == (1, 1, CHUNKS - 1):
                pl.when(jnp.logical_not(on_diagonal) & (me != n_layer - 1))(
                    functools.partial(lambda f: f.start(), copy(block, q, source)))
            elif hold is None or first < hold:
                copy(block, q, source).start()
            else:
                pl.when(jnp.logical_not(on_diagonal))(
                    functools.partial(lambda f: f.start(), copy(block, q, source)))
            first += 1
        return first

    sent_left, sent_right = [0] * n_row, [0] * n_row
    hold_left, hold_right = {1: last * CHUNKS - 2}, {last - 1: 2 * CHUNKS - 1}
    for q in range(CHUNKS):
        mask(q)
        for row in range(1, n_row) if q < AHEAD else []:
            @pl.when(r == row)
            def _():
                sent_left[row] = pass_on(
                    to_left, row, leftward[row], sent_left[row], (), q + 1)
    for load in loads[1 + CHUNKS:]:
        load.wait()
    plane_start(lambda peer: peer < c)
    pl.when(has_right)(lambda: pl.semaphore_wait(ready.at[0], 1))
    for row in range(last):
        @pl.when(r == row)
        def _():
            sent_right[row] = pass_on(to_right, row, rightward[row], 0, (), AHEAD)
    near_above, far_above = counted((1,), True), counted((3,), True)
    pl.when(near_above > 0)(lambda: pl.semaphore_wait(ready.at[1], near_above))
    for row in range(n_row):
        @pl.when(r == row)
        def _():
            sent_left[row] = pass_on(
                to_left, row, leftward[row], sent_left[row], (),
                CHUNKS - 1 if row == last else None, hold_left.get(row))
            sent_right[row] = pass_on(
                to_right, row, rightward[row], sent_right[row], (), None, hold_right.get(row))
    if detour:
        detour_start()
    plane_start(lambda peer: peer > c)
    for h in range(2):
        side_copies(me, h, 0)

    def z_arrive(k, then=None):
        for row in range(n_row):
            if k < max(len(from_right[row]), len(from_left[row])):
                @pl.when(r == row)
                def _():
                    if k < len(from_right[row]):
                        block, q = from_right[row][k]
                        to_left(block, q, col_panel.at[block, span(q)]).wait_recv()
                        sent_left[row] = pass_on(
                            to_left, row, leftward[row], sent_left[row],
                            from_right[row][:k + 1], None, hold_left.get(row))
                        if then:
                            then(row, from_right[row], k)
                    if k < len(from_left[row]):
                        block, q = from_left[row][k]
                        to_right(block, q, col_panel.at[block, span(q)]).wait_recv()
                        sent_right[row] = pass_on(
                            to_right, row, rightward[row], sent_right[row],
                            from_left[row][:k + 1], None, hold_right.get(row))
                        if then:
                            then(row, from_left[row], k)

    def terms(block, start, size):
        out = []
        while size:
            step = min(size, width - start % width)
            out.append(jnp.dot(
                row_panel[block * per + start // width, :, pl.ds(start % width, step)],
                col_panel[block, pl.ds(start, step), :],
                preferred_element_type=jnp.float32))
            start, size = start + step, size - step
        return out

    def add(products):
        total = products[0]
        for product in products[1:]:
            total = total + product
        updated[...] += total

    corner = pl.multiple_of((me % per) * width, width)
    tiles = width // blk
    lanes = lax.broadcasted_iota(jnp.int32, (1, blk), 1)
    eye = (lax.broadcasted_iota(jnp.int32, (blk, blk), 0)
           == lax.broadcasted_iota(jnp.int32, (blk, blk), 1))

    def weight(t, if_square, otherwise):
        kept = keep_mask[t, (me % per) * tiles + t]
        chosen = jnp.where(branch_flag[(me % per) * tiles + t] == 1, if_square, otherwise)
        return (kept * chosen).astype(jnp.float32)

    def pair_sums(block, k):
        slot = block * per + k * blk // width
        out = []
        for t in range(tiles):
            ours = row_panel[slot, pl.ds(corner + t * blk, blk), pl.ds(k * blk % width, blk)]
            if block is r:
                theirs = row_panel[me, pl.ds(k * blk, blk), pl.ds(t * blk, blk)]
            else:
                theirs = col_panel[block, pl.ds(k * blk, blk), pl.ds(t * blk, blk)]
            product = jnp.dot(ours, theirs, preferred_element_type=jnp.float32)
            out.append(jnp.sum(jnp.where(eye, product, 0.0), axis=0, keepdims=True))
        return out

    def trace_copy(z, col, layer):
        return pltpu.make_async_remote_copy(
            src_ref=trace_own, dst_ref=trace_in.at[me],
            send_sem=trace_send.at[0], recv_sem=trace_recv.at[0],
            device_id=(z, col, layer), device_id_type=MESH,
        )

    assert per % n_layer == 0
    firsts = per // n_layer

    def swap_copy(other):
        return pltpu.make_async_remote_copy(
            src_ref=trace_own, dst_ref=trace_swap.at[l],
            send_sem=trace_send.at[0], recv_sem=trace_recv.at[1],
            device_id=(r, c, other), device_id_type=MESH,
        )

    def sum_copy(z, col, layer):
        return pltpu.make_async_remote_copy(
            src_ref=trace_sum, dst_ref=trace_in.at[me],
            send_sem=trace_send.at[0], recv_sem=trace_recv.at[0],
            device_id=(z, col, layer), device_id_type=MESH,
        )

    def send_first():
        trace_swap[l] = trace_own[...]
        for other in layer_peers:
            swap_copy(other).start()
        if n_layer > 1:
            pltpu.make_async_remote_copy(
                src_ref=trace_in.at[pl.ds(0, n_layer - 1)],
                dst_ref=trace_in.at[pl.ds(0, n_layer - 1)],
                send_sem=trace_send.at[0], recv_sem=trace_recv.at[1],
                device_id=(r, c, l), device_id_type=MESH,
            ).wait_recv()
        total = trace_swap[0]
        for layer in range(1, n_layer):
            total = total + trace_swap[layer]
        trace_sum[...] = total
        trace_in[me] = total
        @pl.when(l == 0)
        def _():
            for col in range(n_col):
                for layer in range(n_layer):
                    sum_copy(last, col, layer).start()

        for z in range(last - 1, -1, -1):
            for col in range(n_col):
                if z:
                    sum_copy(z, col, l).start()
                else:
                    pl.when(col != c)(lambda: sum_copy(z, col, l).start())

    everyone = [(z, col, layer) for z in range(n_row) for col in range(n_col)
                for layer in range(n_layer)]

    def add_trace(chunks, start):
        weights = [weight(t, 1, -1) for t in range(tiles)]
        part = spread = others = jnp.zeros((1, blk), jnp.float32)
        if not start:
            part, spread, others = (trace_own[n:n + 1, :] for n in range(3))
        for t in range(tiles if start else 0):
            own = row_panel[me, pl.ds(corner + t * blk, blk), pl.ds(t * blk, blk)]
            line = jnp.sum(
                jnp.where(eye, own.astype(jnp.float32), 0.0), axis=0, keepdims=True)
            part += weight(t, 0, 2) * line
            spread += jnp.where(lanes == me * tiles + t, weights[t], 0.0)
        every = range(rows // blk)
        for block, k in ([(r, k) for k in every] if start else []) + chunks:
            sums = pair_sums(block, k)
            for t in range(tiles):
                part += weights[t] * sums[t]
            if block is not r:
                here = block * (rows // blk) + k
                total = sum(jnp.sum(line, keepdims=True) for line in sums)
                others += jnp.where(lanes == here, total, 0.0)
        trace_own[0:1, :] = part
        trace_own[1:2, :] = spread
        trace_own[2:3, :] = others

    def send_trace(row):
        trace_in[me] = trace_own[...]
        for z, col, layer in everyone:
            if z != row:
                trace_copy(z, col, layer).start()
            else:
                pl.when((col != c) | (layer != l))(
                    lambda: trace_copy(z, col, layer).start())

    middle = (last - 1) * CHUNKS
    pairs = {row: [0] + list(range(row + 1, n_row)) for row in range(1, last)}
    pairs.update({0: [last], last: []})
    asked = list(range(1, n_row))

    def ready_rows(count, distances):
        def at_hand(b, row):
            arrived = (from_left if b < row else from_right)[row][:count]
            apart = (b * per // n_layer) ^ (row * per // n_layer)
            return ([x for x, _ in arrived].count(b) == CHUNKS
                    and (apart in distances or not relayed))

        return [row for row in asked if all(at_hand(b, row) for b in pairs[row])]

    def diagonals(chosen):
        for row in chosen:
            asked.remove(row)

            @pl.when(on_diagonal & (r == row))
            def _():
                add_trace([(b, k) for b in pairs[row] for k in range(rows // blk)], True)
                send_trace(row)
                for copy, plan, sent, hold in (
                        (to_left, leftward, sent_left, hold_left),
                        (to_right, rightward, sent_right, hold_right)):
                    if row in hold:
                        for block, q in plan[row][hold[row]:sent[row]]:
                            copy(block, q, row_panel.at[me, span(q)] if block == row
                                 else col_panel.at[block, span(q)]).start()
            hold_left.pop(row, None)
            hold_right.pop(row, None)

    pl.when(far_above > 0)(lambda: pl.semaphore_wait(ready.at[3], far_above))
    @pl.when(r == last)
    def _():
        sent_left[last] = pass_on(to_left, last, leftward[last], sent_left[last], ())
    pl.when(has_left)(lambda: pl.semaphore_wait(ready.at[2], 1))
    pl.when(has_right)(lambda: answer(2, (right, c, l)))
    side_wait(n_layer - 1, 0)
    pl.when(on_diagonal & (r == 0))(lambda: add_trace([], True))
    diagonals(ready_rows(0, ()))
    for k in range(CHUNKS // 2):
        z_arrive(k)
    for d in direct:
        plane_arrive(d, 0)
    for k in range(CHUNKS // 2, CHUNKS):
        z_arrive(k)
    if detour:
        detour_pass(1)
    for d in direct:
        plane_arrive(d, 1)
    for k in range(CHUNKS, CHUNKS + 1):
        z_arrive(k)
    for k in range(CHUNKS + 1, CHUNKS + 2):
        z_arrive(k)
    def sides(chosen):
        side_wait(len(chosen) * (n_layer - 1), 2 if chosen is relayed else 1)

    soon = ready_rows(CHUNKS + 2, direct)
    in_soon = functools.reduce(jnp.logical_or, [r == row for row in soon], r < 0)
    pl.when(in_soon)(lambda: sides(direct))
    diagonals(soon)
    for turn in range(2):
        for d in relayed:
            plane_arrive(d, turn)
    if detour:
        detour_pass(0)
    for k in range(CHUNKS + 2, middle):
        z_arrive(k)
    pl.when(jnp.logical_not(in_soon))(lambda: sides(direct))
    sides(relayed)
    diagonals(list(asked))

    total = None
    for t in range(per):
        term = jnp.dot(
            row_panel[r * per + t], row_panel[me, pl.ds(t * width, width), :],
            preferred_element_type=jnp.float32)
        total = term if total is None else total + term
    updated[...] = total
    inner = has_left & has_right
    for s in range(1, last):
        pl.when((r - s >= 0) & inner)(lambda: add(terms(r - s, 0, rows)))
        pl.when((r + s <= last) & inner)(lambda: add(terms(r + s, 0, rows)))
    for row, arrived in ((0, from_right[0]), (last, from_left[last])):
        @pl.when(r == row)
        def _():
            products = []
            for block in range(n_row):
                chunks = sorted(q for b, q in arrived[:middle] if b == block)
                if chunks:
                    assert chunks == list(range(len(chunks)))
                    products += terms(block, 0, len(chunks) * piece)
            add(products)

    def finish(row, arrived, k):
        block, q = arrived[k]
        if row == 0 and block in pairs[0]:
            @pl.when(on_diagonal)
            def _():
                add_trace(parts_of([(block, q)]), False)
                if (block, q) == (last, CHUNKS - 1):
                    send_first()
        if k < last * CHUNKS - 1:
            add(terms(block, q * piece, piece))
        else:
            update(terms(block, q * piece, piece))

    def update(products):
        for i in range(rows // blk):
            flag = jnp.full((blk, blk), branch_flag[i]) == 1
            for k in range(width // blk):
                at = (pl.ds(i * blk, blk), pl.ds(k * blk, blk))
                square = updated[at]
                for product in products:
                    square += product[i * blk:(i + 1) * blk, k * blk:(k + 1) * blk]
                doubled = 2.0 * row_panel[(me,) + at].astype(jnp.float32) - square
                kept = jnp.full((blk, blk), keep_mask[k, i].astype(jnp.float32))
                updated[at] = jnp.where(flag, square, doubled) * kept

    def parts_of(chunks):
        share = piece // blk
        return [(b, q * share + k) for b, q in chunks if b in pairs[0] for k in range(share)]

    pl.when(on_diagonal & (r == 0))(
        lambda: add_trace(parts_of(from_right[0][:middle]), False))
    for k in range(middle, last * CHUNKS):
        z_arrive(k, finish)

    pl.when(inner)(lambda: update([]))

    if detour:
        pl.when(by_way & (r < 2))(
            detour_copy(aside, aside, (0, c, l), aside_send, aside_sems.at[0]).wait_send)
    for row in range(n_row):
        @pl.when(r == row)
        def _():
            for copy, plan, sem in (
                    (to_left, leftward[row], left_send),
                    (to_right, rightward[row], right_send)):
                if plan:
                    blocks = pl.ds(0, len(plan) // CHUNKS)
                    pltpu.make_async_remote_copy(
                        src_ref=col_panel.at[blocks], dst_ref=col_panel.at[blocks],
                        send_sem=sem.at[0], recv_sem=z_recv.at[0, 0],
                        device_id=(left, c, l), device_id_type=MESH,
                    ).wait_send()

    def sent_slots(count, ref, sem):
        pltpu.make_async_remote_copy(
            src_ref=ref.at[pl.ds(0, count)], dst_ref=ref.at[pl.ds(0, count)],
            send_sem=sem.at[0], recv_sem=plane_recv.at[0, 0],
            device_id=(r, c, l), device_id_type=MESH,
        ).wait_send()

    sent_slots(n_col - 1, row_panel, plane_send)
    sent_slots((n_layer - 1) * n_col, row_panel, side_send)

    def heard(count):
        pltpu.make_async_remote_copy(
            src_ref=trace_in.at[pl.ds(0, count)], dst_ref=trace_in.at[pl.ds(0, count)],
            send_sem=trace_send.at[0], recv_sem=trace_recv.at[0],
            device_id=(r, c, l), device_id_type=MESH,
        ).wait_recv()

    pl.when(on_diagonal)(lambda: heard(slots - per + firsts - 1))
    pl.when(jnp.logical_not(on_diagonal))(lambda: heard(slots - per + firsts))
    giver = jnp.where(r == last, 0, l)
    parts = trace_in[giver]
    for slot in range(1, firsts):
        parts = parts + trace_in[slot * n_layer + giver]
    for slot in range(per, slots):
        parts = parts + trace_in[slot]
    lines[...] = parts
    pl.when(on_diagonal & has_left)(
        lambda: sent_slots(n_row * slots - 1, trace_in, trace_send))
    first_sent = last * n_col + n_layer - 2
    for core, count in ((l == 0, first_sent + n_col * n_layer), (l > 0, first_sent)):
        pl.when(on_diagonal & jnp.logical_not(has_left) & core)(
            functools.partial(sent_slots, count, trace_in, trace_send))


def deliver(updated, lines, out, trace):
    out[...] = updated[...]
    trace[0, 0] = jnp.sum(lines[0:1, :] + lines[1:2, :] * lines[2:3, :])


def on_device(sizes, density, block_mask, keep_mask, branch_flag):
    n_row, n_col, n_layer = sizes
    rows, width = density.shape
    blk = rows // block_mask.shape[0]
    dma = pltpu.SemaphoreType.DMA
    slots = n_col * n_layer
    vmem, smem = pl.BlockSpec(memory_space=pltpu.VMEM), pl.BlockSpec(memory_space=pltpu.SMEM)
    hbm = pl.BlockSpec(memory_space=pltpu.HBM)
    panel_bytes = 2 * rows * width * (slots + n_row + 1)
    updated, lines = pl.pallas_call(
        functools.partial(kernel, sizes),
        out_shape=(
            jax.ShapeDtypeStruct((rows, width), jnp.float32),
            jax.ShapeDtypeStruct((3, blk), jnp.float32),
        ),
        in_specs=[hbm, hbm, hbm, hbm],
        out_specs=(vmem, vmem),
        scratch_shapes=[
            pltpu.VMEM((rows, width), jnp.bfloat16),
            pltpu.SMEM(block_mask.T.shape, jnp.int32),
            pltpu.SMEM(keep_mask.T.shape, jnp.int32),
            pltpu.SMEM(branch_flag.shape, jnp.int32),
            pltpu.VMEM((slots, rows, width), jnp.bfloat16),
            pltpu.VMEM((n_row, rows, width), jnp.bfloat16),
            pltpu.VMEM((3, blk), jnp.float32),
            pltpu.VMEM((n_row * slots, 3, blk), jnp.float32),
            dma((CHUNKS + 3,)),
            dma((1,)),
            dma((max(n_col - 1, 1), 2)),
            dma((1,)),
            dma((3,)),
            dma((1,)),
            dma((1,)),
            dma((n_row, CHUNKS)),
            dma((1,)),
            dma((2,)),
            pltpu.VMEM((n_layer, 3, blk), jnp.float32),
            pltpu.VMEM((3, blk), jnp.float32),
            pltpu.VMEM((rows // CHUNKS // 2, width), jnp.bfloat16),
            dma((1,)),
            dma((1,)),
            pltpu.SemaphoreType.REGULAR((4,)),
        ],
        compiler_params=pltpu.CompilerParams(
            collective_id=0, has_side_effects=True,
            vmem_limit_bytes=panel_bytes + 8 * rows * width + (4 << 20)),
    )(*[
        pltpu.with_memory_space_constraint(x, pltpu.HBM)
        for x in (density, block_mask.T, keep_mask.T, branch_flag)
    ])
    updated, trace = pl.pallas_call(
        deliver,
        out_shape=(
            jax.ShapeDtypeStruct((rows, width), jnp.float32),
            jax.ShapeDtypeStruct((1, 1), jnp.float32),
        ),
        in_specs=[vmem, vmem],
        out_specs=(vmem, smem),
        compiler_params=pltpu.CompilerParams(
            vmem_limit_bytes=8 * rows * width + (4 << 20)),
    )(updated, lines)
    return updated, trace[0, 0]


def solution(mesh):
    sizes = tuple(mesh.shape[name] for name in ("row", "col", "layer"))
    in_specs = (
        P("row", ("col", "layer")),
        P("row", ("col", "layer")),
        P("row", ("col", "layer")),
        P("row"),
    )
    out_specs = (P("row", ("col", "layer")), P())
    return jax.shard_map(
        functools.partial(on_device, sizes), mesh=mesh, in_specs=in_specs,
        out_specs=out_specs, check_vma=False,
    )
```

```python
import functools

import jax
import jax.numpy as jnp
from jax import lax
from jax.experimental import pallas as pl
from jax.experimental.pallas import tpu as pltpu
from jax.sharding import PartitionSpec as P

MESH = pl.DeviceIdType.MESH
CHUNKS = 4
AHEAD = 2


def partner_of(index, step, size):
    if size & (size - 1):
        return (index + step) % size
    for bit in range(size.bit_length()):
        if step >> bit & 1:
            index = index + (1 - 2 * ((index // (1 << bit)) % 2)) * (1 << bit)
    return index


def passing_plans(n_row):
    last = n_row - 1
    blocks = [[(b, q) for q in range(CHUNKS)] for b in range(n_row)]
    rightward = [sum(blocks[row::-1], []) for row in range(last)] + [[]]
    leftward = [[]] + [sum(blocks[row:], []) for row in range(1, n_row)]
    for row in range(1, last):
        for order, block, count in ((rightward[row], 1, 2), (leftward[row], last - 1, 1)):
            for q in range(CHUNKS - count, CHUNKS):
                order.remove((block, q))
                order.append((block, q))
    leftward[1].remove((1, CHUNKS - 1))
    leftward[1].append((1, CHUNKS - 1))
    return rightward, leftward


def kernel(
    sizes, density_hbm, block_hbm, keep_hbm, flag_hbm, updated, lines,
    density, block_mask, keep_mask, branch_flag,
    row_panel, col_panel, trace_own, trace_in, local_sem,
    plane_send, plane_recv, side_recv, z_send, z_recv,
    trace_send, trace_recv, trace_swap, trace_sum, aside, aplane_send, aside_sems, ready,
):
    n_row, n_col, n_layer = sizes
    rows, width = density.shape
    blk = rows // block_mask.shape[1]
    per = rows // width
    piece = rows // CHUNKS
    slots = n_col * n_layer
    last = n_row - 1
    r, c, l = lax.axis_index("row"), lax.axis_index("col"), lax.axis_index("layer")
    me = c * n_layer + l
    has_left, has_right = r > 0, r < last
    left, right = jnp.maximum(r - 1, 0), jnp.minimum(r + 1, last)
    col_peers = [partner_of(c, d, n_col) for d in range(1, n_col)]
    layer_peers = [partner_of(l, d, n_layer) for d in range(1, n_layer)]

    bits = [d for d in range(1, n_col) if d & (d - 1) == 0]
    relayed = [lo | hi for hi in bits for lo in bits if lo < hi]
    if n_col & (n_col - 1):
        bits, relayed = list(range(1, n_col)), []
    direct = [d for d in range(1, n_col) if d not in relayed]
    halves = {d: (1, 0) if relayed and d > 1 else (0, 1) for d in range(1, n_col)}

    plane_peers = [(c, q, True, 1) for q in layer_peers]
    for d in range(1, n_col):
        p = col_peers[d - 1]
        met = (p * c == 0) if d in relayed and len(bits) == 2 else True
        plane_peers += [(p, q, met, 3 if d in relayed else 1) for q in range(n_layer)]

    def counted(which, above):
        return sum(jnp.where(((p * n_layer + q > me) == above) & met, 1, 0)
                   for p, q, met, to in plane_peers if to in which)

    def span(q):
        return pl.ds(q * piece, piece)

    def load(n, source, target):
        return pltpu.make_async_copy(source, target, local_sem.at[n])

    rest = pl.ds(piece, rows - piece)
    load_first = load(0, density_hbm.at[span(0)], density.at[span(0)])
    load_mask = load(1, block_hbm, block_mask)
    load_rest = load(2, density_hbm.at[rest], density.at[rest])
    load_keep, load_flag = load(0, keep_hbm, keep_mask), load(1, flag_hbm, branch_flag)
    for first in (load_first, load_mask, load_rest):
        first.start()

    barrier = pltpu.get_barrier_semaphore()

    def greet(target):
        pl.semaphore_signal(barrier, inc=1, device_id=target, device_id_type=MESH)

    def answer(which, target):
        pl.semaphore_signal(
            ready.at[which], inc=1, device_id=target, device_id_type=MESH)

    pl.when(has_right)(lambda: greet((right, c, l)))
    for p, q, met, _ in plane_peers:
        pl.when((p * n_layer + q > me) & met)(functools.partial(greet, (r, p, q)))
    below = jnp.where(has_left, 1, 0) + counted((1, 3), False)
    pl.when(below > 0)(lambda: pl.semaphore_wait(barrier, below))
    pl.when(has_left)(lambda: answer(0, (left, c, l)))
    for p, q, met, to in plane_peers:
        pl.when((p * n_layer + q < me) & met)(functools.partial(answer, to, (r, p, q)))
    def mask(q):
        if q == 1:
            load_rest.wait()
        for i in range(q * piece // blk, (q + 1) * piece // blk):
            for k in range(width // blk):
                at = (pl.ds(i * blk, blk), pl.ds(k * blk, blk))
                kept = jnp.full((blk, blk), block_mask[k, i].astype(jnp.float32))
                row_panel[(me,) + at] = density[at] * kept.astype(jnp.bfloat16)

    load_mask.wait()
    load_first.wait()
    load_keep.start()
    load_flag.start()

    def z_copy(block, q, source, target, sem, recv):
        return pltpu.make_async_remote_copy(
            src_ref=source, dst_ref=col_panel.at[block, span(q)],
            send_sem=sem.at[0], recv_sem=z_recv.at[recv, q],
            device_id=(target, c, l), device_id_type=MESH,
        )

    def to_right(block, q, source):
        return z_copy(block, q, source, right, z_send, block)

    def to_left(block, q, source):
        return z_copy(block, q, source, left, z_send, block - 1)

    def half_copy(slot, h, sem, recv, target):
        half = pl.ds(h * (rows // 2), rows // 2)
        return pltpu.make_async_remote_copy(
            src_ref=row_panel.at[slot, half], dst_ref=row_panel.at[slot, half],
            send_sem=sem.at[0], recv_sem=recv, device_id=target, device_id_type=MESH,
        )

    def plane_copy(slot, h, d, peer):
        return half_copy(slot, h, plane_send, plane_recv.at[d - 1, h], (r, peer, l))

    def side_copies(slot, h, group):
        for other in layer_peers:
            half_copy(slot, h, plane_send, side_recv.at[group], (r, c, other)).start()

    def side_wait(count, group):
        blocks = row_panel.at[pl.ds(0, count)]
        if count:
            pltpu.make_async_remote_copy(
                src_ref=blocks, dst_ref=blocks, send_sem=plane_send.at[0],
                recv_sem=side_recv.at[group], device_id=(r, c, l), device_id_type=MESH,
            ).wait_recv()

    def seen(d):
        return n_col - d if n_col & (n_col - 1) else d

    def plane_start(chosen):
        for turn in range(2):
            for d in direct:
                peer = col_peers[d - 1]
                pl.when(chosen(peer))(
                    lambda: plane_copy(me, halves[d][turn], seen(d), peer).start())

    def plane_arrive(d, turn):
        peer, h = col_peers[d - 1], halves[d][turn]
        slot = peer * n_layer + l
        plane_copy(slot, h, d, peer).wait_recv()
        for other in bits if relayed and d in bits else []:
            if (other > d) == (h == 0) and other != d:
                plane_copy(slot, h, d | other, col_peers[other - 1]).start()
        side_copies(slot, h, 2 if d in relayed else 1)

    rightward, leftward = passing_plans(n_row)
    from_left = [[]] + rightward[:-1]
    from_right = leftward[1:] + [[]]

    on_diagonal = me // per == r

    detour = bool(relayed)
    ways = [(c == d) & (l == n_layer - 1) for d in bits[:2]] if detour else []
    by_way = functools.reduce(jnp.logical_or, ways, c < 0)

    def part_of(h):
        return pl.ds((CHUNKS - 1) * piece + h * (piece // 2), piece // 2)

    def detour_copy(source, target, device, sem, recv):
        return pltpu.make_async_remote_copy(
            src_ref=source, dst_ref=target, send_sem=sem.at[0], recv_sem=recv,
            device_id=device, device_id_type=MESH,
        )

    def detour_start():
        for h, d in enumerate(bits[:2]):
            pl.when((r == 1) & (me == n_layer - 1))(detour_copy(
                row_panel.at[me, part_of(h)], aside, (1, d, n_layer - 1),
                z_send, aside_sems.at[0]).start)

    def detour_pass(row):
        @pl.when(by_way & (r == row))
        def _():
            detour_copy(aside, aside, (0, c, l), aplane_send, aside_sems.at[0]).wait_recv()
            if row:
                detour_copy(aside, aside, (0, c, l), aplane_send, aside_sems.at[0]).start()

        for h, way in enumerate(ways if row == 0 else []):
            pl.when(way & (r == row))(detour_copy(
                aside, col_panel.at[1, part_of(h)], (0, 0, n_layer - 1),
                aplane_send, z_recv.at[0, CHUNKS - 1]).start)

    def pass_on(copy, row, plan, first, arrived, stop=None, hold=None):
        while first < len(plan) and (stop is None or first < stop):
            block, q = plan[first]
            if block == row:
                source = row_panel.at[me, span(q)]
            elif (block, q) in arrived:
                source = col_panel.at[block, span(q)]
            else:
                break
            if detour and copy is to_left and (row, block, q) == (1, 1, CHUNKS - 1):
                pl.when(jnp.logical_not(on_diagonal) & (me != n_layer - 1))(
                    functools.partial(lambda f: f.start(), copy(block, q, source)))
            elif hold is None or first < hold:
                copy(block, q, source).start()
            else:
                pl.when(jnp.logical_not(on_diagonal))(
                    functools.partial(lambda f: f.start(), copy(block, q, source)))
            first += 1
        return first

    sent_left, sent_right = [0] * n_row, [0] * n_row
    hold_left, hold_right = {1: last * CHUNKS - 2}, {last - 1: 2 * CHUNKS - 1}
    for q in range(CHUNKS):
        mask(q)
        for row in range(1, n_row) if q < AHEAD else []:
            @pl.when(r == row)
            def _():
                sent_left[row] = pass_on(
                    to_left, row, leftward[row], sent_left[row], (), q + 1)
    plane_start(lambda peer: peer < c)
    pl.when(has_right)(lambda: pl.semaphore_wait(ready.at[0], 1))
    for row in range(last):
        @pl.when(r == row)
        def _():
            sent_right[row] = pass_on(to_right, row, rightward[row], 0, (), AHEAD)
    near_above, far_above = counted((1,), True), counted((3,), True)
    pl.when(near_above > 0)(lambda: pl.semaphore_wait(ready.at[1], near_above))
    for row in range(n_row):
        @pl.when(r == row)
        def _():
            sent_left[row] = pass_on(
                to_left, row, leftward[row], sent_left[row], (),
                CHUNKS - 1 if row == last else None, hold_left.get(row))
            sent_right[row] = pass_on(
                to_right, row, rightward[row], sent_right[row], (), None, hold_right.get(row))
    if detour:
        detour_start()
    plane_start(lambda peer: peer > c)
    for h in range(2):
        side_copies(me, h, 0)

    def z_arrive(k, then=None):
        for row in range(n_row):
            if k < max(len(from_right[row]), len(from_left[row])):
                @pl.when(r == row)
                def _():
                    if k < len(from_right[row]):
                        block, q = from_right[row][k]
                        to_left(block, q, col_panel.at[block, span(q)]).wait_recv()
                        sent_left[row] = pass_on(
                            to_left, row, leftward[row], sent_left[row],
                            from_right[row][:k + 1], None, hold_left.get(row))
                        if then:
                            then(row, from_right[row], k)
                    if k < len(from_left[row]):
                        block, q = from_left[row][k]
                        to_right(block, q, col_panel.at[block, span(q)]).wait_recv()
                        sent_right[row] = pass_on(
                            to_right, row, rightward[row], sent_right[row],
                            from_left[row][:k + 1], None, hold_right.get(row))
                        if then:
                            then(row, from_left[row], k)

    def terms(block, start, size):
        out = []
        while size:
            step = min(size, width - start % width)
            out.append(jnp.dot(
                row_panel[block * per + start // width, :, pl.ds(start % width, step)],
                col_panel[block, pl.ds(start, step), :],
                preferred_element_type=jnp.float32))
            start, size = start + step, size - step
        return out

    def add(products):
        total = products[0]
        for product in products[1:]:
            total = total + product
        updated[...] += total

    corner = pl.multiple_of((me % per) * width, width)
    tiles = width // blk
    lanes = lax.broadcasted_iota(jnp.int32, (1, blk), 1)
    eye = (lax.broadcasted_iota(jnp.int32, (blk, blk), 0)
           == lax.broadcasted_iota(jnp.int32, (blk, blk), 1))

    def weight(t, if_square, otherwise):
        kept = keep_mask[t, (me % per) * tiles + t]
        chosen = jnp.where(branch_flag[(me % per) * tiles + t] == 1, if_square, otherwise)
        return (kept * chosen).astype(jnp.float32)

    def pair_sums(block, k):
        slot = block * per + k * blk // width
        out = []
        for t in range(tiles):
            ours = row_panel[slot, pl.ds(corner + t * blk, blk), pl.ds(k * blk % width, blk)]
            if block is r:
                theirs = row_panel[me, pl.ds(k * blk, blk), pl.ds(t * blk, blk)]
            else:
                theirs = col_panel[block, pl.ds(k * blk, blk), pl.ds(t * blk, blk)]
            product = jnp.dot(ours, theirs, preferred_element_type=jnp.float32)
            out.append(jnp.sum(jnp.where(eye, product, 0.0), axis=0, keepdims=True))
        return out

    def trace_copy(z, col, layer):
        return pltpu.make_async_remote_copy(
            src_ref=trace_own, dst_ref=trace_in.at[me],
            send_sem=trace_send.at[0], recv_sem=trace_recv.at[0],
            device_id=(z, col, layer), device_id_type=MESH,
        )

    assert per % n_layer == 0
    firsts = per // n_layer

    def swap_copy(other):
        return pltpu.make_async_remote_copy(
            src_ref=trace_own, dst_ref=trace_swap.at[l],
            send_sem=trace_send.at[0], recv_sem=trace_recv.at[1],
            device_id=(r, c, other), device_id_type=MESH,
        )

    def sum_copy(z, col, layer):
        return pltpu.make_async_remote_copy(
            src_ref=trace_sum, dst_ref=trace_in.at[me],
            send_sem=trace_send.at[0], recv_sem=trace_recv.at[0],
            device_id=(z, col, layer), device_id_type=MESH,
        )

    def send_first():
        trace_swap[l] = trace_own[...]
        for other in layer_peers:
            swap_copy(other).start()
        if n_layer > 1:
            pltpu.make_async_remote_copy(
                src_ref=trace_in.at[pl.ds(0, n_layer - 1)],
                dst_ref=trace_in.at[pl.ds(0, n_layer - 1)],
                send_sem=trace_send.at[0], recv_sem=trace_recv.at[1],
                device_id=(r, c, l), device_id_type=MESH,
            ).wait_recv()
        total = trace_swap[0]
        for layer in range(1, n_layer):
            total = total + trace_swap[layer]
        trace_sum[...] = total
        trace_in[me] = total
        @pl.when(l == 0)
        def _():
            for col in range(n_col):
                for layer in range(n_layer):
                    sum_copy(last, col, layer).start()

        for z in range(last - 1, -1, -1):
            for col in range(n_col):
                if z:
                    sum_copy(z, col, l).start()
                else:
                    pl.when(col != c)(lambda: sum_copy(z, col, l).start())

    everyone = [(z, col, layer) for z in range(n_row) for col in range(n_col)
                for layer in range(n_layer)]

    def add_trace(chunks, start):
        weights = [weight(t, 1, -1) for t in range(tiles)]
        part = spread = others = jnp.zeros((1, blk), jnp.float32)
        if not start:
            part, spread, others = (trace_own[n:n + 1, :] for n in range(3))
        for t in range(tiles if start else 0):
            own = row_panel[me, pl.ds(corner + t * blk, blk), pl.ds(t * blk, blk)]
            line = jnp.sum(
                jnp.where(eye, own.astype(jnp.float32), 0.0), axis=0, keepdims=True)
            part += weight(t, 0, 2) * line
            spread += jnp.where(lanes == me * tiles + t, weights[t], 0.0)
        every = range(rows // blk)
        for block, k in ([(r, k) for k in every] if start else []) + chunks:
            sums = pair_sums(block, k)
            for t in range(tiles):
                part += weights[t] * sums[t]
            if block is not r:
                here = block * (rows // blk) + k
                total = sum(jnp.sum(line, keepdims=True) for line in sums)
                others += jnp.where(lanes == here, total, 0.0)
        trace_own[0:1, :] = part
        trace_own[1:2, :] = spread
        trace_own[2:3, :] = others

    def send_trace(row):
        trace_in[me] = trace_own[...]
        for z, col, layer in everyone:
            if z != row:
                trace_copy(z, col, layer).start()
            else:
                pl.when((col != c) | (layer != l))(
                    lambda: trace_copy(z, col, layer).start())

    middle = (last - 1) * CHUNKS
    pairs = {row: [0] + list(range(row + 1, n_row)) for row in range(1, last)}
    pairs.update({0: [last], last: []})
    asked = list(range(1, n_row))

    def ready_rows(count, distances):
        def at_hand(b, row):
            arrived = (from_left if b < row else from_right)[row][:count]
            apart = (b * per // n_layer) ^ (row * per // n_layer)
            return ([x for x, _ in arrived].count(b) == CHUNKS
                    and (apart in distances or not relayed))

        return [row for row in asked if all(at_hand(b, row) for b in pairs[row])]

    def diagonals(chosen):
        for row in chosen:
            asked.remove(row)

            @pl.when(on_diagonal & (r == row))
            def _():
                add_trace([(b, k) for b in pairs[row] for k in range(rows // blk)], True)
                send_trace(row)
                for copy, plan, sent, hold in (
                        (to_left, leftward, sent_left, hold_left),
                        (to_right, rightward, sent_right, hold_right)):
                    if row in hold:
                        for block, q in plan[row][hold[row]:sent[row]]:
                            copy(block, q, row_panel.at[me, span(q)] if block == row
                                 else col_panel.at[block, span(q)]).start()
            hold_left.pop(row, None)
            hold_right.pop(row, None)

    load_keep.wait()
    load_flag.wait()
    pl.when(far_above > 0)(lambda: pl.semaphore_wait(ready.at[3], far_above))
    @pl.when(r == last)
    def _():
        sent_left[last] = pass_on(to_left, last, leftward[last], sent_left[last], ())
    pl.when(has_left)(lambda: pl.semaphore_wait(ready.at[2], 1))
    pl.when(has_right)(lambda: answer(2, (right, c, l)))
    side_wait(n_layer - 1, 0)
    pl.when(on_diagonal & (r == 0))(lambda: add_trace([], True))
    diagonals(ready_rows(0, ()))
    for k in range(CHUNKS // 2):
        z_arrive(k)
    for d in direct:
        plane_arrive(d, 0)
    for k in range(CHUNKS // 2, CHUNKS):
        z_arrive(k)
    if detour:
        detour_pass(1)
    for d in direct:
        plane_arrive(d, 1)
    for k in range(CHUNKS, CHUNKS + 1):
        z_arrive(k)
    for k in range(CHUNKS + 1, CHUNKS + 2):
        z_arrive(k)
    def sides(chosen):
        side_wait(len(chosen) * (n_layer - 1), 2 if chosen is relayed else 1)

    soon = ready_rows(CHUNKS + 2, direct)
    in_soon = functools.reduce(jnp.logical_or, [r == row for row in soon], r < 0)
    pl.when(in_soon)(lambda: sides(direct))
    diagonals(soon)
    for turn in range(2):
        for d in relayed:
            plane_arrive(d, turn)
    if detour:
        detour_pass(0)
    for k in range(CHUNKS + 2, middle):
        z_arrive(k)
    pl.when(jnp.logical_not(in_soon))(lambda: sides(direct))
    sides(relayed)
    diagonals(list(asked))

    total = None
    for t in range(per):
        term = jnp.dot(
            row_panel[r * per + t], row_panel[me, pl.ds(t * width, width), :],
            preferred_element_type=jnp.float32)
        total = term if total is None else total + term
    updated[...] = total
    inner = has_left & has_right
    for s in range(1, last):
        pl.when((r - s >= 0) & inner)(lambda: add(terms(r - s, 0, rows)))
        pl.when((r + s <= last) & inner)(lambda: add(terms(r + s, 0, rows)))
    for row, arrived in ((0, from_right[0]), (last, from_left[last])):
        @pl.when(r == row)
        def _():
            products = []
            for block in range(n_row):
                chunks = sorted(q for b, q in arrived[:middle] if b == block)
                if chunks:
                    assert chunks == list(range(len(chunks)))
                    products += terms(block, 0, len(chunks) * piece)
            add(products)

    def finish(row, arrived, k):
        block, q = arrived[k]
        if row == 0 and block in pairs[0]:
            @pl.when(on_diagonal)
            def _():
                add_trace(parts_of([(block, q)]), False)
                if (block, q) == (last, CHUNKS - 1):
                    send_first()
        if k < last * CHUNKS - 1:
            add(terms(block, q * piece, piece))
        else:
            update(terms(block, q * piece, piece))

    def update(products):
        for i in range(rows // blk):
            flag = jnp.full((blk, blk), branch_flag[i]) == 1
            for k in range(width // blk):
                at = (pl.ds(i * blk, blk), pl.ds(k * blk, blk))
                square = updated[at]
                for product in products:
                    square += product[i * blk:(i + 1) * blk, k * blk:(k + 1) * blk]
                doubled = 2.0 * row_panel[(me,) + at].astype(jnp.float32) - square
                kept = jnp.full((blk, blk), keep_mask[k, i].astype(jnp.float32))
                updated[at] = jnp.where(flag, square, doubled) * kept

    def parts_of(chunks):
        share = piece // blk
        return [(b, q * share + k) for b, q in chunks if b in pairs[0] for k in range(share)]

    pl.when(on_diagonal & (r == 0))(
        lambda: add_trace(parts_of(from_right[0][:middle]), False))
    for k in range(middle, last * CHUNKS):
        z_arrive(k, finish)

    pl.when(inner)(lambda: update([]))

    if detour:
        pl.when(by_way & (r < 2))(
            detour_copy(aside, aside, (0, c, l), aplane_send, aside_sems.at[0]).wait_send)
    for row in range(n_row):
        blocks = pl.ds(0, (len(leftward[row]) + len(rightward[row])) // CHUNKS)
        pl.when(r == row)(pltpu.make_async_remote_copy(
            src_ref=row_panel.at[blocks], dst_ref=row_panel.at[blocks],
            send_sem=z_send.at[0], recv_sem=z_recv.at[0, 0],
            device_id=(left, c, l), device_id_type=MESH,
        ).wait_send)

    def sent_slots(count, ref, sem):
        pltpu.make_async_remote_copy(
            src_ref=ref.at[pl.ds(0, count)], dst_ref=ref.at[pl.ds(0, count)],
            send_sem=sem.at[0], recv_sem=plane_recv.at[0, 0],
            device_id=(r, c, l), device_id_type=MESH,
        ).wait_send()

    sent_slots(n_layer * n_col - 1, row_panel, plane_send)

    def heard(count):
        pltpu.make_async_remote_copy(
            src_ref=trace_in.at[pl.ds(0, count)], dst_ref=trace_in.at[pl.ds(0, count)],
            send_sem=trace_send.at[0], recv_sem=trace_recv.at[0],
            device_id=(r, c, l), device_id_type=MESH,
        ).wait_recv()

    pl.when(on_diagonal)(lambda: heard(slots - per + firsts - 1))
    pl.when(jnp.logical_not(on_diagonal))(lambda: heard(slots - per + firsts))
    giver = jnp.where(r == last, 0, l)
    parts = trace_in[giver]
    for slot in range(1, firsts):
        parts = parts + trace_in[slot * n_layer + giver]
    for slot in range(per, slots):
        parts = parts + trace_in[slot]
    lines[...] = parts
    pl.when(on_diagonal & has_left)(
        lambda: sent_slots(n_row * slots - 1, trace_in, trace_send))
    first_sent = last * n_col + n_layer - 2
    for core, count in ((l == 0, first_sent + n_col * n_layer), (l > 0, first_sent)):
        pl.when(on_diagonal & jnp.logical_not(has_left) & core)(
            functools.partial(sent_slots, count, trace_in, trace_send))


def deliver(updated, lines, out, trace):
    out[...] = updated[...]
    trace[0, 0] = jnp.sum(lines[0:1, :] + lines[1:2, :] * lines[2:3, :])


def on_device(sizes, density, block_mask, keep_mask, branch_flag):
    n_row, n_col, n_layer = sizes
    rows, width = density.shape
    blk = rows // block_mask.shape[0]
    dma = pltpu.SemaphoreType.DMA
    slots = n_col * n_layer
    vmem, smem = pl.BlockSpec(memory_space=pltpu.VMEM), pl.BlockSpec(memory_space=pltpu.SMEM)
    hbm = pl.BlockSpec(memory_space=pltpu.HBM)
    panel_bytes = 2 * rows * width * (slots + n_row + 1)
    updated, lines = pl.pallas_call(
        functools.partial(kernel, sizes),
        out_shape=(
            jax.ShapeDtypeStruct((rows, width), jnp.float32),
            jax.ShapeDtypeStruct((3, blk), jnp.float32),
        ),
        in_specs=[hbm, hbm, hbm, hbm],
        out_specs=(vmem, vmem),
        scratch_shapes=[
            pltpu.VMEM((rows, width), jnp.bfloat16),
            pltpu.SMEM(block_mask.T.shape, jnp.int32),
            pltpu.SMEM(keep_mask.T.shape, jnp.int32),
            pltpu.SMEM(branch_flag.shape, jnp.int32),
            pltpu.VMEM((slots, rows, width), jnp.bfloat16),
            pltpu.VMEM((n_row, rows, width), jnp.bfloat16),
            pltpu.VMEM((3, blk), jnp.float32),
            pltpu.VMEM((n_row * slots, 3, blk), jnp.float32),
            dma((3,)),
            dma((1,)),
            dma((max(n_col - 1, 1), 2)),
            dma((3,)),
            dma((1,)),
            dma((n_row - 1, CHUNKS)),
            dma((1,)),
            dma((2,)),
            pltpu.VMEM((n_layer, 3, blk), jnp.float32),
            pltpu.VMEM((3, blk), jnp.float32),
            pltpu.VMEM((rows // CHUNKS // 2, width), jnp.bfloat16),
            dma((1,)),
            dma((1,)),
            pltpu.SemaphoreType.REGULAR((4,)),
        ],
        compiler_params=pltpu.CompilerParams(
            collective_id=0, has_side_effects=True,
            vmem_limit_bytes=panel_bytes + 8 * rows * width + (4 << 20)),
    )(*[
        pltpu.with_memory_space_constraint(x, pltpu.HBM)
        for x in (density, block_mask.T, keep_mask.T, branch_flag)
    ])
    updated, trace = pl.pallas_call(
        deliver,
        out_shape=(
            jax.ShapeDtypeStruct((rows, width), jnp.float32),
            jax.ShapeDtypeStruct((1, 1), jnp.float32),
        ),
        in_specs=[vmem, vmem],
        out_specs=(vmem, smem),
        compiler_params=pltpu.CompilerParams(
            vmem_limit_bytes=8 * rows * width + (4 << 20)),
    )(updated, lines)
    return updated, trace[0, 0]


def solution(mesh):
    sizes = tuple(mesh.shape[name] for name in ("row", "col", "layer"))
    in_specs = (
        P("row", ("col", "layer")),
        P("row", ("col", "layer")),
        P("row", ("col", "layer")),
        P("row"),
    )
    out_specs = (P("row", ("col", "layer")), P())
    return jax.shard_map(
        functools.partial(on_device, sizes), mesh=mesh, in_specs=in_specs,
        out_specs=out_specs, check_vma=False,
    )
```

```python
import functools

import jax
import jax.numpy as jnp
from jax import lax
from jax.experimental import pallas as pl
from jax.experimental.pallas import tpu as pltpu
from jax.sharding import PartitionSpec as P

MESH = pl.DeviceIdType.MESH
CHUNKS = 4
AHEAD = 2


def partner_of(index, step, size):
    if size & (size - 1):
        return (index + step) % size
    for bit in range(size.bit_length()):
        if step >> bit & 1:
            index = index + (1 - 2 * ((index // (1 << bit)) % 2)) * (1 << bit)
    return index


def passing_plans(n_row):
    last = n_row - 1
    blocks = [[(b, q) for q in range(CHUNKS)] for b in range(n_row)]
    rightward = [sum(blocks[row::-1], []) for row in range(last)] + [[]]
    leftward = [[]] + [sum(blocks[row:], []) for row in range(1, n_row)]
    for row in range(1, last):
        for order, block, count in ((rightward[row], 1, 2), (leftward[row], last - 1, 1)):
            for q in range(CHUNKS - count, CHUNKS):
                order.remove((block, q))
                order.append((block, q))
    leftward[1].remove((1, CHUNKS - 1))
    leftward[1].append((1, CHUNKS - 1))
    return rightward, leftward


def kernel(
    sizes, density_hbm, block_hbm, keep_hbm, flag_hbm, updated, lines,
    density, block_mask, keep_mask, branch_flag,
    row_panel, col_panel, trace_own, trace_in, local_sem,
    plane_send, plane_recv, side_recv, z_send, z_recv,
    trace_send, trace_recv, trace_swap, trace_sum, aside, aplane_send, aside_sems, ready,
):
    n_row, n_col, n_layer = sizes
    rows, width = density.shape
    blk = rows // block_mask.shape[1]
    per = rows // width
    piece = rows // CHUNKS
    slots = n_col * n_layer
    last = n_row - 1
    r, c, l = lax.axis_index("row"), lax.axis_index("col"), lax.axis_index("layer")
    me = c * n_layer + l
    has_left, has_right = r > 0, r < last
    left, right = jnp.maximum(r - 1, 0), jnp.minimum(r + 1, last)
    col_peers = [partner_of(c, d, n_col) for d in range(1, n_col)]
    layer_peers = [partner_of(l, d, n_layer) for d in range(1, n_layer)]

    bits = [d for d in range(1, n_col) if d & (d - 1) == 0]
    relayed = [lo | hi for hi in bits for lo in bits if lo < hi]
    if n_col & (n_col - 1):
        bits, relayed = list(range(1, n_col)), []
    direct = [d for d in range(1, n_col) if d not in relayed]
    halves = {d: (1, 0) if relayed and d > 1 else (0, 1) for d in range(1, n_col)}

    plane_peers = [(c, q, True, 1) for q in layer_peers]
    for d in range(1, n_col):
        p = col_peers[d - 1]
        met = (p * c == 0) if d in relayed and len(bits) == 2 else True
        plane_peers += [(p, q, met, 3 if d in relayed else 1) for q in range(n_layer)]

    def counted(which, above):
        return sum(jnp.where(((p * n_layer + q > me) == above) & met, 1, 0)
                   for p, q, met, to in plane_peers if to in which)

    def span(q):
        return pl.ds(q * piece, piece)

    def load(n, source, target):
        return pltpu.make_async_copy(source, target, local_sem.at[n])

    rest = pl.ds(piece, rows - piece)
    load_first = load(0, density_hbm.at[span(0)], density.at[span(0)])
    load_mask = load(1, block_hbm, block_mask)
    load_rest = load(2, density_hbm.at[rest], density.at[rest])
    load_keep, load_flag = load(0, keep_hbm, keep_mask), load(1, flag_hbm, branch_flag)
    for first in (load_first, load_mask, load_rest):
        first.start()

    barrier = pltpu.get_barrier_semaphore()

    def greet(target):
        pl.semaphore_signal(barrier, inc=1, device_id=target, device_id_type=MESH)

    def answer(which, target):
        pl.semaphore_signal(
            ready.at[which], inc=1, device_id=target, device_id_type=MESH)

    pl.when(has_right)(lambda: greet((right, c, l)))
    for p, q, met, _ in plane_peers:
        pl.when((p * n_layer + q > me) & met)(functools.partial(greet, (r, p, q)))
    below = jnp.where(has_left, 1, 0) + counted((1, 3), False)
    pl.when(below > 0)(lambda: pl.semaphore_wait(barrier, below))
    pl.when(has_left)(lambda: answer(0, (left, c, l)))
    for p, q, met, to in plane_peers:
        pl.when((p * n_layer + q < me) & met)(functools.partial(answer, to, (r, p, q)))
    def mask(q):
        if q == 1:
            load_rest.wait()
        for i in range(q * piece // blk, (q + 1) * piece // blk):
            for k in range(width // blk):
                at = (pl.ds(i * blk, blk), pl.ds(k * blk, blk))
                kept = jnp.full((blk, blk), block_mask[k, i].astype(jnp.float32))
                row_panel[(me,) + at] = density[at] * kept.astype(jnp.bfloat16)

    load_mask.wait()
    load_first.wait()
    load_keep.start()
    load_flag.start()

    def z_copy(block, q, source, target, sem, recv):
        return pltpu.make_async_remote_copy(
            src_ref=source, dst_ref=col_panel.at[block, span(q)],
            send_sem=sem.at[0], recv_sem=z_recv.at[recv, q],
            device_id=(target, c, l), device_id_type=MESH,
        )

    def to_right(block, q, source):
        return z_copy(block, q, source, right, z_send, block)

    def to_left(block, q, source):
        return z_copy(block, q, source, left, z_send, block - 1)

    def half_copy(slot, h, sem, recv, target):
        half = pl.ds(h * (rows // 2), rows // 2)
        return pltpu.make_async_remote_copy(
            src_ref=row_panel.at[slot, half], dst_ref=row_panel.at[slot, half],
            send_sem=sem.at[0], recv_sem=recv, device_id=target, device_id_type=MESH,
        )

    def plane_copy(slot, h, d, peer):
        return half_copy(slot, h, plane_send, plane_recv.at[d - 1, h], (r, peer, l))

    def side_copies(slot, h, group):
        for other in layer_peers:
            half_copy(slot, h, plane_send, side_recv.at[group], (r, c, other)).start()

    def side_wait(count, group):
        blocks = row_panel.at[pl.ds(0, count)]
        if count:
            pltpu.make_async_remote_copy(
                src_ref=blocks, dst_ref=blocks, send_sem=plane_send.at[0],
                recv_sem=side_recv.at[group], device_id=(r, c, l), device_id_type=MESH,
            ).wait_recv()

    def seen(d):
        return n_col - d if n_col & (n_col - 1) else d

    def plane_start(chosen):
        for turn in range(2):
            for d in direct:
                peer = col_peers[d - 1]
                pl.when(chosen(peer))(
                    lambda: plane_copy(me, halves[d][turn], seen(d), peer).start())

    def plane_arrive(d, turn):
        peer, h = col_peers[d - 1], halves[d][turn]
        slot = peer * n_layer + l
        plane_copy(slot, h, d, peer).wait_recv()
        for other in bits if relayed and d in bits else []:
            if (other > d) == (h == 0) and other != d:
                plane_copy(slot, h, d | other, col_peers[other - 1]).start()
        side_copies(slot, h, 2 if d in relayed else 1)

    rightward, leftward = passing_plans(n_row)
    from_left = [[]] + rightward[:-1]
    from_right = leftward[1:] + [[]]

    on_diagonal = me // per == r

    detour = bool(relayed)
    ways = [(c == d) & (l == n_layer - 1) for d in bits[:2]] if detour else []
    by_way = functools.reduce(jnp.logical_or, ways, c < 0)

    def part_of(h):
        return pl.ds((CHUNKS - 1) * piece + h * (piece // 2), piece // 2)

    def detour_copy(source, target, device, sem, recv):
        return pltpu.make_async_remote_copy(
            src_ref=source, dst_ref=target, send_sem=sem.at[0], recv_sem=recv,
            device_id=device, device_id_type=MESH,
        )

    def detour_start():
        for h, d in enumerate(bits[:2]):
            pl.when((r == 1) & (me == n_layer - 1))(detour_copy(
                row_panel.at[me, part_of(h)], aside, (1, d, n_layer - 1),
                z_send, aside_sems.at[0]).start)

    def detour_pass(row):
        @pl.when(by_way & (r == row))
        def _():
            detour_copy(aside, aside, (0, c, l), aplane_send, aside_sems.at[0]).wait_recv()
            if row:
                detour_copy(aside, aside, (0, c, l), aplane_send, aside_sems.at[0]).start()

        for h, way in enumerate(ways if row == 0 else []):
            pl.when(way & (r == row))(detour_copy(
                aside, col_panel.at[1, part_of(h)], (0, 0, n_layer - 1),
                aplane_send, z_recv.at[0, CHUNKS - 1]).start)

    def pass_on(copy, row, plan, first, arrived, stop=None, hold=None):
        while first < len(plan) and (stop is None or first < stop):
            block, q = plan[first]
            if block == row:
                source = row_panel.at[me, span(q)]
            elif (block, q) in arrived:
                source = col_panel.at[block, span(q)]
            else:
                break
            if detour and copy is to_left and (row, block, q) == (1, 1, CHUNKS - 1):
                pl.when(jnp.logical_not(on_diagonal) & (me != n_layer - 1))(
                    functools.partial(lambda f: f.start(), copy(block, q, source)))
            elif hold is None or first < hold:
                copy(block, q, source).start()
            else:
                pl.when(jnp.logical_not(on_diagonal))(
                    functools.partial(lambda f: f.start(), copy(block, q, source)))
            first += 1
        return first

    sent_left, sent_right = [0] * n_row, [0] * n_row
    hold_left, hold_right = {1: last * CHUNKS - 2}, {last - 1: 2 * CHUNKS}
    for q in range(CHUNKS):
        mask(q)
        for row in range(1, n_row) if q < AHEAD else []:
            @pl.when(r == row)
            def _():
                sent_left[row] = pass_on(
                    to_left, row, leftward[row], sent_left[row], (), q + 1)
    plane_start(lambda peer: peer < c)
    pl.when(has_right)(lambda: pl.semaphore_wait(ready.at[0], 1))
    for row in range(last):
        @pl.when(r == row)
        def _():
            sent_right[row] = pass_on(to_right, row, rightward[row], 0, (), AHEAD)
    near_above, far_above = counted((1,), True), counted((3,), True)
    pl.when(near_above > 0)(lambda: pl.semaphore_wait(ready.at[1], near_above))
    for row in range(n_row):
        @pl.when(r == row)
        def _():
            sent_left[row] = pass_on(
                to_left, row, leftward[row], sent_left[row], (),
                CHUNKS - 1 if row == last else None, hold_left.get(row))
            sent_right[row] = pass_on(
                to_right, row, rightward[row], sent_right[row], (), None, hold_right.get(row))
    if detour:
        detour_start()
    plane_start(lambda peer: peer > c)
    for h in range(2):
        side_copies(me, h, 0)

    def z_arrive(k, then=None):
        for row in range(n_row):
            if k < max(len(from_right[row]), len(from_left[row])):
                @pl.when(r == row)
                def _():
                    if k < len(from_right[row]):
                        block, q = from_right[row][k]
                        to_left(block, q, col_panel.at[block, span(q)]).wait_recv()
                        sent_left[row] = pass_on(
                            to_left, row, leftward[row], sent_left[row],
                            from_right[row][:k + 1], None, hold_left.get(row))
                        if then:
                            then(row, from_right[row], k)
                    if k < len(from_left[row]):
                        block, q = from_left[row][k]
                        to_right(block, q, col_panel.at[block, span(q)]).wait_recv()
                        sent_right[row] = pass_on(
                            to_right, row, rightward[row], sent_right[row],
                            from_left[row][:k + 1], None, hold_right.get(row))
                        if then:
                            then(row, from_left[row], k)

    def terms(block, start, size):
        out = []
        while size:
            step = min(size, width - start % width)
            out.append(jnp.dot(
                row_panel[block * per + start // width, :, pl.ds(start % width, step)],
                col_panel[block, pl.ds(start, step), :],
                preferred_element_type=jnp.float32))
            start, size = start + step, size - step
        return out

    def add(products):
        total = products[0]
        for product in products[1:]:
            total = total + product
        updated[...] += total

    corner = pl.multiple_of((me % per) * width, width)
    tiles = width // blk
    lanes = lax.broadcasted_iota(jnp.int32, (1, blk), 1)
    eye = (lax.broadcasted_iota(jnp.int32, (blk, blk), 0)
           == lax.broadcasted_iota(jnp.int32, (blk, blk), 1))

    def weight(t, if_square, otherwise):
        kept = keep_mask[t, (me % per) * tiles + t]
        chosen = jnp.where(branch_flag[(me % per) * tiles + t] == 1, if_square, otherwise)
        return (kept * chosen).astype(jnp.float32)

    def pair_sums(block, k):
        slot = block * per + k * blk // width
        out = []
        for t in range(tiles):
            ours = row_panel[slot, pl.ds(corner + t * blk, blk), pl.ds(k * blk % width, blk)]
            if block is r:
                theirs = row_panel[me, pl.ds(k * blk, blk), pl.ds(t * blk, blk)]
            else:
                theirs = col_panel[block, pl.ds(k * blk, blk), pl.ds(t * blk, blk)]
            product = jnp.dot(ours, theirs, preferred_element_type=jnp.float32)
            out.append(jnp.sum(jnp.where(eye, product, 0.0), axis=0, keepdims=True))
        return out

    def trace_copy(z, col, layer):
        return pltpu.make_async_remote_copy(
            src_ref=trace_own, dst_ref=trace_in.at[me],
            send_sem=trace_send.at[0], recv_sem=trace_recv.at[0],
            device_id=(z, col, layer), device_id_type=MESH,
        )

    assert per % n_layer == 0
    firsts = per // n_layer

    def swap_copy(other):
        return pltpu.make_async_remote_copy(
            src_ref=trace_own, dst_ref=trace_swap.at[l],
            send_sem=trace_send.at[0], recv_sem=trace_recv.at[1],
            device_id=(r, c, other), device_id_type=MESH,
        )

    def sum_copy(z, col, layer):
        return pltpu.make_async_remote_copy(
            src_ref=trace_sum, dst_ref=trace_in.at[me],
            send_sem=trace_send.at[0], recv_sem=trace_recv.at[0],
            device_id=(z, col, layer), device_id_type=MESH,
        )

    def send_first():
        trace_swap[l] = trace_own[...]
        for other in layer_peers:
            swap_copy(other).start()
        if n_layer > 1:
            pltpu.make_async_remote_copy(
                src_ref=trace_in.at[pl.ds(0, n_layer - 1)],
                dst_ref=trace_in.at[pl.ds(0, n_layer - 1)],
                send_sem=trace_send.at[0], recv_sem=trace_recv.at[1],
                device_id=(r, c, l), device_id_type=MESH,
            ).wait_recv()
        total = trace_swap[0]
        for layer in range(1, n_layer):
            total = total + trace_swap[layer]
        trace_sum[...] = total
        trace_in[me] = total
        @pl.when(l == 0)
        def _():
            for col in range(n_col):
                for layer in range(n_layer):
                    sum_copy(last, col, layer).start()

        for z in range(last - 1, -1, -1):
            for col in range(n_col):
                if z:
                    sum_copy(z, col, l).start()
                else:
                    pl.when(col != c)(lambda: sum_copy(z, col, l).start())

    everyone = [(z, col, layer) for z in range(n_row) for col in range(n_col)
                for layer in range(n_layer)]

    def add_trace(chunks, start):
        weights = [weight(t, 1, -1) for t in range(tiles)]
        part = spread = others = jnp.zeros((1, blk), jnp.float32)
        if not start:
            part, spread, others = (trace_own[n:n + 1, :] for n in range(3))
        for t in range(tiles if start else 0):
            own = row_panel[me, pl.ds(corner + t * blk, blk), pl.ds(t * blk, blk)]
            line = jnp.sum(
                jnp.where(eye, own.astype(jnp.float32), 0.0), axis=0, keepdims=True)
            part += weight(t, 0, 2) * line
            spread += jnp.where(lanes == me * tiles + t, weights[t], 0.0)
        every = range(rows // blk)
        for block, k in ([(r, k) for k in every] if start else []) + chunks:
            sums = pair_sums(block, k)
            for t in range(tiles):
                part += weights[t] * sums[t]
            if block is not r:
                here = block * (rows // blk) + k
                total = sum(jnp.sum(line, keepdims=True) for line in sums)
                others += jnp.where(lanes == here, total, 0.0)
        trace_own[0:1, :] = part
        trace_own[1:2, :] = spread
        trace_own[2:3, :] = others

    def send_trace(row):
        trace_in[me] = trace_own[...]
        for z, col, layer in everyone:
            if z != row:
                trace_copy(z, col, layer).start()
            else:
                pl.when((col != c) | (layer != l))(
                    lambda: trace_copy(z, col, layer).start())

    middle = (last - 1) * CHUNKS
    pairs = {row: [0] + list(range(row + 1, n_row)) for row in range(1, last)}
    pairs.update({0: [last], last: []})
    asked = list(range(1, n_row))

    def ready_rows(count, distances):
        def at_hand(b, row):
            arrived = (from_left if b < row else from_right)[row][:count]
            apart = (b * per // n_layer) ^ (row * per // n_layer)
            return ([x for x, _ in arrived].count(b) == CHUNKS
                    and (apart in distances or not relayed))

        return [row for row in asked if all(at_hand(b, row) for b in pairs[row])]

    def diagonals(chosen):
        for row in chosen:
            asked.remove(row)

            @pl.when(on_diagonal & (r == row))
            def _():
                add_trace([(b, k) for b in pairs[row] for k in range(rows // blk)], True)
                send_trace(row)
                for copy, plan, sent, hold in (
                        (to_left, leftward, sent_left, hold_left),
                        (to_right, rightward, sent_right, hold_right)):
                    if row in hold:
                        for block, q in plan[row][hold[row]:sent[row]]:
                            copy(block, q, row_panel.at[me, span(q)] if block == row
                                 else col_panel.at[block, span(q)]).start()
            hold_left.pop(row, None)
            hold_right.pop(row, None)

    load_keep.wait()
    load_flag.wait()
    pl.when(far_above > 0)(lambda: pl.semaphore_wait(ready.at[3], far_above))
    @pl.when(r == last)
    def _():
        sent_left[last] = pass_on(to_left, last, leftward[last], sent_left[last], ())
    pl.when(has_left)(lambda: pl.semaphore_wait(ready.at[2], 1))
    pl.when(has_right)(lambda: answer(2, (right, c, l)))
    side_wait(n_layer - 1, 0)
    pl.when(on_diagonal & (r == 0))(lambda: add_trace([], True))
    diagonals(ready_rows(0, ()))
    for k in range(CHUNKS // 2):
        z_arrive(k)
    for d in direct:
        plane_arrive(d, 0)
    for k in range(CHUNKS // 2, CHUNKS):
        z_arrive(k)
    if detour:
        detour_pass(1)
    for d in direct:
        plane_arrive(d, 1)
    for k in range(CHUNKS, CHUNKS + 1):
        z_arrive(k)
    for k in range(CHUNKS + 1, CHUNKS + 2):
        z_arrive(k)
    def sides(chosen):
        side_wait(len(chosen) * (n_layer - 1), 2 if chosen is relayed else 1)

    soon = ready_rows(CHUNKS + 2, direct)
    in_soon = functools.reduce(jnp.logical_or, [r == row for row in soon], r < 0)
    pl.when(in_soon)(lambda: sides(direct))
    diagonals(soon)
    for turn in range(2):
        for d in relayed:
            plane_arrive(d, turn)
    if detour:
        detour_pass(0)
    for k in range(CHUNKS + 2, middle):
        z_arrive(k)
    pl.when(jnp.logical_not(in_soon))(lambda: sides(direct))
    sides(relayed)
    diagonals(list(asked))

    total = None
    for t in range(per):
        term = jnp.dot(
            row_panel[r * per + t], row_panel[me, pl.ds(t * width, width), :],
            preferred_element_type=jnp.float32)
        total = term if total is None else total + term
    updated[...] = total
    inner = has_left & has_right
    for s in range(1, last):
        pl.when((r - s >= 0) & inner)(lambda: add(terms(r - s, 0, rows)))
        pl.when((r + s <= last) & inner)(lambda: add(terms(r + s, 0, rows)))
    for row, arrived in ((0, from_right[0]), (last, from_left[last])):
        @pl.when(r == row)
        def _():
            products = []
            for block in range(n_row):
                chunks = sorted(q for b, q in arrived[:middle] if b == block)
                if chunks:
                    assert chunks == list(range(len(chunks)))
                    products += terms(block, 0, len(chunks) * piece)
            add(products)

    def finish(row, arrived, k):
        block, q = arrived[k]
        if row == 0 and block in pairs[0]:
            @pl.when(on_diagonal)
            def _():
                add_trace(parts_of([(block, q)]), False)
                if (block, q) == (last, CHUNKS - 1):
                    send_first()
        if k < last * CHUNKS - 1:
            add(terms(block, q * piece, piece))
        else:
            update(terms(block, q * piece, piece))

    def update(products):
        for i in range(rows // blk):
            flag = jnp.full((blk, blk), branch_flag[i]) == 1
            for k in range(width // blk):
                at = (pl.ds(i * blk, blk), pl.ds(k * blk, blk))
                square = updated[at]
                for product in products:
                    square += product[i * blk:(i + 1) * blk, k * blk:(k + 1) * blk]
                doubled = 2.0 * row_panel[(me,) + at].astype(jnp.float32) - square
                kept = jnp.full((blk, blk), keep_mask[k, i].astype(jnp.float32))
                updated[at] = jnp.where(flag, square, doubled) * kept

    def parts_of(chunks):
        share = piece // blk
        return [(b, q * share + k) for b, q in chunks if b in pairs[0] for k in range(share)]

    pl.when(on_diagonal & (r == 0))(
        lambda: add_trace(parts_of(from_right[0][:middle]), False))
    for k in range(middle, last * CHUNKS):
        z_arrive(k, finish)

    pl.when(inner)(lambda: update([]))

    if detour:
        pl.when(by_way & (r < 2))(
            detour_copy(aside, aside, (0, c, l), aplane_send, aside_sems.at[0]).wait_send)
    for row in range(n_row):
        blocks = pl.ds(0, (len(leftward[row]) + len(rightward[row])) // CHUNKS)
        pl.when(r == row)(pltpu.make_async_remote_copy(
            src_ref=row_panel.at[blocks], dst_ref=row_panel.at[blocks],
            send_sem=z_send.at[0], recv_sem=z_recv.at[0, 0],
            device_id=(left, c, l), device_id_type=MESH,
        ).wait_send)

    def sent_slots(count, ref, sem):
        pltpu.make_async_remote_copy(
            src_ref=ref.at[pl.ds(0, count)], dst_ref=ref.at[pl.ds(0, count)],
            send_sem=sem.at[0], recv_sem=plane_recv.at[0, 0],
            device_id=(r, c, l), device_id_type=MESH,
        ).wait_send()

    sent_slots(n_layer * n_col - 1, row_panel, plane_send)

    def heard(count):
        pltpu.make_async_remote_copy(
            src_ref=trace_in.at[pl.ds(0, count)], dst_ref=trace_in.at[pl.ds(0, count)],
            send_sem=trace_send.at[0], recv_sem=trace_recv.at[0],
            device_id=(r, c, l), device_id_type=MESH,
        ).wait_recv()

    pl.when(on_diagonal)(lambda: heard(slots - per + firsts - 1))
    pl.when(jnp.logical_not(on_diagonal))(lambda: heard(slots - per + firsts))
    giver = jnp.where(r == last, 0, l)
    parts = trace_in[giver]
    for slot in range(1, firsts):
        parts = parts + trace_in[slot * n_layer + giver]
    for slot in range(per, slots):
        parts = parts + trace_in[slot]
    lines[...] = parts
    pl.when(on_diagonal & has_left)(
        lambda: sent_slots(n_row * slots - 1, trace_in, trace_send))
    first_sent = last * n_col + n_layer - 2
    for core, count in ((l == 0, first_sent + n_col * n_layer), (l > 0, first_sent)):
        pl.when(on_diagonal & jnp.logical_not(has_left) & core)(
            functools.partial(sent_slots, count, trace_in, trace_send))


def deliver(updated, lines, out, trace, total, sems):
    whole = pltpu.make_async_copy(updated, out, sems.at[0])
    whole.start()
    total[...] = jnp.sum(lines[0:1, :] + lines[1:2, :] * lines[2:3, :], keepdims=True)
    single = pltpu.make_async_copy(total, trace, sems.at[1])
    single.start()
    whole.wait()
    single.wait()


def on_device(sizes, density, block_mask, keep_mask, branch_flag):
    n_row, n_col, n_layer = sizes
    rows, width = density.shape
    blk = rows // block_mask.shape[0]
    dma = pltpu.SemaphoreType.DMA
    slots = n_col * n_layer
    vmem = pl.BlockSpec(memory_space=pltpu.VMEM)
    hbm = pl.BlockSpec(memory_space=pltpu.HBM)
    panel_bytes = 2 * rows * width * (slots + n_row + 1)
    updated, lines = pl.pallas_call(
        functools.partial(kernel, sizes),
        out_shape=(
            jax.ShapeDtypeStruct((rows, width), jnp.float32),
            jax.ShapeDtypeStruct((3, blk), jnp.float32),
        ),
        in_specs=[hbm, hbm, hbm, hbm],
        out_specs=(vmem, vmem),
        scratch_shapes=[
            pltpu.VMEM((rows, width), jnp.bfloat16),
            pltpu.SMEM(block_mask.T.shape, jnp.int32),
            pltpu.SMEM(keep_mask.T.shape, jnp.int32),
            pltpu.SMEM(branch_flag.shape, jnp.int32),
            pltpu.VMEM((slots, rows, width), jnp.bfloat16),
            pltpu.VMEM((n_row, rows, width), jnp.bfloat16),
            pltpu.VMEM((3, blk), jnp.float32),
            pltpu.VMEM((n_row * slots, 3, blk), jnp.float32),
            dma((3,)),
            dma((1,)),
            dma((max(n_col - 1, 1), 2)),
            dma((3,)),
            dma((1,)),
            dma((n_row - 1, CHUNKS)),
            dma((1,)),
            dma((2,)),
            pltpu.VMEM((n_layer, 3, blk), jnp.float32),
            pltpu.VMEM((3, blk), jnp.float32),
            pltpu.VMEM((rows // CHUNKS // 2, width), jnp.bfloat16),
            dma((1,)),
            dma((1,)),
            pltpu.SemaphoreType.REGULAR((4,)),
        ],
        compiler_params=pltpu.CompilerParams(
            collective_id=0, has_side_effects=True,
            vmem_limit_bytes=panel_bytes + 8 * rows * width + (4 << 20)),
    )(*[
        pltpu.with_memory_space_constraint(x, pltpu.HBM)
        for x in (density, block_mask.T, keep_mask.T, branch_flag)
    ])
    updated, trace = pl.pallas_call(
        deliver,
        out_shape=(
            jax.ShapeDtypeStruct((rows, width), jnp.float32),
            jax.ShapeDtypeStruct((1, 1), jnp.float32),
        ),
        in_specs=[vmem, vmem],
        out_specs=(hbm, hbm),
        scratch_shapes=[pltpu.VMEM((1, 1), jnp.float32), dma((2,))],
        compiler_params=pltpu.CompilerParams(
            vmem_limit_bytes=8 * rows * width + (4 << 20)),
    )(updated, lines)
    return updated, trace[0, 0]


def solution(mesh):
    sizes = tuple(mesh.shape[name] for name in ("row", "col", "layer"))
    in_specs = (
        P("row", ("col", "layer")),
        P("row", ("col", "layer")),
        P("row", ("col", "layer")),
        P("row"),
    )
    out_specs = (P("row", ("col", "layer")), P())
    return jax.shard_map(
        functools.partial(on_device, sizes), mesh=mesh, in_specs=in_specs,
        out_specs=out_specs, check_vma=False,
    )
```

```python
import functools

import jax
import jax.numpy as jnp
from jax import lax
from jax.experimental import pallas as pl
from jax.experimental.pallas import tpu as pltpu
from jax.sharding import PartitionSpec as P

MESH = pl.DeviceIdType.MESH
CHUNKS = 4
AHEAD = 2


def partner_of(index, step, size):
    if size & (size - 1):
        return (index + step) % size
    for bit in range(size.bit_length()):
        if step >> bit & 1:
            index = index + (1 - 2 * ((index // (1 << bit)) % 2)) * (1 << bit)
    return index


def passing_plans(n_row):
    last = n_row - 1
    blocks = [[(b, q) for q in range(CHUNKS)] for b in range(n_row)]
    rightward = [sum(blocks[row::-1], []) for row in range(last)] + [[]]
    leftward = [[]] + [sum(blocks[row:], []) for row in range(1, n_row)]
    for row in range(1, last):
        for order, block, count in ((rightward[row], 1, 2), (leftward[row], last - 1, 1)):
            for q in range(CHUNKS - count, CHUNKS):
                order.remove((block, q))
                order.append((block, q))
    leftward[1].remove((1, CHUNKS - 1))
    leftward[1].append((1, CHUNKS - 1))
    return rightward, leftward


def kernel(
    sizes, density_hbm, block_hbm, keep_hbm, flag_hbm, updated, lines,
    density, block_mask, keep_mask, branch_flag,
    row_panel, col_panel, trace_own, trace_in, local_sem,
    plane_send, plane_recv, side_recv, z_send, z_recv,
    trace_send, trace_recv, trace_swap, trace_sum, aside, aplane_send, aside_sems, ready,
):
    n_row, n_col, n_layer = sizes
    rows, width = density.shape
    blk = rows // block_mask.shape[1]
    per = rows // width
    piece = rows // CHUNKS
    slots = n_col * n_layer
    last = n_row - 1
    r, c, l = lax.axis_index("row"), lax.axis_index("col"), lax.axis_index("layer")
    me = c * n_layer + l
    has_left, has_right = r > 0, r < last
    left, right = jnp.maximum(r - 1, 0), jnp.minimum(r + 1, last)
    col_peers = [partner_of(c, d, n_col) for d in range(1, n_col)]
    layer_peers = [partner_of(l, d, n_layer) for d in range(1, n_layer)]

    bits = [d for d in range(1, n_col) if d & (d - 1) == 0]
    relayed = [lo | hi for hi in bits for lo in bits if lo < hi]
    if n_col & (n_col - 1):
        bits, relayed = list(range(1, n_col)), []
    direct = [d for d in range(1, n_col) if d not in relayed]
    halves = {d: (1, 0) if relayed and d > 1 else (0, 1) for d in range(1, n_col)}

    plane_peers = [(c, q, True, 1) for q in layer_peers]
    for d in range(1, n_col):
        p = col_peers[d - 1]
        met = (p * c == 0) if d in relayed and len(bits) == 2 else True
        plane_peers += [(p, q, met, 3 if d in relayed else 1) for q in range(n_layer)]

    def counted(which, above):
        return sum(jnp.where(((p * n_layer + q > me) == above) & met, 1, 0)
                   for p, q, met, to in plane_peers if to in which)

    def span(q):
        return pl.ds(q * piece, piece)

    def load(n, source, target):
        return pltpu.make_async_copy(source, target, local_sem.at[n])

    rest = pl.ds(piece, rows - piece)
    load_first = load(0, density_hbm.at[span(0)], density.at[span(0)])
    load_mask = load(1, block_hbm, block_mask)
    load_rest = load(2, density_hbm.at[rest], density.at[rest])
    load_keep, load_flag = load(0, keep_hbm, keep_mask), load(1, flag_hbm, branch_flag)
    for first in (load_first, load_mask, load_rest):
        first.start()

    barrier = pltpu.get_barrier_semaphore()

    def greet(target):
        pl.semaphore_signal(barrier, inc=1, device_id=target, device_id_type=MESH)

    def answer(which, target):
        pl.semaphore_signal(
            ready.at[which], inc=1, device_id=target, device_id_type=MESH)

    pl.when(has_right)(lambda: greet((right, c, l)))
    for p, q, met, _ in plane_peers:
        pl.when((p * n_layer + q > me) & met)(functools.partial(greet, (r, p, q)))
    below = jnp.where(has_left, 1, 0) + counted((1, 3), False)
    pl.when(below > 0)(lambda: pl.semaphore_wait(barrier, below))
    pl.when(has_left)(lambda: answer(0, (left, c, l)))
    for p, q, met, to in plane_peers:
        pl.when((p * n_layer + q < me) & met)(functools.partial(answer, to, (r, p, q)))
    def mask(q):
        if q == 1:
            load_rest.wait()
        for i in range(q * piece // blk, (q + 1) * piece // blk):
            for k in range(width // blk):
                at = (pl.ds(i * blk, blk), pl.ds(k * blk, blk))
                kept = jnp.full((blk, blk), block_mask[k, i].astype(jnp.float32))
                row_panel[(me,) + at] = density[at] * kept.astype(jnp.bfloat16)

    load_mask.wait()
    load_first.wait()
    load_keep.start()
    load_flag.start()

    def z_copy(block, q, source, target, sem, recv):
        return pltpu.make_async_remote_copy(
            src_ref=source, dst_ref=col_panel.at[block, span(q)],
            send_sem=sem.at[0], recv_sem=z_recv.at[recv, q],
            device_id=(target, c, l), device_id_type=MESH,
        )

    def to_right(block, q, source):
        return z_copy(block, q, source, right, z_send, block)

    def to_left(block, q, source):
        return z_copy(block, q, source, left, z_send, block - 1)

    def half_copy(slot, h, sem, recv, target):
        half = pl.ds(h * (rows // 2), rows // 2)
        return pltpu.make_async_remote_copy(
            src_ref=row_panel.at[slot, half], dst_ref=row_panel.at[slot, half],
            send_sem=sem.at[0], recv_sem=recv, device_id=target, device_id_type=MESH,
        )

    def plane_copy(slot, h, d, peer):
        return half_copy(slot, h, plane_send, plane_recv.at[d - 1, h], (r, peer, l))

    def side_copies(slot, h, group):
        for other in layer_peers:
            half_copy(slot, h, plane_send, side_recv.at[group], (r, c, other)).start()

    def side_wait(count, group):
        blocks = row_panel.at[pl.ds(0, count)]
        if count:
            pltpu.make_async_remote_copy(
                src_ref=blocks, dst_ref=blocks, send_sem=plane_send.at[0],
                recv_sem=side_recv.at[group], device_id=(r, c, l), device_id_type=MESH,
            ).wait_recv()

    def seen(d):
        return n_col - d if n_col & (n_col - 1) else d

    def plane_start(chosen):
        for turn in range(2):
            for d in direct:
                peer = col_peers[d - 1]
                pl.when(chosen(peer))(
                    lambda: plane_copy(me, halves[d][turn], seen(d), peer).start())

    def plane_arrive(d, turn):
        peer, h = col_peers[d - 1], halves[d][turn]
        slot = peer * n_layer + l
        plane_copy(slot, h, d, peer).wait_recv()
        for other in bits if relayed and d in bits else []:
            if (other > d) == (h == 0) and other != d:
                plane_copy(slot, h, d | other, col_peers[other - 1]).start()
        side_copies(slot, h, 2 if d in relayed else 1)

    rightward, leftward = passing_plans(n_row)
    from_left = [[]] + rightward[:-1]
    from_right = leftward[1:] + [[]]

    on_diagonal = me // per == r

    detour = bool(relayed)
    ways = [(c == d) & (l == n_layer - 1) for d in bits[:2]] if detour else []
    by_way = functools.reduce(jnp.logical_or, ways, c < 0)

    def part_of(h):
        return pl.ds((CHUNKS - 1) * piece + h * (piece // 2), piece // 2)

    def detour_copy(source, target, device, sem, recv):
        return pltpu.make_async_remote_copy(
            src_ref=source, dst_ref=target, send_sem=sem.at[0], recv_sem=recv,
            device_id=device, device_id_type=MESH,
        )

    def detour_start():
        for h, d in enumerate(bits[:2]):
            pl.when((r == 1) & (me == n_layer - 1))(detour_copy(
                row_panel.at[me, part_of(h)], aside, (1, d, n_layer - 1),
                z_send, aside_sems.at[0]).start)

    def detour_pass(row):
        @pl.when(by_way & (r == row))
        def _():
            detour_copy(aside, aside, (0, c, l), aplane_send, aside_sems.at[0]).wait_recv()
            if row:
                detour_copy(aside, aside, (0, c, l), aplane_send, aside_sems.at[0]).start()

        for h, way in enumerate(ways if row == 0 else []):
            pl.when(way & (r == row))(detour_copy(
                aside, col_panel.at[1, part_of(h)], (0, 0, n_layer - 1),
                aplane_send, z_recv.at[0, CHUNKS - 1]).start)

    def pass_on(copy, row, plan, first, arrived, stop=None, hold=None):
        while first < len(plan) and (stop is None or first < stop):
            block, q = plan[first]
            if block == row:
                source = row_panel.at[me, span(q)]
            elif (block, q) in arrived:
                source = col_panel.at[block, span(q)]
            else:
                break
            if detour and copy is to_left and (row, block, q) == (1, 1, CHUNKS - 1):
                pl.when(jnp.logical_not(on_diagonal) & (me != n_layer - 1))(
                    functools.partial(lambda f: f.start(), copy(block, q, source)))
            elif hold is None or first < hold:
                copy(block, q, source).start()
            else:
                pl.when(jnp.logical_not(on_diagonal))(
                    functools.partial(lambda f: f.start(), copy(block, q, source)))
            first += 1
        return first

    sent_left, sent_right = [0] * n_row, [0] * n_row
    hold_left, hold_right = {1: last * CHUNKS - 2}, {last - 1: 2 * CHUNKS}
    for q in range(CHUNKS):
        mask(q)
        for row in range(1, n_row) if q < AHEAD else []:
            @pl.when(r == row)
            def _():
                sent_left[row] = pass_on(
                    to_left, row, leftward[row], sent_left[row], (), q + 1)
    plane_start(lambda peer: peer < c)
    pl.when(has_right)(lambda: pl.semaphore_wait(ready.at[0], 1))
    for row in range(last):
        @pl.when(r == row)
        def _():
            sent_right[row] = pass_on(to_right, row, rightward[row], 0, (), AHEAD)
    near_above, far_above = counted((1,), True), counted((3,), True)
    pl.when(near_above > 0)(lambda: pl.semaphore_wait(ready.at[1], near_above))
    for row in range(n_row):
        @pl.when(r == row)
        def _():
            sent_left[row] = pass_on(
                to_left, row, leftward[row], sent_left[row], (),
                CHUNKS - 1 if row == last else None, hold_left.get(row))
            sent_right[row] = pass_on(
                to_right, row, rightward[row], sent_right[row], (), None, hold_right.get(row))
    if detour:
        detour_start()
    plane_start(lambda peer: peer > c)
    for h in range(2):
        side_copies(me, h, 0)

    def z_arrive(k, then=None):
        for row in range(n_row):
            if k < max(len(from_right[row]), len(from_left[row])):
                @pl.when(r == row)
                def _():
                    if k < len(from_right[row]):
                        block, q = from_right[row][k]
                        to_left(block, q, col_panel.at[block, span(q)]).wait_recv()
                        sent_left[row] = pass_on(
                            to_left, row, leftward[row], sent_left[row],
                            from_right[row][:k + 1], None, hold_left.get(row))
                        if then:
                            then(row, from_right[row], k)
                    if k < len(from_left[row]):
                        block, q = from_left[row][k]
                        to_right(block, q, col_panel.at[block, span(q)]).wait_recv()
                        sent_right[row] = pass_on(
                            to_right, row, rightward[row], sent_right[row],
                            from_left[row][:k + 1], None, hold_right.get(row))
                        if then:
                            then(row, from_left[row], k)

    def terms(block, start, size):
        out = []
        while size:
            step = min(size, width - start % width)
            out.append(jnp.dot(
                row_panel[block * per + start // width, :, pl.ds(start % width, step)],
                col_panel[block, pl.ds(start, step), :],
                preferred_element_type=jnp.float32))
            start, size = start + step, size - step
        return out

    def add(products):
        total = products[0]
        for product in products[1:]:
            total = total + product
        updated[...] += total

    corner = pl.multiple_of((me % per) * width, width)
    tiles = width // blk
    lanes = lax.broadcasted_iota(jnp.int32, (1, blk), 1)
    eye = (lax.broadcasted_iota(jnp.int32, (blk, blk), 0)
           == lax.broadcasted_iota(jnp.int32, (blk, blk), 1))

    def weight(t, if_square, otherwise):
        kept = keep_mask[t, (me % per) * tiles + t]
        chosen = jnp.where(branch_flag[(me % per) * tiles + t] == 1, if_square, otherwise)
        return (kept * chosen).astype(jnp.float32)

    def pair_sums(block, k):
        slot = block * per + k * blk // width
        out = []
        for t in range(tiles):
            ours = row_panel[slot, pl.ds(corner + t * blk, blk), pl.ds(k * blk % width, blk)]
            if block is r:
                theirs = row_panel[me, pl.ds(k * blk, blk), pl.ds(t * blk, blk)]
            else:
                theirs = col_panel[block, pl.ds(k * blk, blk), pl.ds(t * blk, blk)]
            product = jnp.dot(ours, theirs, preferred_element_type=jnp.float32)
            out.append(jnp.sum(jnp.where(eye, product, 0.0), axis=0, keepdims=True))
        return out

    def trace_copy(z, col, layer):
        return pltpu.make_async_remote_copy(
            src_ref=trace_own, dst_ref=trace_in.at[me],
            send_sem=trace_send.at[0], recv_sem=trace_recv.at[0],
            device_id=(z, col, layer), device_id_type=MESH,
        )

    assert per % n_layer == 0
    firsts = per // n_layer

    def swap_copy(other):
        return pltpu.make_async_remote_copy(
            src_ref=trace_own, dst_ref=trace_swap.at[l],
            send_sem=trace_send.at[0], recv_sem=trace_recv.at[1],
            device_id=(r, c, other), device_id_type=MESH,
        )

    def sum_copy(z, col, layer):
        return pltpu.make_async_remote_copy(
            src_ref=trace_sum, dst_ref=trace_in.at[me],
            send_sem=trace_send.at[0], recv_sem=trace_recv.at[0],
            device_id=(z, col, layer), device_id_type=MESH,
        )

    def send_first():
        trace_swap[l] = trace_own[...]
        for other in layer_peers:
            swap_copy(other).start()
        if n_layer > 1:
            pltpu.make_async_remote_copy(
                src_ref=trace_in.at[pl.ds(0, n_layer - 1)],
                dst_ref=trace_in.at[pl.ds(0, n_layer - 1)],
                send_sem=trace_send.at[0], recv_sem=trace_recv.at[1],
                device_id=(r, c, l), device_id_type=MESH,
            ).wait_recv()
        total = trace_swap[0]
        for layer in range(1, n_layer):
            total = total + trace_swap[layer]
        trace_sum[...] = total
        trace_in[me] = total
        @pl.when(l == 0)
        def _():
            for col in range(n_col):
                for layer in range(n_layer):
                    sum_copy(last, col, layer).start()

        for z in range(last - 1, -1, -1):
            for col in range(n_col):
                if z:
                    sum_copy(z, col, l).start()
                else:
                    pl.when(col != c)(lambda: sum_copy(z, col, l).start())

    everyone = [(z, col, layer) for z in range(n_row) for col in range(n_col)
                for layer in range(n_layer)]

    def add_trace(chunks, start):
        weights = [weight(t, 1, -1) for t in range(tiles)]
        part = spread = others = jnp.zeros((1, blk), jnp.float32)
        if not start:
            part, spread, others = (trace_own[n:n + 1, :] for n in range(3))
        for t in range(tiles if start else 0):
            own = row_panel[me, pl.ds(corner + t * blk, blk), pl.ds(t * blk, blk)]
            line = jnp.sum(
                jnp.where(eye, own.astype(jnp.float32), 0.0), axis=0, keepdims=True)
            part += weight(t, 0, 2) * line
            spread += jnp.where(lanes == me * tiles + t, weights[t], 0.0)
        every = range(rows // blk)
        for block, k in ([(r, k) for k in every] if start else []) + chunks:
            sums = pair_sums(block, k)
            for t in range(tiles):
                part += weights[t] * sums[t]
            if block is not r:
                here = block * (rows // blk) + k
                total = sum(jnp.sum(line, keepdims=True) for line in sums)
                others += jnp.where(lanes == here, total, 0.0)
        trace_own[0:1, :] = part
        trace_own[1:2, :] = spread
        trace_own[2:3, :] = others

    def send_trace(row):
        trace_in[me] = trace_own[...]
        for z, col, layer in everyone:
            if z != row:
                trace_copy(z, col, layer).start()
            else:
                pl.when((col != c) | (layer != l))(
                    lambda: trace_copy(z, col, layer).start())

    middle = (last - 1) * CHUNKS
    pairs = {row: [0] + list(range(row + 1, n_row)) for row in range(1, last)}
    pairs.update({0: [last], last: []})
    asked = list(range(1, n_row))

    def ready_rows(count, distances):
        def at_hand(b, row):
            arrived = (from_left if b < row else from_right)[row][:count]
            apart = (b * per // n_layer) ^ (row * per // n_layer)
            return ([x for x, _ in arrived].count(b) == CHUNKS
                    and (apart in distances or not relayed))

        return [row for row in asked if all(at_hand(b, row) for b in pairs[row])]

    def diagonals(chosen):
        for row in chosen:
            asked.remove(row)

            @pl.when(on_diagonal & (r == row))
            def _():
                add_trace([(b, k) for b in pairs[row] for k in range(rows // blk)], True)
                send_trace(row)
                for copy, plan, sent, hold in (
                        (to_left, leftward, sent_left, hold_left),
                        (to_right, rightward, sent_right, hold_right)):
                    if row in hold:
                        for block, q in plan[row][hold[row]:sent[row]]:
                            copy(block, q, row_panel.at[me, span(q)] if block == row
                                 else col_panel.at[block, span(q)]).start()
            hold_left.pop(row, None)
            hold_right.pop(row, None)

    load_keep.wait()
    load_flag.wait()
    pl.when(far_above > 0)(lambda: pl.semaphore_wait(ready.at[3], far_above))
    @pl.when(r == last)
    def _():
        sent_left[last] = pass_on(to_left, last, leftward[last], sent_left[last], ())
    pl.when(has_left)(lambda: pl.semaphore_wait(ready.at[2], 1))
    pl.when(has_right)(lambda: answer(2, (right, c, l)))
    side_wait(n_layer - 1, 0)
    pl.when(on_diagonal & (r == 0))(lambda: add_trace([], True))
    diagonals(ready_rows(0, ()))
    for k in range(CHUNKS // 2):
        z_arrive(k)
    for d in direct:
        plane_arrive(d, 0)
    for k in range(CHUNKS // 2, CHUNKS):
        z_arrive(k)
    if detour:
        detour_pass(1)
    for d in direct:
        plane_arrive(d, 1)
    for k in range(CHUNKS, CHUNKS + 1):
        z_arrive(k)
    for k in range(CHUNKS + 1, CHUNKS + 2):
        z_arrive(k)
    def sides(chosen):
        side_wait(len(chosen) * (n_layer - 1), 2 if chosen is relayed else 1)

    soon = ready_rows(CHUNKS + 2, direct)
    in_soon = functools.reduce(jnp.logical_or, [r == row for row in soon], r < 0)
    pl.when(in_soon)(lambda: sides(direct))
    diagonals(soon)
    for turn in range(2):
        for d in relayed:
            plane_arrive(d, turn)
    if detour:
        detour_pass(0)
    for k in range(CHUNKS + 2, middle):
        z_arrive(k)
    pl.when(jnp.logical_not(in_soon))(lambda: sides(direct))
    sides(relayed)
    diagonals(list(asked))

    total = None
    for t in range(per):
        term = jnp.dot(
            row_panel[r * per + t], row_panel[me, pl.ds(t * width, width), :],
            preferred_element_type=jnp.float32)
        total = term if total is None else total + term
    updated[...] = total
    inner = has_left & has_right
    for s in range(1, last):
        pl.when((r - s >= 0) & inner)(lambda: add(terms(r - s, 0, rows)))
        pl.when((r + s <= last) & inner)(lambda: add(terms(r + s, 0, rows)))
    for row, arrived in ((0, from_right[0]), (last, from_left[last])):
        @pl.when(r == row)
        def _():
            products = []
            for block in range(n_row):
                chunks = sorted(q for b, q in arrived[:middle] if b == block)
                if chunks:
                    assert chunks == list(range(len(chunks)))
                    products += terms(block, 0, len(chunks) * piece)
            add(products)

    def finish(row, arrived, k):
        block, q = arrived[k]
        if row == 0 and block in pairs[0]:
            @pl.when(on_diagonal)
            def _():
                add_trace(parts_of([(block, q)]), False)
                if (block, q) == (last, CHUNKS - 1):
                    send_first()
        if k < last * CHUNKS - 1:
            add(terms(block, q * piece, piece))
        else:
            update(terms(block, q * piece, piece))

    def update(products):
        for i in range(rows // blk):
            flag = jnp.full((blk, blk), branch_flag[i]) == 1
            for k in range(width // blk):
                at = (pl.ds(i * blk, blk), pl.ds(k * blk, blk))
                square = updated[at]
                for product in products:
                    square += product[i * blk:(i + 1) * blk, k * blk:(k + 1) * blk]
                doubled = 2.0 * row_panel[(me,) + at].astype(jnp.float32) - square
                kept = jnp.full((blk, blk), keep_mask[k, i].astype(jnp.float32))
                updated[at] = jnp.where(flag, square, doubled) * kept

    def parts_of(chunks):
        share = piece // blk
        return [(b, q * share + k) for b, q in chunks if b in pairs[0] for k in range(share)]

    pl.when(on_diagonal & (r == 0))(
        lambda: add_trace(parts_of(from_right[0][:middle]), False))
    for k in range(middle, last * CHUNKS):
        z_arrive(k, finish)

    pl.when(inner)(lambda: update([]))

    if detour:
        pl.when(by_way & (r < 2))(
            detour_copy(aside, aside, (0, c, l), aplane_send, aside_sems.at[0]).wait_send)
    for row in range(n_row):
        blocks = pl.ds(0, (len(leftward[row]) + len(rightward[row])) // CHUNKS)
        pl.when(r == row)(pltpu.make_async_remote_copy(
            src_ref=row_panel.at[blocks], dst_ref=row_panel.at[blocks],
            send_sem=z_send.at[0], recv_sem=z_recv.at[0, 0],
            device_id=(left, c, l), device_id_type=MESH,
        ).wait_send)

    def sent_slots(count, ref, sem):
        pltpu.make_async_remote_copy(
            src_ref=ref.at[pl.ds(0, count)], dst_ref=ref.at[pl.ds(0, count)],
            send_sem=sem.at[0], recv_sem=plane_recv.at[0, 0],
            device_id=(r, c, l), device_id_type=MESH,
        ).wait_send()

    sent_slots(n_layer * n_col - 1, row_panel, plane_send)

    def heard(count):
        pltpu.make_async_remote_copy(
            src_ref=trace_in.at[pl.ds(0, count)], dst_ref=trace_in.at[pl.ds(0, count)],
            send_sem=trace_send.at[0], recv_sem=trace_recv.at[0],
            device_id=(r, c, l), device_id_type=MESH,
        ).wait_recv()

    pl.when(on_diagonal)(lambda: heard(slots - per + firsts - 1))
    pl.when(jnp.logical_not(on_diagonal))(lambda: heard(slots - per + firsts))
    giver = jnp.where(r == last, 0, l)
    parts = trace_in[giver]
    for slot in range(1, firsts):
        parts = parts + trace_in[slot * n_layer + giver]
    for slot in range(per, slots):
        parts = parts + trace_in[slot]
    lines[...] = parts
    pl.when(on_diagonal & has_left)(
        lambda: sent_slots(n_row * slots - 1, trace_in, trace_send))
    first_sent = last * n_col + n_layer - 2
    for core, count in ((l == 0, first_sent + n_col * n_layer), (l > 0, first_sent)):
        pl.when(on_diagonal & jnp.logical_not(has_left) & core)(
            functools.partial(sent_slots, count, trace_in, trace_send))


def deliver(updated, lines, out, trace):
    out[...] = updated[...]
    trace[0, 0] = jnp.sum(lines[0:1, :] + lines[1:2, :] * lines[2:3, :])


def on_device(sizes, density, block_mask, keep_mask, branch_flag):
    n_row, n_col, n_layer = sizes
    rows, width = density.shape
    blk = rows // block_mask.shape[0]
    dma = pltpu.SemaphoreType.DMA
    slots = n_col * n_layer
    vmem, smem = pl.BlockSpec(memory_space=pltpu.VMEM), pl.BlockSpec(memory_space=pltpu.SMEM)
    hbm = pl.BlockSpec(memory_space=pltpu.HBM)
    panel_bytes = 2 * rows * width * (slots + n_row + 1)
    updated, lines = pl.pallas_call(
        functools.partial(kernel, sizes),
        out_shape=(
            jax.ShapeDtypeStruct((rows, width), jnp.float32),
            jax.ShapeDtypeStruct((3, blk), jnp.float32),
        ),
        in_specs=[hbm, hbm, hbm, hbm],
        out_specs=(vmem, vmem),
        scratch_shapes=[
            pltpu.VMEM((rows, width), jnp.bfloat16),
            pltpu.SMEM(block_mask.T.shape, jnp.int32),
            pltpu.SMEM(keep_mask.T.shape, jnp.int32),
            pltpu.SMEM(branch_flag.shape, jnp.int32),
            pltpu.VMEM((slots, rows, width), jnp.bfloat16),
            pltpu.VMEM((n_row, rows, width), jnp.bfloat16),
            pltpu.VMEM((3, blk), jnp.float32),
            pltpu.VMEM((n_row * slots, 3, blk), jnp.float32),
            dma((3,)),
            dma((1,)),
            dma((max(n_col - 1, 1), 2)),
            dma((3,)),
            dma((1,)),
            dma((n_row - 1, CHUNKS)),
            dma((1,)),
            dma((2,)),
            pltpu.VMEM((n_layer, 3, blk), jnp.float32),
            pltpu.VMEM((3, blk), jnp.float32),
            pltpu.VMEM((rows // CHUNKS // 2, width), jnp.bfloat16),
            dma((1,)),
            dma((1,)),
            pltpu.SemaphoreType.REGULAR((4,)),
        ],
        compiler_params=pltpu.CompilerParams(
            collective_id=0, has_side_effects=True,
            vmem_limit_bytes=panel_bytes + 8 * rows * width + (4 << 20)),
    )(*[
        pltpu.with_memory_space_constraint(x, pltpu.HBM)
        for x in (density, block_mask.T, keep_mask.T, branch_flag)
    ])
    updated, trace = pl.pallas_call(
        deliver,
        out_shape=(
            jax.ShapeDtypeStruct((rows, width), jnp.float32),
            jax.ShapeDtypeStruct((1, 1), jnp.float32),
        ),
        in_specs=[vmem, vmem],
        out_specs=(vmem, smem),
        compiler_params=pltpu.CompilerParams(
            vmem_limit_bytes=8 * rows * width + (4 << 20)),
    )(updated, lines)
    return updated, trace[0, 0]


def solution(mesh):
    sizes = tuple(mesh.shape[name] for name in ("row", "col", "layer"))
    in_specs = (
        P("row", ("col", "layer")),
        P("row", ("col", "layer")),
        P("row", ("col", "layer")),
        P("row"),
    )
    out_specs = (P("row", ("col", "layer")), P())
    return jax.shard_map(
        functools.partial(on_device, sizes), mesh=mesh, in_specs=in_specs,
        out_specs=out_specs, check_vma=False,
    )
```
